128 devices in a mesh: gx: 16 (over z, y), gy: 8 (over x, core).
Axes of the slice: x: 4, y: 4, z: 4, core: 2. Of those that a mesh axis runs over, the one named last changes fastest.
Arguments:
- pumping: float32 [16, 4, 128, 1024], P(None, None, 'gx', 'gy'), may hold values from -1080 to 1080
- conductivity: float32 [4, 128, 1024], P(None, 'gx', 'gy'), may hold values from 0.2 to 5
- capacity: float32 [4, 128, 1024], P(None, 'gx', 'gy'), may hold values from 1 to 10
Outputs:
- solution: float32 [16, 4, 128, 1024], P(None, None, 'gx', 'gy')
- residual: float32 [16, 4, 128, 1024], P(None, None, 'gx', 'gy')
The draws below stay inside these ranges and needn't reach their ends.
All inputs are finite; a program needn't handle non-finite values.
Results may differ from the reference program's by a relative error of at most 0.0035.
Values sent between devices are 32-bit elements; how exact they have to be, the bound alone decides.
A program may use at most 64 MiB of HBM per device.

```python
import math
import jax
import jax.numpy as jnp
from jax import lax

NZ = 4
RHS = 16
S = 4
CYCLES = 5
BASIS = 80
NX = 128
NY = 1024


def draw_pumping(key, part):
    key_one = jax.random.fold_in(key, 11)
    key_two = jax.random.fold_in(key, 23)
    base_field = jax.random.truncated_normal(key_one, -6.0, 6.0, (RHS, NZ, NX, NY), jnp.float32)
    scales = jnp.exp(jax.random.uniform(key_two, (RHS,), jnp.float32) * math.log(10.0))
    rise_rows = 1.0 + 2.0 * jnp.arange(NX, dtype=jnp.float32) / max(NX - 1, 1)
    rise_cols = 1.0 + 2.0 * jnp.arange(NY, dtype=jnp.float32) / max(NY - 1, 1)
    return 2.0 * base_field * scales[:, None, None, None] * rise_rows[None, None, :, None] * rise_cols[None, None, None, :]


def steps_of(key, extent, cuts, low, largest):
    loudness = 1.0
    for position, parts in cuts:
        draws = jax.random.uniform(jax.random.fold_in(jax.random.fold_in(key, 6), position), (parts,), jnp.float32, low / len(cuts), largest / len(cuts))
        loudness = loudness * jnp.repeat(jnp.exp(draws), extent[position] // parts).reshape((-1,) + (1,) * (len(extent) - 1 - position))
    return loudness


def setup_inputs(seed: int = 0) -> dict:
    streams_of = jax.random.split(jax.random.key(seed), 4)
    pumping = draw_pumping(jax.random.fold_in(streams_of[3], 71), 0)
    conductivity = jnp.clip(jnp.exp(math.log(5.0) - 3.218876 * jax.random.uniform(streams_of[1], (NZ, NX, NY), jnp.float32) ** steps_of(streams_of[1], (NZ, NX, NY), ((1, 16), (2, 8)), -0.2, 0.2)), 0.2, 5.0)
    capacity = jnp.clip(jnp.exp(math.log(10.0) - 2.3025851 * jax.random.uniform(streams_of[2], (NZ, NX, NY), jnp.float32) ** steps_of(streams_of[2], (NZ, NX, NY), ((1, 16), (2, 8)), -0.2, 0.2)), 1.0, 10.0)
    return dict(pumping=pumping, conductivity=conductivity, capacity=capacity)


def face_terms(cond):
    padded = jnp.pad(cond, 1)
    core = cond
    terms = ((core + padded[:-2, 1:-1, 1:-1]) * 0.5, (core + padded[2:, 1:-1, 1:-1]) * 0.5, (core + padded[1:-1, :-2, 1:-1]) * 0.5, (core + padded[1:-1, 2:, 1:-1]) * 0.5, (core + padded[1:-1, 1:-1, :-2]) * 0.5, (core + padded[1:-1, 1:-1, 2:]) * 0.5)
    return terms

def apply_off(padded, terms):
    total = terms[0] * padded[:, :-2, 1:-1, 1:-1] + terms[1] * padded[:, 2:, 1:-1, 1:-1]
    total = total + terms[2] * padded[:, 1:-1, :-2, 1:-1] + terms[3] * padded[:, 1:-1, 2:, 1:-1]
    total = total + terms[4] * padded[:, 1:-1, 1:-1, :-2] + terms[5] * padded[:, 1:-1, 1:-1, 2:]
    return total

def small_solve(gram_all):
    shift_matrix = jnp.eye(BASIS, BASIS - RHS, dtype=jnp.float32) + jnp.eye(BASIS, BASIS - RHS, k=-RHS, dtype=jnp.float32)
    first_block = jnp.eye(BASIS, RHS, dtype=jnp.float32)
    hp = lax.Precision.HIGHEST
    gram_shift = jnp.dot(gram_all, shift_matrix, precision=hp)
    normal = jnp.dot(shift_matrix.T, gram_shift, precision=hp)
    right_side = jnp.dot(gram_shift.T, first_block, precision=hp)
    lower = jnp.linalg.cholesky(normal)
    y = jax.scipy.linalg.cho_solve((lower, True), right_side)
    coeffs = first_block - jnp.dot(shift_matrix, y, precision=hp)
    return (y, coeffs)

def reference(pumping, conductivity, capacity):
    hp = lax.Precision.HIGHEST
    terms = face_terms(conductivity)
    diagonal = capacity + terms[0] + terms[1] + terms[2] + terms[3] + terms[4] + terms[5]
    shape = pumping.shape
    solution = jnp.zeros(shape, jnp.float32)
    residual = pumping / diagonal
    for restart in range(CYCLES):
        blocks = [residual]
        for k in range(S):
            padded = jnp.pad(blocks[-1], ((0, 0), (1, 1), (1, 1), (1, 1)))
            blocks.append(-apply_off(padded, terms) / diagonal)
        flat = [b.reshape(RHS, -1) for b in blocks]
        rows = []
        for k in range(S + 1):
            row = []
            for j in range(S + 1):
                row.append(jnp.dot(flat[k], flat[j].T, precision=hp))
            rows.append(row)
        gram_all = jnp.block(rows)
        y, coeffs = small_solve(gram_all)
        update = jnp.zeros((RHS, flat[0].shape[1]), jnp.float32)
        fresh = jnp.zeros((RHS, flat[0].shape[1]), jnp.float32)
        for k in range(S + 1):
            if k < S:
                update = update + jnp.dot(y[k * RHS:(k + 1) * RHS].T, flat[k], precision=hp)
            fresh = fresh + jnp.dot(coeffs[k * RHS:(k + 1) * RHS].T, flat[k], precision=hp)
        solution = solution + update.reshape(shape)
        residual = fresh.reshape(shape)
    return (solution, residual)
```

```python
import jax
import jax.numpy as jnp
from jax import lax
from jax.sharding import PartitionSpec as P

RHS = 16
S = 4
CYCLES = 5
BASIS = 80


def padded_2(array, sides, width):
    for axis, dim in sides:
        devices, length = (lax.axis_size(axis), array.shape[dim])
        up = [(i, (i + 1) % devices) for i in range(devices - 1)]
        down = [(j, i) for i, j in up]
        last = lax.slice_in_dim(array, length - width, length, axis=dim)
        leading = lax.slice_in_dim(array, 0, width, axis=dim)
        before = lax.ppermute(last, axis, up)
        after = lax.ppermute(leading, axis, down)
        array = jnp.concatenate([before, array, after], axis=dim)
    return array


def halo_4(array):
    out = {}
    for axis, dim in (("gx", 2), ("gy", 3)):
        devices, length = (lax.axis_size(axis), array.shape[dim])
        up = [(i, (i + 1) % devices) for i in range(devices - 1)]
        down = [(j, i) for i, j in up]
        last = lax.slice_in_dim(array, length - 1, length, axis=dim)
        leading = lax.slice_in_dim(array, 0, 1, axis=dim)
        out[axis] = (lax.ppermute(last, axis, up), lax.ppermute(leading, axis, down))
    xb, xa = out["gx"]
    yb, ya = out["gy"]
    rows = jnp.concatenate([xb, array, xa], axis=2)
    zero_pad = ((0, 0), (0, 0), (1, 1), (0, 0))
    return jnp.concatenate([jnp.pad(yb, zero_pad), rows, jnp.pad(ya, zero_pad)], axis=3)


def face_terms(padded, storage):
    core = padded[1:-1, 1:-1, 1:-1]
    terms = (
        (core + padded[:-2, 1:-1, 1:-1]) * 0.5,
        (core + padded[2:, 1:-1, 1:-1]) * 0.5,
        (core + padded[1:-1, :-2, 1:-1]) * 0.5,
        (core + padded[1:-1, 2:, 1:-1]) * 0.5,
        (core + padded[1:-1, 1:-1, :-2]) * 0.5,
        (core + padded[1:-1, 1:-1, 2:]) * 0.5,
    )
    diagonal = storage + terms[0] + terms[1] + terms[2] + terms[3] + terms[4] + terms[5]
    return (terms, diagonal)


def apply_off(padded, terms):
    total = terms[0] * padded[:, :-2, 1:-1, 1:-1] + terms[1] * padded[:, 2:, 1:-1, 1:-1]
    total = total + terms[2] * padded[:, 1:-1, :-2, 1:-1] + terms[3] * padded[:, 1:-1, 2:, 1:-1]
    total = total + terms[4] * padded[:, 1:-1, 1:-1, :-2] + terms[5] * padded[:, 1:-1, 1:-1, 2:]
    return total


def small_solve(gram_all):
    shift_matrix = jnp.eye(BASIS, BASIS - RHS, dtype=jnp.float32) + jnp.eye(
        BASIS, BASIS - RHS, k=-RHS, dtype=jnp.float32
    )
    first_block = jnp.eye(BASIS, RHS, dtype=jnp.float32)
    hp = lax.Precision.HIGHEST
    gram_shift = jnp.dot(gram_all, shift_matrix, precision=hp)
    normal = jnp.dot(shift_matrix.T, gram_shift, precision=hp)
    right_side = jnp.dot(gram_shift.T, first_block, precision=hp)
    lower = jnp.linalg.cholesky(normal)
    y = jax.scipy.linalg.cho_solve((lower, True), right_side)
    coeffs = first_block - jnp.dot(shift_matrix, y, precision=hp)
    return (y, coeffs)


def shards(pumping, conductivity, capacity):
    hp = lax.Precision.HIGHEST
    shape = pumping.shape
    cond_halo = padded_2(conductivity, (("gx", 1), ("gy", 2)), 1)
    cond_pad = jnp.pad(cond_halo, ((1, 1), (0, 0), (0, 0)))
    terms, diagonal = face_terms(cond_pad, capacity)
    solution = jnp.zeros(shape, jnp.float32)
    residual = pumping / diagonal
    for restart in range(CYCLES):
        blocks = [residual]
        for k in range(S):
            bordered = halo_4(blocks[-1])
            padded = jnp.pad(bordered, ((0, 0), (1, 1), (0, 0), (0, 0)))
            blocks.append(-apply_off(padded, terms) / diagonal)
        stacked = jnp.concatenate(blocks, 0).reshape(BASIS, -1)
        local_gram = jnp.dot(stacked, stacked.T, precision=hp)
        gram_all = lax.psum(local_gram, ("gx", "gy"))
        y, coeffs = small_solve(gram_all)
        solution = solution + jnp.dot(y.T, stacked[: BASIS - RHS], precision=hp).reshape(shape)
        residual = jnp.dot(coeffs.T, stacked, precision=hp).reshape(shape)
    return (solution, residual)


def solution(mesh):
    return jax.shard_map(
        shards,
        mesh=mesh,
        in_specs=(P(None, None, "gx", "gy"), P(None, "gx", "gy"), P(None, "gx", "gy")),
        out_specs=(P(None, None, "gx", "gy"), P(None, None, "gx", "gy")),
        check_vma=False,
    )
```

```python
import jax
import jax.numpy as jnp
from jax import lax
from jax.sharding import PartitionSpec as P
from jax.experimental import pallas as pl
from jax.experimental.pallas import tpu as pltpu

RHS = 16
S = 4
CYCLES = 5
BASIS = 80


def padded_2(array, sides, width):
    for axis, dim in sides:
        devices, length = (lax.axis_size(axis), array.shape[dim])
        up = [(i, (i + 1) % devices) for i in range(devices - 1)]
        down = [(j, i) for i, j in up]
        last = lax.slice_in_dim(array, length - width, length, axis=dim)
        leading = lax.slice_in_dim(array, 0, width, axis=dim)
        before = lax.ppermute(last, axis, up)
        after = lax.ppermute(leading, axis, down)
        array = jnp.concatenate([before, array, after], axis=dim)
    return array


def halo_4(array):
    out = {}
    for axis, dim in (("gx", 2), ("gy", 3)):
        devices, length = (lax.axis_size(axis), array.shape[dim])
        up = [(i, (i + 1) % devices) for i in range(devices - 1)]
        down = [(j, i) for i, j in up]
        last = lax.slice_in_dim(array, length - 1, length, axis=dim)
        leading = lax.slice_in_dim(array, 0, 1, axis=dim)
        out[axis] = (lax.ppermute(last, axis, up), lax.ppermute(leading, axis, down))
    xb, xa = out["gx"]
    yb, ya = out["gy"]
    rows = jnp.concatenate([xb, array, xa], axis=2)
    zero_pad = ((0, 0), (0, 0), (1, 1), (0, 0))
    return jnp.concatenate([jnp.pad(yb, zero_pad), rows, jnp.pad(ya, zero_pad)], axis=3)


def face_terms(padded, storage):
    core = padded[1:-1, 1:-1, 1:-1]
    terms = (
        (core + padded[:-2, 1:-1, 1:-1]) * 0.5,
        (core + padded[2:, 1:-1, 1:-1]) * 0.5,
        (core + padded[1:-1, :-2, 1:-1]) * 0.5,
        (core + padded[1:-1, 2:, 1:-1]) * 0.5,
        (core + padded[1:-1, 1:-1, :-2]) * 0.5,
        (core + padded[1:-1, 1:-1, 2:]) * 0.5,
    )
    diagonal = storage + terms[0] + terms[1] + terms[2] + terms[3] + terms[4] + terms[5]
    return (terms, diagonal)


def apply_off(padded, terms):
    total = terms[0] * padded[:, :-2, 1:-1, 1:-1] + terms[1] * padded[:, 2:, 1:-1, 1:-1]
    total = total + terms[2] * padded[:, 1:-1, :-2, 1:-1] + terms[3] * padded[:, 1:-1, 2:, 1:-1]
    total = total + terms[4] * padded[:, 1:-1, 1:-1, :-2] + terms[5] * padded[:, 1:-1, 1:-1, 2:]
    return total


def _device(axis, index, other_axis, other_index):
    return {axis: index, other_axis: other_index}


def allreduce_kernel(axis, other_axis, n, x_ref, o_ref, slots, send_sem, recv_sem):
    me = lax.axis_index(axis)
    other = lax.axis_index(other_axis)
    barrier = pltpu.get_barrier_semaphore()
    for j in range(n):
        @pl.when(j != me)
        def _():
            pl.semaphore_signal(
                barrier, inc=1, device_id=_device(axis, j, other_axis, other),
                device_id_type=pl.DeviceIdType.MESH,
            )
    pl.semaphore_wait(barrier, n - 1)

    def copy_to(j):
        return pltpu.make_async_remote_copy(
            src_ref=x_ref,
            dst_ref=slots.at[me],
            send_sem=send_sem.at[j],
            recv_sem=recv_sem.at[me],
            device_id=_device(axis, j, other_axis, other),
            device_id_type=pl.DeviceIdType.MESH,
        )

    def copy_from(j):
        return pltpu.make_async_remote_copy(
            src_ref=x_ref,
            dst_ref=slots.at[j],
            send_sem=send_sem.at[j],
            recv_sem=recv_sem.at[j],
            device_id=_device(axis, j, other_axis, other),
            device_id_type=pl.DeviceIdType.MESH,
        )

    for j in range(n):
        @pl.when(j != me)
        def _():
            copy_to(j).start()

    slots[me] = x_ref[...]
    for j in range(n):
        @pl.when(j != me)
        def _():
            copy_to(j).wait_send()
            copy_from(j).wait_recv()

    acc = slots[0]
    for j in range(1, n):
        acc = acc + slots[j]
    o_ref[...] = acc


def allreduce_axis(x, axis, other_axis, collective_id):
    n = lax.axis_size(axis)
    return pl.pallas_call(
        lambda *refs: allreduce_kernel(axis, other_axis, n, *refs),
        out_shape=jax.ShapeDtypeStruct(x.shape, x.dtype),
        in_specs=[pl.BlockSpec(memory_space=pltpu.VMEM)],
        out_specs=pl.BlockSpec(memory_space=pltpu.VMEM),
        scratch_shapes=[
            pltpu.VMEM((n,) + x.shape, x.dtype),
            pltpu.SemaphoreType.DMA((n,)),
            pltpu.SemaphoreType.DMA((n,)),
        ],
        compiler_params=pltpu.CompilerParams(collective_id=collective_id, has_side_effects=True),
        name=f"allreduce_{axis}",
    )(x)


def gram_sum(local_gram):
    partial = allreduce_axis(local_gram, "gy", "gx", 0)
    return allreduce_axis(partial, "gx", "gy", 1)


def small_solve(gram_all):
    shift_matrix = jnp.eye(BASIS, BASIS - RHS, dtype=jnp.float32) + jnp.eye(
        BASIS, BASIS - RHS, k=-RHS, dtype=jnp.float32
    )
    first_block = jnp.eye(BASIS, RHS, dtype=jnp.float32)
    hp = lax.Precision.HIGHEST
    gram_shift = jnp.dot(gram_all, shift_matrix, precision=hp)
    normal = jnp.dot(shift_matrix.T, gram_shift, precision=hp)
    right_side = jnp.dot(gram_shift.T, first_block, precision=hp)
    lower = jnp.linalg.cholesky(normal)
    y = jax.scipy.linalg.cho_solve((lower, True), right_side)
    coeffs = first_block - jnp.dot(shift_matrix, y, precision=hp)
    return (y, coeffs)


def shards(pumping, conductivity, capacity):
    hp = lax.Precision.HIGHEST
    shape = pumping.shape
    cond_halo = padded_2(conductivity, (("gx", 1), ("gy", 2)), 1)
    cond_pad = jnp.pad(cond_halo, ((1, 1), (0, 0), (0, 0)))
    terms, diagonal = face_terms(cond_pad, capacity)
    solution = jnp.zeros(shape, jnp.float32)
    residual = pumping / diagonal
    for restart in range(CYCLES):
        blocks = [residual]
        for k in range(S):
            bordered = halo_4(blocks[-1])
            padded = jnp.pad(bordered, ((0, 0), (1, 1), (0, 0), (0, 0)))
            blocks.append(-apply_off(padded, terms) / diagonal)
        stacked = jnp.concatenate(blocks, 0).reshape(BASIS, -1)
        local_gram = jnp.dot(stacked, stacked.T, precision=hp)
        gram_all = gram_sum(local_gram)
        y, coeffs = small_solve(gram_all)
        solution = solution + jnp.dot(y.T, stacked[: BASIS - RHS], precision=hp).reshape(shape)
        residual = jnp.dot(coeffs.T, stacked, precision=hp).reshape(shape)
    return (solution, residual)


def solution(mesh):
    return jax.shard_map(
        shards,
        mesh=mesh,
        in_specs=(P(None, None, "gx", "gy"), P(None, "gx", "gy"), P(None, "gx", "gy")),
        out_specs=(P(None, None, "gx", "gy"), P(None, None, "gx", "gy")),
        check_vma=False,
    )
```

```python
import jax
import jax.numpy as jnp
from jax import lax
from jax.sharding import PartitionSpec as P
from jax.experimental import pallas as pl
from jax.experimental.pallas import tpu as pltpu

RHS = 16
S = 4
CYCLES = 5
BASIS = 80


def padded_2(array, sides, width):
    for axis, dim in sides:
        devices, length = (lax.axis_size(axis), array.shape[dim])
        up = [(i, (i + 1) % devices) for i in range(devices - 1)]
        down = [(j, i) for i, j in up]
        last = lax.slice_in_dim(array, length - width, length, axis=dim)
        leading = lax.slice_in_dim(array, 0, width, axis=dim)
        before = lax.ppermute(last, axis, up)
        after = lax.ppermute(leading, axis, down)
        array = jnp.concatenate([before, array, after], axis=dim)
    return array


def halo_4(array):
    out = {}
    for axis, dim in (("gx", 2), ("gy", 3)):
        devices, length = (lax.axis_size(axis), array.shape[dim])
        up = [(i, (i + 1) % devices) for i in range(devices - 1)]
        down = [(j, i) for i, j in up]
        last = lax.slice_in_dim(array, length - 1, length, axis=dim)
        leading = lax.slice_in_dim(array, 0, 1, axis=dim)
        out[axis] = (lax.ppermute(last, axis, up), lax.ppermute(leading, axis, down))
    xb, xa = out["gx"]
    yb, ya = out["gy"]
    rows = jnp.concatenate([xb, array, xa], axis=2)
    zero_pad = ((0, 0), (0, 0), (1, 1), (0, 0))
    return jnp.concatenate([jnp.pad(yb, zero_pad), rows, jnp.pad(ya, zero_pad)], axis=3)


def halo_kernel(nx, ny, xlo, xhi, ylo, yhi, xb_o, xa_o, yb_o, ya_o,
                r_xb, r_xa, r_yb, r_ya, send_sem, recv_sem):
    gx = lax.axis_index("gx")
    gy = lax.axis_index("gy")
    plan = (
        (gx < nx - 1, {"gx": gx + 1, "gy": gy}, xhi, r_xb, 0, gx > 0, xb_o),
        (gx > 0, {"gx": gx - 1, "gy": gy}, xlo, r_xa, 1, gx < nx - 1, xa_o),
        (gy < ny - 1, {"gx": gx, "gy": gy + 1}, yhi, r_yb, 2, gy > 0, yb_o),
        (gy > 0, {"gx": gx, "gy": gy - 1}, ylo, r_ya, 3, gy < ny - 1, ya_o),
    )
    barrier = pltpu.get_barrier_semaphore()
    for has_target, target, _, _, _, _, _ in plan:
        @pl.when(has_target)
        def _():
            pl.semaphore_signal(barrier, inc=1, device_id=target, device_id_type=pl.DeviceIdType.MESH)
    peers = (gx + nx - 1) // nx + (2 * nx - 2 - gx) // nx + (gy + ny - 1) // ny + (2 * ny - 2 - gy) // ny
    pl.semaphore_wait(barrier, peers)

    def copy(target, src, slot, k):
        return pltpu.make_async_remote_copy(
            src_ref=src, dst_ref=slot, send_sem=send_sem.at[k], recv_sem=recv_sem.at[k],
            device_id=target, device_id_type=pl.DeviceIdType.MESH,
        )

    for has_target, target, src, slot, k, _, _ in plan:
        @pl.when(has_target)
        def _():
            copy(target, src, slot, k).start()
    for has_target, target, src, slot, k, has_sender, out in plan:
        @pl.when(has_target)
        def _():
            copy(target, src, slot, k).wait_send()

        @pl.when(has_sender)
        def _():
            copy(target, src, slot, k).wait_recv()
            out[...] = slot[...]

        @pl.when(jnp.logical_not(has_sender))
        def _():
            out[...] = jnp.zeros(out.shape, out.dtype)


def halo_fast(array):
    rhs, nz, bx, by = array.shape
    nx, ny = lax.axis_size("gx"), lax.axis_size("gy")
    xlo = array[:, :, 0, :].reshape(rhs * nz, by)
    xhi = array[:, :, bx - 1, :].reshape(rhs * nz, by)
    ylo = array[:, :, :, 0].reshape(-1, 128)
    yhi = array[:, :, :, by - 1].reshape(-1, 128)
    vmem = pl.BlockSpec(memory_space=pltpu.VMEM)
    shapes = [jax.ShapeDtypeStruct(a.shape, a.dtype) for a in (xlo, xhi, ylo, yhi)]
    xb, xa, yb, ya = pl.pallas_call(
        lambda *refs: halo_kernel(nx, ny, *refs),
        out_shape=shapes,
        in_specs=[vmem] * 4,
        out_specs=[vmem] * 4,
        scratch_shapes=[pltpu.VMEM(a.shape, a.dtype) for a in shapes]
        + [pltpu.SemaphoreType.DMA((4,)), pltpu.SemaphoreType.DMA((4,))],
        compiler_params=pltpu.CompilerParams(collective_id=2, has_side_effects=True),
        name="halo_exchange",
    )(xlo, xhi, ylo, yhi)
    xb = xb.reshape(rhs, nz, 1, by)
    xa = xa.reshape(rhs, nz, 1, by)
    yb = yb.reshape(rhs, nz, bx, 1)
    ya = ya.reshape(rhs, nz, bx, 1)
    rows = jnp.concatenate([xb, array, xa], axis=2)
    zero_pad = ((0, 0), (0, 0), (1, 1), (0, 0))
    return jnp.concatenate([jnp.pad(yb, zero_pad), rows, jnp.pad(ya, zero_pad)], axis=3)


def face_terms(padded, storage):
    core = padded[1:-1, 1:-1, 1:-1]
    terms = (
        (core + padded[:-2, 1:-1, 1:-1]) * 0.5,
        (core + padded[2:, 1:-1, 1:-1]) * 0.5,
        (core + padded[1:-1, :-2, 1:-1]) * 0.5,
        (core + padded[1:-1, 2:, 1:-1]) * 0.5,
        (core + padded[1:-1, 1:-1, :-2]) * 0.5,
        (core + padded[1:-1, 1:-1, 2:]) * 0.5,
    )
    diagonal = storage + terms[0] + terms[1] + terms[2] + terms[3] + terms[4] + terms[5]
    return (terms, diagonal)


def apply_off(padded, terms):
    total = terms[0] * padded[:, :-2, 1:-1, 1:-1] + terms[1] * padded[:, 2:, 1:-1, 1:-1]
    total = total + terms[2] * padded[:, 1:-1, :-2, 1:-1] + terms[3] * padded[:, 1:-1, 2:, 1:-1]
    total = total + terms[4] * padded[:, 1:-1, 1:-1, :-2] + terms[5] * padded[:, 1:-1, 1:-1, 2:]
    return total


def _device(axis, index, other_axis, other_index):
    return {axis: index, other_axis: other_index}


def allreduce_kernel(axis, other_axis, n, x_ref, o_ref, slots, send_sem, recv_sem):
    me = lax.axis_index(axis)
    other = lax.axis_index(other_axis)
    barrier = pltpu.get_barrier_semaphore()
    for j in range(n):
        @pl.when(j != me)
        def _():
            pl.semaphore_signal(
                barrier, inc=1, device_id=_device(axis, j, other_axis, other),
                device_id_type=pl.DeviceIdType.MESH,
            )
    pl.semaphore_wait(barrier, n - 1)

    def copy_to(j):
        return pltpu.make_async_remote_copy(
            src_ref=x_ref,
            dst_ref=slots.at[me],
            send_sem=send_sem.at[j],
            recv_sem=recv_sem.at[me],
            device_id=_device(axis, j, other_axis, other),
            device_id_type=pl.DeviceIdType.MESH,
        )

    def copy_from(j):
        return pltpu.make_async_remote_copy(
            src_ref=x_ref,
            dst_ref=slots.at[j],
            send_sem=send_sem.at[j],
            recv_sem=recv_sem.at[j],
            device_id=_device(axis, j, other_axis, other),
            device_id_type=pl.DeviceIdType.MESH,
        )

    for j in range(n):
        @pl.when(j != me)
        def _():
            copy_to(j).start()

    slots[me] = x_ref[...]
    for j in range(n):
        @pl.when(j != me)
        def _():
            copy_to(j).wait_send()
            copy_from(j).wait_recv()

    acc = slots[0]
    for j in range(1, n):
        acc = acc + slots[j]
    o_ref[...] = acc


def allreduce_axis(x, axis, other_axis, collective_id):
    n = lax.axis_size(axis)
    return pl.pallas_call(
        lambda *refs: allreduce_kernel(axis, other_axis, n, *refs),
        out_shape=jax.ShapeDtypeStruct(x.shape, x.dtype),
        in_specs=[pl.BlockSpec(memory_space=pltpu.VMEM)],
        out_specs=pl.BlockSpec(memory_space=pltpu.VMEM),
        scratch_shapes=[
            pltpu.VMEM((n,) + x.shape, x.dtype),
            pltpu.SemaphoreType.DMA((n,)),
            pltpu.SemaphoreType.DMA((n,)),
        ],
        compiler_params=pltpu.CompilerParams(collective_id=collective_id, has_side_effects=True),
        name=f"allreduce_{axis}",
    )(x)


def gram_sum(local_gram):
    partial = allreduce_axis(local_gram, "gy", "gx", 0)
    return allreduce_axis(partial, "gx", "gy", 1)


def small_solve(gram_all):
    shift_matrix = jnp.eye(BASIS, BASIS - RHS, dtype=jnp.float32) + jnp.eye(
        BASIS, BASIS - RHS, k=-RHS, dtype=jnp.float32
    )
    first_block = jnp.eye(BASIS, RHS, dtype=jnp.float32)
    hp = lax.Precision.HIGHEST
    gram_shift = jnp.dot(gram_all, shift_matrix, precision=hp)
    normal = jnp.dot(shift_matrix.T, gram_shift, precision=hp)
    right_side = jnp.dot(gram_shift.T, first_block, precision=hp)
    lower = jnp.linalg.cholesky(normal)
    y = jax.scipy.linalg.cho_solve((lower, True), right_side)
    coeffs = first_block - jnp.dot(shift_matrix, y, precision=hp)
    return (y, coeffs)


def shards(pumping, conductivity, capacity):
    hp = lax.Precision.HIGHEST
    shape = pumping.shape
    cond_halo = padded_2(conductivity, (("gx", 1), ("gy", 2)), 1)
    cond_pad = jnp.pad(cond_halo, ((1, 1), (0, 0), (0, 0)))
    terms, diagonal = face_terms(cond_pad, capacity)
    solution = jnp.zeros(shape, jnp.float32)
    residual = pumping / diagonal
    for restart in range(CYCLES):
        blocks = [residual]
        for k in range(S):
            bordered = halo_fast(blocks[-1])
            padded = jnp.pad(bordered, ((0, 0), (1, 1), (0, 0), (0, 0)))
            blocks.append(-apply_off(padded, terms) / diagonal)
        stacked = jnp.concatenate(blocks, 0).reshape(BASIS, -1)
        local_gram = jnp.dot(stacked, stacked.T, precision=hp)
        gram_all = gram_sum(local_gram)
        y, coeffs = small_solve(gram_all)
        solution = solution + jnp.dot(y.T, stacked[: BASIS - RHS], precision=hp).reshape(shape)
        residual = jnp.dot(coeffs.T, stacked, precision=hp).reshape(shape)
    return (solution, residual)


def solution(mesh):
    return jax.shard_map(
        shards,
        mesh=mesh,
        in_specs=(P(None, None, "gx", "gy"), P(None, "gx", "gy"), P(None, "gx", "gy")),
        out_specs=(P(None, None, "gx", "gy"), P(None, None, "gx", "gy")),
        check_vma=False,
    )
```

```python
import jax
import jax.numpy as jnp
from jax import lax
from jax.sharding import PartitionSpec as P
from jax.experimental import pallas as pl
from jax.experimental.pallas import tpu as pltpu

RHS = 16
S = 4
CYCLES = 5
BASIS = 80


def padded_2(array, sides, width):
    for axis, dim in sides:
        devices, length = (lax.axis_size(axis), array.shape[dim])
        up = [(i, (i + 1) % devices) for i in range(devices - 1)]
        down = [(j, i) for i, j in up]
        last = lax.slice_in_dim(array, length - width, length, axis=dim)
        leading = lax.slice_in_dim(array, 0, width, axis=dim)
        before = lax.ppermute(last, axis, up)
        after = lax.ppermute(leading, axis, down)
        array = jnp.concatenate([before, array, after], axis=dim)
    return array


def halo_4(array):
    out = {}
    for axis, dim in (("gx", 2), ("gy", 3)):
        devices, length = (lax.axis_size(axis), array.shape[dim])
        up = [(i, (i + 1) % devices) for i in range(devices - 1)]
        down = [(j, i) for i, j in up]
        last = lax.slice_in_dim(array, length - 1, length, axis=dim)
        leading = lax.slice_in_dim(array, 0, 1, axis=dim)
        out[axis] = (lax.ppermute(last, axis, up), lax.ppermute(leading, axis, down))
    xb, xa = out["gx"]
    yb, ya = out["gy"]
    rows = jnp.concatenate([xb, array, xa], axis=2)
    zero_pad = ((0, 0), (0, 0), (1, 1), (0, 0))
    return jnp.concatenate([jnp.pad(yb, zero_pad), rows, jnp.pad(ya, zero_pad)], axis=3)


def halo_kernel(nx, ny, xlo, xhi, ylo, yhi, xb_o, xa_o, yb_o, ya_o,
                r_xb, r_xa, r_yb, r_ya, send_sem, recv_sem):
    gx = lax.axis_index("gx")
    gy = lax.axis_index("gy")
    plan = (
        (gx < nx - 1, {"gx": gx + 1, "gy": gy}, xhi, r_xb, 0, gx > 0, xb_o),
        (gx > 0, {"gx": gx - 1, "gy": gy}, xlo, r_xa, 1, gx < nx - 1, xa_o),
        (gy < ny - 1, {"gx": gx, "gy": gy + 1}, yhi, r_yb, 2, gy > 0, yb_o),
        (gy > 0, {"gx": gx, "gy": gy - 1}, ylo, r_ya, 3, gy < ny - 1, ya_o),
    )
    barrier = pltpu.get_barrier_semaphore()
    for has_target, target, _, _, _, _, _ in plan:
        @pl.when(has_target)
        def _():
            pl.semaphore_signal(barrier, inc=1, device_id=target, device_id_type=pl.DeviceIdType.MESH)
    peers = (gx + nx - 1) // nx + (2 * nx - 2 - gx) // nx + (gy + ny - 1) // ny + (2 * ny - 2 - gy) // ny
    pl.semaphore_wait(barrier, peers)

    def copy(target, src, slot, k):
        return pltpu.make_async_remote_copy(
            src_ref=src, dst_ref=slot, send_sem=send_sem.at[k], recv_sem=recv_sem.at[k],
            device_id=target, device_id_type=pl.DeviceIdType.MESH,
        )

    for has_target, target, src, slot, k, _, _ in plan:
        @pl.when(has_target)
        def _():
            copy(target, src, slot, k).start()
    for has_target, target, src, slot, k, has_sender, out in plan:
        @pl.when(has_target)
        def _():
            copy(target, src, slot, k).wait_send()

        @pl.when(has_sender)
        def _():
            copy(target, src, slot, k).wait_recv()
            out[...] = slot[...]

        @pl.when(jnp.logical_not(has_sender))
        def _():
            out[...] = jnp.zeros(out.shape, out.dtype)


def halo_fast(array):
    rhs, nz, bx, by = array.shape
    nx, ny = lax.axis_size("gx"), lax.axis_size("gy")
    xlo = array[:, :, 0, :].reshape(rhs * nz, by)
    xhi = array[:, :, bx - 1, :].reshape(rhs * nz, by)
    ylo = array[:, :, :, 0].reshape(-1, 128)
    yhi = array[:, :, :, by - 1].reshape(-1, 128)
    vmem = pl.BlockSpec(memory_space=pltpu.VMEM)
    shapes = [jax.ShapeDtypeStruct(a.shape, a.dtype) for a in (xlo, xhi, ylo, yhi)]
    xb, xa, yb, ya = pl.pallas_call(
        lambda *refs: halo_kernel(nx, ny, *refs),
        out_shape=shapes,
        in_specs=[vmem] * 4,
        out_specs=[vmem] * 4,
        scratch_shapes=[pltpu.VMEM(a.shape, a.dtype) for a in shapes]
        + [pltpu.SemaphoreType.DMA((4,)), pltpu.SemaphoreType.DMA((4,))],
        compiler_params=pltpu.CompilerParams(collective_id=2, has_side_effects=True),
        name="halo_exchange",
    )(xlo, xhi, ylo, yhi)
    xb = xb.reshape(rhs, nz, 1, by)
    xa = xa.reshape(rhs, nz, 1, by)
    yb = yb.reshape(rhs, nz, bx, 1)
    ya = ya.reshape(rhs, nz, bx, 1)
    rows = jnp.concatenate([xb, array, xa], axis=2)
    zero_pad = ((0, 0), (0, 0), (1, 1), (0, 0))
    return jnp.concatenate([jnp.pad(yb, zero_pad), rows, jnp.pad(ya, zero_pad)], axis=3)


def krylov_kernel(nx, ny, bx, v0_ref, terms_ref, diag_ref, out_ref,
                  halo_x, xsend, ysend, xr, yr, send_sem, recv_sem):
    gx = lax.axis_index("gx")
    gy = lax.axis_index("gy")
    rhs = out_ref.shape[1] // terms_ref.shape[1]
    rows, lanes = terms_ref.shape[1], terms_ref.shape[2]
    cells = out_ref.shape[1]
    zero_x = jnp.zeros(xr.shape[2:], jnp.float32)
    zero_y = jnp.zeros(yr.shape[2:], jnp.float32)
    for k in range(xr.shape[0]):
        for d in range(2):
            xr[k, d] = zero_x
            yr[k, d] = zero_y
    targets = (
        (gx < nx - 1, {"gx": gx + 1, "gy": gy}, gx > 0),
        (gx > 0, {"gx": gx - 1, "gy": gy}, gx < nx - 1),
        (gy < ny - 1, {"gx": gx, "gy": gy + 1}, gy > 0),
        (gy > 0, {"gx": gx, "gy": gy - 1}, gy < ny - 1),
    )
    barrier = pltpu.get_barrier_semaphore()
    for has_target, target, _ in targets:
        @pl.when(has_target)
        def _():
            pl.semaphore_signal(barrier, inc=1, device_id=target, device_id_type=pl.DeviceIdType.MESH)
    peers = (gx + nx - 1) // nx + (2 * nx - 2 - gx) // nx + (gy + ny - 1) // ny + (2 * ny - 2 - gy) // ny
    pl.semaphore_wait(barrier, peers)

    row = lax.broadcasted_iota(jnp.int32, (rhs, rows, lanes), 1)
    lane = lax.broadcasted_iota(jnp.int32, (rhs, rows, lanes), 2)
    xpos = row % bx
    zpos = row // bx
    nzp = rows // bx
    t = [terms_ref[i][None] for i in range(6)]
    diag = diag_ref[...][None]
    trow = lax.broadcasted_iota(jnp.int32, (lanes, cells), 0)

    out_ref[0] = v0_ref[...]
    for k in range(xr.shape[0]):
        flat = out_ref[k]
        xsend[0] = out_ref[k, pl.ds(0, cells // bx, stride=bx), :]
        xsend[1] = out_ref[k, pl.ds(bx - 1, cells // bx, stride=bx), :]
        tr = flat.T
        ysend[...] = jnp.where(trow[:8] == 0, tr[0:1], jnp.where(trow[:8] == 1, tr[lanes - 1:lanes], 0.0))
        plan = (
            (xsend.at[1], xr.at[k, 0]),
            (xsend.at[0], xr.at[k, 1]),
            (ysend, yr.at[k, 0]),
            (ysend, yr.at[k, 1]),
        )

        def copy(d):
            return pltpu.make_async_remote_copy(
                src_ref=plan[d][0], dst_ref=plan[d][1], send_sem=send_sem.at[d],
                recv_sem=recv_sem.at[k, d], device_id=targets[d][1],
                device_id_type=pl.DeviceIdType.MESH,
            )

        for d in range(4):
            @pl.when(targets[d][0])
            def _():
                copy(d).start()
        for d in range(4):
            @pl.when(targets[d][0])
            def _():
                copy(d).wait_send()

            @pl.when(targets[d][2])
            def _():
                copy(d).wait_recv()

        halo_x[pl.ds(0, cells // bx, stride=bx), :] = xr[k, 0]
        halo_x[pl.ds(bx - 1, cells // bx, stride=bx), :] = xr[k, 1]
        before = yr[k, 0][1:2]
        after = yr[k, 1][0:1]
        ycols = jnp.where(trow == 0, before, jnp.where(trow == lanes - 1, after, 0.0)).T
        v = flat.reshape(rhs, rows, lanes)
        hx = halo_x[...].reshape(rhs, rows, lanes)
        hy = ycols.reshape(rhs, rows, lanes)
        zm = jnp.where(zpos == 0, 0.0, pltpu.roll(v, bx, 1))
        zp = jnp.where(zpos == nzp - 1, 0.0, pltpu.roll(v, rows - bx, 1))
        xm = jnp.where(xpos == 0, hx, pltpu.roll(v, 1, 1))
        xp = jnp.where(xpos == bx - 1, hx, pltpu.roll(v, rows - 1, 1))
        ym = jnp.where(lane == 0, hy, pltpu.roll(v, 1, 2))
        yp = jnp.where(lane == lanes - 1, hy, pltpu.roll(v, lanes - 1, 2))
        total = t[0] * zm + t[1] * zp
        total = total + t[2] * xm + t[3] * xp
        total = total + t[4] * ym + t[5] * yp
        out_ref[k + 1] = (-total / diag).reshape(cells, lanes)


def krylov_basis(v0, terms, diagonal):
    rhs, nz, bx, by = v0.shape
    nx, ny = lax.axis_size("gx"), lax.axis_size("gy")
    cells = rhs * nz * bx
    vmem = pl.BlockSpec(memory_space=pltpu.VMEM)
    out = pl.pallas_call(
        lambda *refs: krylov_kernel(nx, ny, bx, *refs),
        out_shape=jax.ShapeDtypeStruct((S + 1, cells, by), jnp.float32),
        in_specs=[vmem] * 3,
        out_specs=vmem,
        scratch_shapes=[
            pltpu.VMEM((cells, by), jnp.float32),
            pltpu.VMEM((2, cells // bx, by), jnp.float32),
            pltpu.VMEM((8, cells), jnp.float32),
            pltpu.VMEM((S, 2, cells // bx, by), jnp.float32),
            pltpu.VMEM((S, 2, 8, cells), jnp.float32),
            pltpu.SemaphoreType.DMA((4,)),
            pltpu.SemaphoreType.DMA((S, 4)),
        ],
        compiler_params=pltpu.CompilerParams(collective_id=3, has_side_effects=True),
        name="krylov_basis",
    )(v0.reshape(cells, by), jnp.stack(terms).reshape(6, nz * bx, by), diagonal.reshape(nz * bx, by))
    return out.reshape(S + 1, rhs, nz, bx, by)


def face_terms(padded, storage):
    core = padded[1:-1, 1:-1, 1:-1]
    terms = (
        (core + padded[:-2, 1:-1, 1:-1]) * 0.5,
        (core + padded[2:, 1:-1, 1:-1]) * 0.5,
        (core + padded[1:-1, :-2, 1:-1]) * 0.5,
        (core + padded[1:-1, 2:, 1:-1]) * 0.5,
        (core + padded[1:-1, 1:-1, :-2]) * 0.5,
        (core + padded[1:-1, 1:-1, 2:]) * 0.5,
    )
    diagonal = storage + terms[0] + terms[1] + terms[2] + terms[3] + terms[4] + terms[5]
    return (terms, diagonal)


def apply_off(padded, terms):
    total = terms[0] * padded[:, :-2, 1:-1, 1:-1] + terms[1] * padded[:, 2:, 1:-1, 1:-1]
    total = total + terms[2] * padded[:, 1:-1, :-2, 1:-1] + terms[3] * padded[:, 1:-1, 2:, 1:-1]
    total = total + terms[4] * padded[:, 1:-1, 1:-1, :-2] + terms[5] * padded[:, 1:-1, 1:-1, 2:]
    return total


def _device(axis, index, other_axis, other_index):
    return {axis: index, other_axis: other_index}


def allreduce_kernel(axis, other_axis, n, x_ref, o_ref, slots, send_sem, recv_sem):
    me = lax.axis_index(axis)
    other = lax.axis_index(other_axis)
    barrier = pltpu.get_barrier_semaphore()
    for j in range(n):
        @pl.when(j != me)
        def _():
            pl.semaphore_signal(
                barrier, inc=1, device_id=_device(axis, j, other_axis, other),
                device_id_type=pl.DeviceIdType.MESH,
            )
    pl.semaphore_wait(barrier, n - 1)

    def copy_to(j):
        return pltpu.make_async_remote_copy(
            src_ref=x_ref,
            dst_ref=slots.at[me],
            send_sem=send_sem.at[j],
            recv_sem=recv_sem.at[me],
            device_id=_device(axis, j, other_axis, other),
            device_id_type=pl.DeviceIdType.MESH,
        )

    def copy_from(j):
        return pltpu.make_async_remote_copy(
            src_ref=x_ref,
            dst_ref=slots.at[j],
            send_sem=send_sem.at[j],
            recv_sem=recv_sem.at[j],
            device_id=_device(axis, j, other_axis, other),
            device_id_type=pl.DeviceIdType.MESH,
        )

    for j in range(n):
        @pl.when(j != me)
        def _():
            copy_to(j).start()

    slots[me] = x_ref[...]
    for j in range(n):
        @pl.when(j != me)
        def _():
            copy_to(j).wait_send()
            copy_from(j).wait_recv()

    acc = slots[0]
    for j in range(1, n):
        acc = acc + slots[j]
    o_ref[...] = acc


def allreduce_axis(x, axis, other_axis, collective_id):
    n = lax.axis_size(axis)
    return pl.pallas_call(
        lambda *refs: allreduce_kernel(axis, other_axis, n, *refs),
        out_shape=jax.ShapeDtypeStruct(x.shape, x.dtype),
        in_specs=[pl.BlockSpec(memory_space=pltpu.VMEM)],
        out_specs=pl.BlockSpec(memory_space=pltpu.VMEM),
        scratch_shapes=[
            pltpu.VMEM((n,) + x.shape, x.dtype),
            pltpu.SemaphoreType.DMA((n,)),
            pltpu.SemaphoreType.DMA((n,)),
        ],
        compiler_params=pltpu.CompilerParams(collective_id=collective_id, has_side_effects=True),
        name=f"allreduce_{axis}",
    )(x)


def gram_sum(local_gram):
    partial = allreduce_axis(local_gram, "gy", "gx", 0)
    return allreduce_axis(partial, "gx", "gy", 1)


def small_solve(gram_all):
    shift_matrix = jnp.eye(BASIS, BASIS - RHS, dtype=jnp.float32) + jnp.eye(
        BASIS, BASIS - RHS, k=-RHS, dtype=jnp.float32
    )
    first_block = jnp.eye(BASIS, RHS, dtype=jnp.float32)
    hp = lax.Precision.HIGHEST
    gram_shift = jnp.dot(gram_all, shift_matrix, precision=hp)
    normal = jnp.dot(shift_matrix.T, gram_shift, precision=hp)
    right_side = jnp.dot(gram_shift.T, first_block, precision=hp)
    lower = jnp.linalg.cholesky(normal)
    y = jax.scipy.linalg.cho_solve((lower, True), right_side)
    coeffs = first_block - jnp.dot(shift_matrix, y, precision=hp)
    return (y, coeffs)


def shards(pumping, conductivity, capacity):
    hp = lax.Precision.HIGHEST
    shape = pumping.shape
    cond_halo = padded_2(conductivity, (("gx", 1), ("gy", 2)), 1)
    cond_pad = jnp.pad(cond_halo, ((1, 1), (0, 0), (0, 0)))
    terms, diagonal = face_terms(cond_pad, capacity)
    solution = jnp.zeros(shape, jnp.float32)
    residual = pumping / diagonal
    for restart in range(CYCLES):
        stacked = krylov_basis(residual, terms, diagonal).reshape(BASIS, -1)
        local_gram = jnp.dot(stacked, stacked.T, precision=hp)
        gram_all = gram_sum(local_gram)
        y, coeffs = small_solve(gram_all)
        solution = solution + jnp.dot(y.T, stacked[: BASIS - RHS], precision=hp).reshape(shape)
        residual = jnp.dot(coeffs.T, stacked, precision=hp).reshape(shape)
    return (solution, residual)


def solution(mesh):
    return jax.shard_map(
        shards,
        mesh=mesh,
        in_specs=(P(None, None, "gx", "gy"), P(None, "gx", "gy"), P(None, "gx", "gy")),
        out_specs=(P(None, None, "gx", "gy"), P(None, None, "gx", "gy")),
        check_vma=False,
    )
```

```python
import jax
import jax.numpy as jnp
from jax import lax
from jax.sharding import PartitionSpec as P
from jax.experimental import pallas as pl
from jax.experimental.pallas import tpu as pltpu

RHS = 16
S = 4
CYCLES = 5
BASIS = 80


def padded_2(array, sides, width):
    for axis, dim in sides:
        devices, length = (lax.axis_size(axis), array.shape[dim])
        up = [(i, (i + 1) % devices) for i in range(devices - 1)]
        down = [(j, i) for i, j in up]
        last = lax.slice_in_dim(array, length - width, length, axis=dim)
        leading = lax.slice_in_dim(array, 0, width, axis=dim)
        before = lax.ppermute(last, axis, up)
        after = lax.ppermute(leading, axis, down)
        array = jnp.concatenate([before, array, after], axis=dim)
    return array


def halo_4(array):
    out = {}
    for axis, dim in (("gx", 2), ("gy", 3)):
        devices, length = (lax.axis_size(axis), array.shape[dim])
        up = [(i, (i + 1) % devices) for i in range(devices - 1)]
        down = [(j, i) for i, j in up]
        last = lax.slice_in_dim(array, length - 1, length, axis=dim)
        leading = lax.slice_in_dim(array, 0, 1, axis=dim)
        out[axis] = (lax.ppermute(last, axis, up), lax.ppermute(leading, axis, down))
    xb, xa = out["gx"]
    yb, ya = out["gy"]
    rows = jnp.concatenate([xb, array, xa], axis=2)
    zero_pad = ((0, 0), (0, 0), (1, 1), (0, 0))
    return jnp.concatenate([jnp.pad(yb, zero_pad), rows, jnp.pad(ya, zero_pad)], axis=3)


def halo_kernel(nx, ny, xlo, xhi, ylo, yhi, xb_o, xa_o, yb_o, ya_o,
                r_xb, r_xa, r_yb, r_ya, send_sem, recv_sem):
    gx = lax.axis_index("gx")
    gy = lax.axis_index("gy")
    plan = (
        (gx < nx - 1, {"gx": gx + 1, "gy": gy}, xhi, r_xb, 0, gx > 0, xb_o),
        (gx > 0, {"gx": gx - 1, "gy": gy}, xlo, r_xa, 1, gx < nx - 1, xa_o),
        (gy < ny - 1, {"gx": gx, "gy": gy + 1}, yhi, r_yb, 2, gy > 0, yb_o),
        (gy > 0, {"gx": gx, "gy": gy - 1}, ylo, r_ya, 3, gy < ny - 1, ya_o),
    )
    barrier = pltpu.get_barrier_semaphore()
    for has_target, target, _, _, _, _, _ in plan:
        @pl.when(has_target)
        def _():
            pl.semaphore_signal(barrier, inc=1, device_id=target, device_id_type=pl.DeviceIdType.MESH)
    peers = (gx + nx - 1) // nx + (2 * nx - 2 - gx) // nx + (gy + ny - 1) // ny + (2 * ny - 2 - gy) // ny
    pl.semaphore_wait(barrier, peers)

    def copy(target, src, slot, k):
        return pltpu.make_async_remote_copy(
            src_ref=src, dst_ref=slot, send_sem=send_sem.at[k], recv_sem=recv_sem.at[k],
            device_id=target, device_id_type=pl.DeviceIdType.MESH,
        )

    for has_target, target, src, slot, k, _, _ in plan:
        @pl.when(has_target)
        def _():
            copy(target, src, slot, k).start()
    for has_target, target, src, slot, k, has_sender, out in plan:
        @pl.when(has_target)
        def _():
            copy(target, src, slot, k).wait_send()

        @pl.when(has_sender)
        def _():
            copy(target, src, slot, k).wait_recv()
            out[...] = slot[...]

        @pl.when(jnp.logical_not(has_sender))
        def _():
            out[...] = jnp.zeros(out.shape, out.dtype)


def halo_fast(array):
    rhs, nz, bx, by = array.shape
    nx, ny = lax.axis_size("gx"), lax.axis_size("gy")
    xlo = array[:, :, 0, :].reshape(rhs * nz, by)
    xhi = array[:, :, bx - 1, :].reshape(rhs * nz, by)
    ylo = array[:, :, :, 0].reshape(-1, 128)
    yhi = array[:, :, :, by - 1].reshape(-1, 128)
    vmem = pl.BlockSpec(memory_space=pltpu.VMEM)
    shapes = [jax.ShapeDtypeStruct(a.shape, a.dtype) for a in (xlo, xhi, ylo, yhi)]
    xb, xa, yb, ya = pl.pallas_call(
        lambda *refs: halo_kernel(nx, ny, *refs),
        out_shape=shapes,
        in_specs=[vmem] * 4,
        out_specs=[vmem] * 4,
        scratch_shapes=[pltpu.VMEM(a.shape, a.dtype) for a in shapes]
        + [pltpu.SemaphoreType.DMA((4,)), pltpu.SemaphoreType.DMA((4,))],
        compiler_params=pltpu.CompilerParams(collective_id=2, has_side_effects=True),
        name="halo_exchange",
    )(xlo, xhi, ylo, yhi)
    xb = xb.reshape(rhs, nz, 1, by)
    xa = xa.reshape(rhs, nz, 1, by)
    yb = yb.reshape(rhs, nz, bx, 1)
    ya = ya.reshape(rhs, nz, bx, 1)
    rows = jnp.concatenate([xb, array, xa], axis=2)
    zero_pad = ((0, 0), (0, 0), (1, 1), (0, 0))
    return jnp.concatenate([jnp.pad(yb, zero_pad), rows, jnp.pad(ya, zero_pad)], axis=3)


def krylov_kernel(nx, ny, bx, v0_ref, terms_ref, diag_ref, out_ref,
                  halo_x, xsend, ysend, xr, yr, send_sem, recv_sem):
    gx = lax.axis_index("gx")
    gy = lax.axis_index("gy")
    rhs = out_ref.shape[1] // terms_ref.shape[1]
    rows, lanes = terms_ref.shape[1], terms_ref.shape[2]
    cells = out_ref.shape[1]
    zero_x = jnp.zeros(xr.shape[2:], jnp.float32)
    zero_y = jnp.zeros(yr.shape[2:], jnp.float32)
    for k in range(xr.shape[0]):
        for d in range(2):
            xr[k, d] = zero_x
            yr[k, d] = zero_y
    targets = (
        (gx < nx - 1, {"gx": gx + 1, "gy": gy}, gx > 0),
        (gx > 0, {"gx": gx - 1, "gy": gy}, gx < nx - 1),
        (gy < ny - 1, {"gx": gx, "gy": gy + 1}, gy > 0),
        (gy > 0, {"gx": gx, "gy": gy - 1}, gy < ny - 1),
    )
    barrier = pltpu.get_barrier_semaphore()
    for has_target, target, _ in targets:
        @pl.when(has_target)
        def _():
            pl.semaphore_signal(barrier, inc=1, device_id=target, device_id_type=pl.DeviceIdType.MESH)
    peers = (gx + nx - 1) // nx + (2 * nx - 2 - gx) // nx + (gy + ny - 1) // ny + (2 * ny - 2 - gy) // ny
    pl.semaphore_wait(barrier, peers)

    row = lax.broadcasted_iota(jnp.int32, (rhs, rows, lanes), 1)
    lane = lax.broadcasted_iota(jnp.int32, (rhs, rows, lanes), 2)
    xpos = row % bx
    zpos = row // bx
    nzp = rows // bx
    t = [terms_ref[i][None] for i in range(6)]
    diag = diag_ref[...][None]
    trow = lax.broadcasted_iota(jnp.int32, (lanes, cells), 0)

    out_ref[0] = v0_ref[...]
    for k in range(xr.shape[0]):
        flat = out_ref[k]
        xsend[0] = out_ref[k, pl.ds(0, cells // bx, stride=bx), :]
        xsend[1] = out_ref[k, pl.ds(bx - 1, cells // bx, stride=bx), :]
        tr = flat.T
        ysend[...] = jnp.where(trow[:8] == 0, tr[0:1], jnp.where(trow[:8] == 1, tr[lanes - 1:lanes], 0.0))
        plan = (
            (xsend.at[1], xr.at[k, 0]),
            (xsend.at[0], xr.at[k, 1]),
            (ysend, yr.at[k, 0]),
            (ysend, yr.at[k, 1]),
        )

        def copy(d):
            return pltpu.make_async_remote_copy(
                src_ref=plan[d][0], dst_ref=plan[d][1], send_sem=send_sem.at[d],
                recv_sem=recv_sem.at[k, d], device_id=targets[d][1],
                device_id_type=pl.DeviceIdType.MESH,
            )

        for d in range(4):
            @pl.when(targets[d][0])
            def _():
                copy(d).start()
        for d in range(4):
            @pl.when(targets[d][0])
            def _():
                copy(d).wait_send()

            @pl.when(targets[d][2])
            def _():
                copy(d).wait_recv()

        halo_x[pl.ds(0, cells // bx, stride=bx), :] = xr[k, 0]
        halo_x[pl.ds(bx - 1, cells // bx, stride=bx), :] = xr[k, 1]
        before = yr[k, 0][1:2]
        after = yr[k, 1][0:1]
        ycols = jnp.where(trow == 0, before, jnp.where(trow == lanes - 1, after, 0.0)).T
        v = flat.reshape(rhs, rows, lanes)
        hx = halo_x[...].reshape(rhs, rows, lanes)
        hy = ycols.reshape(rhs, rows, lanes)
        zm = jnp.where(zpos == 0, 0.0, pltpu.roll(v, bx, 1))
        zp = jnp.where(zpos == nzp - 1, 0.0, pltpu.roll(v, rows - bx, 1))
        xm = jnp.where(xpos == 0, hx, pltpu.roll(v, 1, 1))
        xp = jnp.where(xpos == bx - 1, hx, pltpu.roll(v, rows - 1, 1))
        ym = jnp.where(lane == 0, hy, pltpu.roll(v, 1, 2))
        yp = jnp.where(lane == lanes - 1, hy, pltpu.roll(v, lanes - 1, 2))
        total = t[0] * zm + t[1] * zp
        total = total + t[2] * xm + t[3] * xp
        total = total + t[4] * ym + t[5] * yp
        out_ref[k + 1] = (-total / diag).reshape(cells, lanes)


def krylov_basis(v0, terms, diagonal):
    rhs, nz, bx, by = v0.shape
    nx, ny = lax.axis_size("gx"), lax.axis_size("gy")
    cells = rhs * nz * bx
    vmem = pl.BlockSpec(memory_space=pltpu.VMEM)
    out = pl.pallas_call(
        lambda *refs: krylov_kernel(nx, ny, bx, *refs),
        out_shape=jax.ShapeDtypeStruct((S + 1, cells, by), jnp.float32),
        in_specs=[vmem] * 3,
        out_specs=vmem,
        scratch_shapes=[
            pltpu.VMEM((cells, by), jnp.float32),
            pltpu.VMEM((2, cells // bx, by), jnp.float32),
            pltpu.VMEM((8, cells), jnp.float32),
            pltpu.VMEM((S, 2, cells // bx, by), jnp.float32),
            pltpu.VMEM((S, 2, 8, cells), jnp.float32),
            pltpu.SemaphoreType.DMA((4,)),
            pltpu.SemaphoreType.DMA((S, 4)),
        ],
        compiler_params=pltpu.CompilerParams(collective_id=3, has_side_effects=True),
        name="krylov_basis",
    )(v0.reshape(cells, by), jnp.stack(terms).reshape(6, nz * bx, by), diagonal.reshape(nz * bx, by))
    return out.reshape(S + 1, rhs, nz, bx, by)


def face_terms(padded, storage):
    core = padded[1:-1, 1:-1, 1:-1]
    terms = (
        (core + padded[:-2, 1:-1, 1:-1]) * 0.5,
        (core + padded[2:, 1:-1, 1:-1]) * 0.5,
        (core + padded[1:-1, :-2, 1:-1]) * 0.5,
        (core + padded[1:-1, 2:, 1:-1]) * 0.5,
        (core + padded[1:-1, 1:-1, :-2]) * 0.5,
        (core + padded[1:-1, 1:-1, 2:]) * 0.5,
    )
    diagonal = storage + terms[0] + terms[1] + terms[2] + terms[3] + terms[4] + terms[5]
    return (terms, diagonal)


def apply_off(padded, terms):
    total = terms[0] * padded[:, :-2, 1:-1, 1:-1] + terms[1] * padded[:, 2:, 1:-1, 1:-1]
    total = total + terms[2] * padded[:, 1:-1, :-2, 1:-1] + terms[3] * padded[:, 1:-1, 2:, 1:-1]
    total = total + terms[4] * padded[:, 1:-1, 1:-1, :-2] + terms[5] * padded[:, 1:-1, 1:-1, 2:]
    return total


def _device(axis, index, other_axis, other_index):
    return {axis: index, other_axis: other_index}


def allreduce_kernel(axis, other_axis, n, x_ref, o_ref, rs, ag, mine, send_sem, rs_sem, ag_sem):
    me = lax.axis_index(axis)
    other = lax.axis_index(other_axis)
    part = x_ref.shape[0] // n
    barrier = pltpu.get_barrier_semaphore()
    for j in range(n):
        @pl.when(j != me)
        def _():
            pl.semaphore_signal(
                barrier, inc=1, device_id=_device(axis, j, other_axis, other),
                device_id_type=pl.DeviceIdType.MESH,
            )
    pl.semaphore_wait(barrier, n - 1)

    def scatter(j, slot):
        return pltpu.make_async_remote_copy(
            src_ref=x_ref.at[pl.ds(j * part, part)],
            dst_ref=rs.at[slot],
            send_sem=send_sem.at[j],
            recv_sem=rs_sem.at[slot],
            device_id=_device(axis, j, other_axis, other),
            device_id_type=pl.DeviceIdType.MESH,
        )

    def gather(j, slot):
        return pltpu.make_async_remote_copy(
            src_ref=mine,
            dst_ref=ag.at[slot],
            send_sem=send_sem.at[j],
            recv_sem=ag_sem.at[slot],
            device_id=_device(axis, j, other_axis, other),
            device_id_type=pl.DeviceIdType.MESH,
        )

    for j in range(n):
        @pl.when(j != me)
        def _():
            scatter(j, me).start()

    rs[me] = x_ref[pl.ds(pl.multiple_of(me * part, part), part)]
    for j in range(n):
        @pl.when(j != me)
        def _():
            scatter(j, me).wait_send()
            scatter(j, j).wait_recv()

    acc = rs[0]
    for j in range(1, n):
        acc = acc + rs[j]
    mine[...] = acc
    for j in range(n):
        @pl.when(j != me)
        def _():
            gather(j, me).start()
    ag[me] = acc
    for j in range(n):
        @pl.when(j != me)
        def _():
            gather(j, me).wait_send()
            gather(j, j).wait_recv()
    for j in range(n):
        o_ref[pl.ds(j * part, part)] = ag[j]


def allreduce_axis(x, axis, other_axis, collective_id):
    n = lax.axis_size(axis)
    part = x.shape[0] // n
    block = (part,) + x.shape[1:]
    return pl.pallas_call(
        lambda *refs: allreduce_kernel(axis, other_axis, n, *refs),
        out_shape=jax.ShapeDtypeStruct(x.shape, x.dtype),
        in_specs=[pl.BlockSpec(memory_space=pltpu.VMEM)],
        out_specs=pl.BlockSpec(memory_space=pltpu.VMEM),
        scratch_shapes=[
            pltpu.VMEM((n,) + block, x.dtype),
            pltpu.VMEM((n,) + block, x.dtype),
            pltpu.VMEM(block, x.dtype),
            pltpu.SemaphoreType.DMA((n,)),
            pltpu.SemaphoreType.DMA((n,)),
            pltpu.SemaphoreType.DMA((n,)),
        ],
        compiler_params=pltpu.CompilerParams(collective_id=collective_id, has_side_effects=True),
        name=f"allreduce_{axis}",
    )(x)


def gram_sum(local_gram):
    size = local_gram.shape[0]
    wide = jnp.pad(local_gram, ((0, 128 - size), (0, 128 - size)))
    partial = allreduce_axis(wide, "gy", "gx", 0)
    return allreduce_axis(partial, "gx", "gy", 1)[:size, :size]


def small_solve(gram_all):
    shift_matrix = jnp.eye(BASIS, BASIS - RHS, dtype=jnp.float32) + jnp.eye(
        BASIS, BASIS - RHS, k=-RHS, dtype=jnp.float32
    )
    first_block = jnp.eye(BASIS, RHS, dtype=jnp.float32)
    hp = lax.Precision.HIGHEST
    gram_shift = jnp.dot(gram_all, shift_matrix, precision=hp)
    normal = jnp.dot(shift_matrix.T, gram_shift, precision=hp)
    right_side = jnp.dot(gram_shift.T, first_block, precision=hp)
    lower = jnp.linalg.cholesky(normal)
    y = jax.scipy.linalg.cho_solve((lower, True), right_side)
    coeffs = first_block - jnp.dot(shift_matrix, y, precision=hp)
    return (y, coeffs)


def shards(pumping, conductivity, capacity):
    hp = lax.Precision.HIGHEST
    shape = pumping.shape
    cond_halo = padded_2(conductivity, (("gx", 1), ("gy", 2)), 1)
    cond_pad = jnp.pad(cond_halo, ((1, 1), (0, 0), (0, 0)))
    terms, diagonal = face_terms(cond_pad, capacity)
    solution = jnp.zeros(shape, jnp.float32)
    residual = pumping / diagonal
    for restart in range(CYCLES):
        stacked = krylov_basis(residual, terms, diagonal).reshape(BASIS, -1)
        local_gram = jnp.dot(stacked, stacked.T, precision=hp)
        gram_all = gram_sum(local_gram)
        y, coeffs = small_solve(gram_all)
        solution = solution + jnp.dot(y.T, stacked[: BASIS - RHS], precision=hp).reshape(shape)
        residual = jnp.dot(coeffs.T, stacked, precision=hp).reshape(shape)
    return (solution, residual)


def solution(mesh):
    return jax.shard_map(
        shards,
        mesh=mesh,
        in_specs=(P(None, None, "gx", "gy"), P(None, "gx", "gy"), P(None, "gx", "gy")),
        out_specs=(P(None, None, "gx", "gy"), P(None, None, "gx", "gy")),
        check_vma=False,
    )
```

```python
import jax
import jax.numpy as jnp
from jax import lax
from jax.sharding import PartitionSpec as P
from jax.experimental import pallas as pl
from jax.experimental.pallas import tpu as pltpu

RHS = 16
S = 4
CYCLES = 5
BASIS = 80


def padded_2(array, sides, width):
    for axis, dim in sides:
        devices, length = (lax.axis_size(axis), array.shape[dim])
        up = [(i, (i + 1) % devices) for i in range(devices - 1)]
        down = [(j, i) for i, j in up]
        last = lax.slice_in_dim(array, length - width, length, axis=dim)
        leading = lax.slice_in_dim(array, 0, width, axis=dim)
        before = lax.ppermute(last, axis, up)
        after = lax.ppermute(leading, axis, down)
        array = jnp.concatenate([before, array, after], axis=dim)
    return array


def halo_4(array):
    out = {}
    for axis, dim in (("gx", 2), ("gy", 3)):
        devices, length = (lax.axis_size(axis), array.shape[dim])
        up = [(i, (i + 1) % devices) for i in range(devices - 1)]
        down = [(j, i) for i, j in up]
        last = lax.slice_in_dim(array, length - 1, length, axis=dim)
        leading = lax.slice_in_dim(array, 0, 1, axis=dim)
        out[axis] = (lax.ppermute(last, axis, up), lax.ppermute(leading, axis, down))
    xb, xa = out["gx"]
    yb, ya = out["gy"]
    rows = jnp.concatenate([xb, array, xa], axis=2)
    zero_pad = ((0, 0), (0, 0), (1, 1), (0, 0))
    return jnp.concatenate([jnp.pad(yb, zero_pad), rows, jnp.pad(ya, zero_pad)], axis=3)


def halo_kernel(nx, ny, xlo, xhi, ylo, yhi, xb_o, xa_o, yb_o, ya_o,
                r_xb, r_xa, r_yb, r_ya, send_sem, recv_sem):
    gx = lax.axis_index("gx")
    gy = lax.axis_index("gy")
    plan = (
        (gx < nx - 1, {"gx": gx + 1, "gy": gy}, xhi, r_xb, 0, gx > 0, xb_o),
        (gx > 0, {"gx": gx - 1, "gy": gy}, xlo, r_xa, 1, gx < nx - 1, xa_o),
        (gy < ny - 1, {"gx": gx, "gy": gy + 1}, yhi, r_yb, 2, gy > 0, yb_o),
        (gy > 0, {"gx": gx, "gy": gy - 1}, ylo, r_ya, 3, gy < ny - 1, ya_o),
    )
    barrier = pltpu.get_barrier_semaphore()
    for has_target, target, _, _, _, _, _ in plan:
        @pl.when(has_target)
        def _():
            pl.semaphore_signal(barrier, inc=1, device_id=target, device_id_type=pl.DeviceIdType.MESH)
    peers = (gx + nx - 1) // nx + (2 * nx - 2 - gx) // nx + (gy + ny - 1) // ny + (2 * ny - 2 - gy) // ny
    pl.semaphore_wait(barrier, peers)

    def copy(target, src, slot, k):
        return pltpu.make_async_remote_copy(
            src_ref=src, dst_ref=slot, send_sem=send_sem.at[k], recv_sem=recv_sem.at[k],
            device_id=target, device_id_type=pl.DeviceIdType.MESH,
        )

    for has_target, target, src, slot, k, _, _ in plan:
        @pl.when(has_target)
        def _():
            copy(target, src, slot, k).start()
    for has_target, target, src, slot, k, has_sender, out in plan:
        @pl.when(has_target)
        def _():
            copy(target, src, slot, k).wait_send()

        @pl.when(has_sender)
        def _():
            copy(target, src, slot, k).wait_recv()
            out[...] = slot[...]

        @pl.when(jnp.logical_not(has_sender))
        def _():
            out[...] = jnp.zeros(out.shape, out.dtype)


def halo_fast(array):
    rhs, nz, bx, by = array.shape
    nx, ny = lax.axis_size("gx"), lax.axis_size("gy")
    xlo = array[:, :, 0, :].reshape(rhs * nz, by)
    xhi = array[:, :, bx - 1, :].reshape(rhs * nz, by)
    ylo = array[:, :, :, 0].reshape(-1, 128)
    yhi = array[:, :, :, by - 1].reshape(-1, 128)
    vmem = pl.BlockSpec(memory_space=pltpu.VMEM)
    shapes = [jax.ShapeDtypeStruct(a.shape, a.dtype) for a in (xlo, xhi, ylo, yhi)]
    xb, xa, yb, ya = pl.pallas_call(
        lambda *refs: halo_kernel(nx, ny, *refs),
        out_shape=shapes,
        in_specs=[vmem] * 4,
        out_specs=[vmem] * 4,
        scratch_shapes=[pltpu.VMEM(a.shape, a.dtype) for a in shapes]
        + [pltpu.SemaphoreType.DMA((4,)), pltpu.SemaphoreType.DMA((4,))],
        compiler_params=pltpu.CompilerParams(collective_id=2, has_side_effects=True),
        name="halo_exchange",
    )(xlo, xhi, ylo, yhi)
    xb = xb.reshape(rhs, nz, 1, by)
    xa = xa.reshape(rhs, nz, 1, by)
    yb = yb.reshape(rhs, nz, bx, 1)
    ya = ya.reshape(rhs, nz, bx, 1)
    rows = jnp.concatenate([xb, array, xa], axis=2)
    zero_pad = ((0, 0), (0, 0), (1, 1), (0, 0))
    return jnp.concatenate([jnp.pad(yb, zero_pad), rows, jnp.pad(ya, zero_pad)], axis=3)


def exchange_reduce(axis, other_axis, n, src, mine, rs, ag, full, send_sem, rs_sem, ag_sem):
    me = lax.axis_index(axis)
    other = lax.axis_index(other_axis)
    part = src.shape[0] // n

    def scatter(j, slot):
        return pltpu.make_async_remote_copy(
            src_ref=src.at[pl.ds(j * part, part)], dst_ref=rs.at[slot], send_sem=send_sem.at[j],
            recv_sem=rs_sem.at[slot], device_id=_device(axis, j, other_axis, other),
            device_id_type=pl.DeviceIdType.MESH,
        )

    def gather(j, slot):
        return pltpu.make_async_remote_copy(
            src_ref=mine, dst_ref=ag.at[slot], send_sem=send_sem.at[j],
            recv_sem=ag_sem.at[slot], device_id=_device(axis, j, other_axis, other),
            device_id_type=pl.DeviceIdType.MESH,
        )

    for j in range(n):
        @pl.when(j != me)
        def _():
            scatter(j, me).start()
    rs[me] = src[pl.ds(pl.multiple_of(me * part, part), part)]
    for j in range(n):
        @pl.when(j != me)
        def _():
            scatter(j, me).wait_send()
            scatter(j, j).wait_recv()
    acc = rs[0]
    for j in range(1, n):
        acc = acc + rs[j]
    mine[...] = acc
    for j in range(n):
        @pl.when(j != me)
        def _():
            gather(j, me).start()
    ag[me] = acc
    for j in range(n):
        @pl.when(j != me)
        def _():
            gather(j, me).wait_send()
            gather(j, j).wait_recv()
    for j in range(n):
        full[pl.ds(j * part, part)] = ag[j]


def cycle_kernel(nx, ny, bx, v0_ref, terms_ref, diag_ref, out_ref, gram_ref,
                 halo_x, xsend, ysend, xr, yr, send_sem, recv_sem,
                 gpad, gy_full, mine_y, rs_y, ag_y, mine_x, rs_x, ag_x,
                 y_send, y_rs, y_ag, x_send, x_rs, x_ag):
    gx = lax.axis_index("gx")
    gy = lax.axis_index("gy")
    rhs = out_ref.shape[1] // terms_ref.shape[1]
    rows, lanes = terms_ref.shape[1], terms_ref.shape[2]
    cells = out_ref.shape[1]
    zero_x = jnp.zeros(xr.shape[2:], jnp.float32)
    zero_y = jnp.zeros(yr.shape[2:], jnp.float32)
    for k in range(xr.shape[0]):
        for d in range(2):
            xr[k, d] = zero_x
            yr[k, d] = zero_y
    targets = (
        (gx < nx - 1, {"gx": gx + 1, "gy": gy}, gx > 0),
        (gx > 0, {"gx": gx - 1, "gy": gy}, gx < nx - 1),
        (gy < ny - 1, {"gx": gx, "gy": gy + 1}, gy > 0),
        (gy > 0, {"gx": gx, "gy": gy - 1}, gy < ny - 1),
    )
    barrier = pltpu.get_barrier_semaphore()
    for j in range(nx):
        @pl.when(j != gx)
        def _():
            pl.semaphore_signal(barrier, inc=1, device_id={"gx": j, "gy": gy},
                                device_id_type=pl.DeviceIdType.MESH)
    for j in range(ny):
        @pl.when(j != gy)
        def _():
            pl.semaphore_signal(barrier, inc=1, device_id={"gx": gx, "gy": j},
                                device_id_type=pl.DeviceIdType.MESH)
    pl.semaphore_wait(barrier, nx + ny - 2)

    row = lax.broadcasted_iota(jnp.int32, (rhs, rows, lanes), 1)
    lane = lax.broadcasted_iota(jnp.int32, (rhs, rows, lanes), 2)
    xpos = row % bx
    zpos = row // bx
    nzp = rows // bx
    t = [terms_ref[i][None] for i in range(6)]
    diag = diag_ref[...][None]
    trow = lax.broadcasted_iota(jnp.int32, (lanes, cells), 0)

    out_ref[0] = v0_ref[...]
    for k in range(xr.shape[0]):
        flat = out_ref[k]
        xsend[0] = out_ref[k, pl.ds(0, cells // bx, stride=bx), :]
        xsend[1] = out_ref[k, pl.ds(bx - 1, cells // bx, stride=bx), :]
        tr = flat.T
        ysend[...] = jnp.where(trow[:8] == 0, tr[0:1], jnp.where(trow[:8] == 1, tr[lanes - 1:lanes], 0.0))
        plan = (
            (xsend.at[1], xr.at[k, 0]),
            (xsend.at[0], xr.at[k, 1]),
            (ysend, yr.at[k, 0]),
            (ysend, yr.at[k, 1]),
        )

        def copy(d):
            return pltpu.make_async_remote_copy(
                src_ref=plan[d][0], dst_ref=plan[d][1], send_sem=send_sem.at[d],
                recv_sem=recv_sem.at[k, d], device_id=targets[d][1],
                device_id_type=pl.DeviceIdType.MESH,
            )

        for d in range(4):
            @pl.when(targets[d][0])
            def _():
                copy(d).start()
        for d in range(4):
            @pl.when(targets[d][0])
            def _():
                copy(d).wait_send()

            @pl.when(targets[d][2])
            def _():
                copy(d).wait_recv()

        halo_x[pl.ds(0, cells // bx, stride=bx), :] = xr[k, 0]
        halo_x[pl.ds(bx - 1, cells // bx, stride=bx), :] = xr[k, 1]
        before = yr[k, 0][1:2]
        after = yr[k, 1][0:1]
        ycols = jnp.where(trow == 0, before, jnp.where(trow == lanes - 1, after, 0.0)).T
        v = flat.reshape(rhs, rows, lanes)
        hx = halo_x[...].reshape(rhs, rows, lanes)
        hy = ycols.reshape(rhs, rows, lanes)
        zm = jnp.where(zpos == 0, 0.0, pltpu.roll(v, bx, 1))
        zp = jnp.where(zpos == nzp - 1, 0.0, pltpu.roll(v, rows - bx, 1))
        xm = jnp.where(xpos == 0, hx, pltpu.roll(v, 1, 1))
        xp = jnp.where(xpos == bx - 1, hx, pltpu.roll(v, rows - 1, 1))
        ym = jnp.where(lane == 0, hy, pltpu.roll(v, 1, 2))
        yp = jnp.where(lane == lanes - 1, hy, pltpu.roll(v, lanes - 1, 2))
        total = t[0] * zm + t[1] * zp
        total = total + t[2] * xm + t[3] * xp
        total = total + t[4] * ym + t[5] * yp
        out_ref[k + 1] = (-total / diag).reshape(cells, lanes)

    basis = out_ref.shape[0] * rhs

    def gram_step(zx, acc):
        a = jnp.concatenate(
            [out_ref[k, pl.ds(zx, rhs, stride=rows), :] for k in range(out_ref.shape[0])], axis=0)
        return acc + lax.dot_general(a, a, (((1,), (1,)), ((), ())),
                                     precision=lax.Precision.HIGHEST,
                                     preferred_element_type=jnp.float32)

    local = lax.fori_loop(0, rows, gram_step, jnp.zeros((basis, basis), jnp.float32))
    gpad[...] = jnp.zeros(gpad.shape, jnp.float32)
    gpad[0:basis, 0:basis] = local
    exchange_reduce("gy", "gx", ny, gpad, mine_y, rs_y, ag_y, gy_full, y_send, y_rs, y_ag)
    exchange_reduce("gx", "gy", nx, gy_full, mine_x, rs_x, ag_x, gram_ref, x_send, x_rs, x_ag)


def cycle_step(v0, terms, diagonal):
    rhs, nz, bx, by = v0.shape
    nx, ny = lax.axis_size("gx"), lax.axis_size("gy")
    cells = rhs * nz * bx
    vmem = pl.BlockSpec(memory_space=pltpu.VMEM)
    pad = 128
    py, px = pad // ny, pad // nx
    f32 = jnp.float32
    basis, gram = pl.pallas_call(
        lambda *refs: cycle_kernel(nx, ny, bx, *refs),
        out_shape=(jax.ShapeDtypeStruct((S + 1, cells, by), f32), jax.ShapeDtypeStruct((pad, pad), f32)),
        in_specs=[vmem] * 3,
        out_specs=(vmem, vmem),
        scratch_shapes=[
            pltpu.VMEM((cells, by), f32),
            pltpu.VMEM((2, cells // bx, by), f32),
            pltpu.VMEM((8, cells), f32),
            pltpu.VMEM((S, 2, cells // bx, by), f32),
            pltpu.VMEM((S, 2, 8, cells), f32),
            pltpu.SemaphoreType.DMA((4,)),
            pltpu.SemaphoreType.DMA((S, 4)),
            pltpu.VMEM((pad, pad), f32),
            pltpu.VMEM((pad, pad), f32),
            pltpu.VMEM((py, pad), f32),
            pltpu.VMEM((ny, py, pad), f32),
            pltpu.VMEM((ny, py, pad), f32),
            pltpu.VMEM((px, pad), f32),
            pltpu.VMEM((nx, px, pad), f32),
            pltpu.VMEM((nx, px, pad), f32),
            pltpu.SemaphoreType.DMA((ny,)),
            pltpu.SemaphoreType.DMA((ny,)),
            pltpu.SemaphoreType.DMA((ny,)),
            pltpu.SemaphoreType.DMA((nx,)),
            pltpu.SemaphoreType.DMA((nx,)),
            pltpu.SemaphoreType.DMA((nx,)),
        ],
        compiler_params=pltpu.CompilerParams(collective_id=3, has_side_effects=True),
        name="gmres_cycle",
    )(v0.reshape(cells, by), jnp.stack(terms).reshape(6, nz * bx, by), diagonal.reshape(nz * bx, by))
    return basis.reshape(BASIS, -1), gram[:BASIS, :BASIS]


def face_terms(padded, storage):
    core = padded[1:-1, 1:-1, 1:-1]
    terms = (
        (core + padded[:-2, 1:-1, 1:-1]) * 0.5,
        (core + padded[2:, 1:-1, 1:-1]) * 0.5,
        (core + padded[1:-1, :-2, 1:-1]) * 0.5,
        (core + padded[1:-1, 2:, 1:-1]) * 0.5,
        (core + padded[1:-1, 1:-1, :-2]) * 0.5,
        (core + padded[1:-1, 1:-1, 2:]) * 0.5,
    )
    diagonal = storage + terms[0] + terms[1] + terms[2] + terms[3] + terms[4] + terms[5]
    return (terms, diagonal)


def apply_off(padded, terms):
    total = terms[0] * padded[:, :-2, 1:-1, 1:-1] + terms[1] * padded[:, 2:, 1:-1, 1:-1]
    total = total + terms[2] * padded[:, 1:-1, :-2, 1:-1] + terms[3] * padded[:, 1:-1, 2:, 1:-1]
    total = total + terms[4] * padded[:, 1:-1, 1:-1, :-2] + terms[5] * padded[:, 1:-1, 1:-1, 2:]
    return total


def _device(axis, index, other_axis, other_index):
    return {axis: index, other_axis: other_index}


def allreduce_kernel(axis, other_axis, n, x_ref, o_ref, rs, ag, mine, send_sem, rs_sem, ag_sem):
    me = lax.axis_index(axis)
    other = lax.axis_index(other_axis)
    part = x_ref.shape[0] // n
    barrier = pltpu.get_barrier_semaphore()
    for j in range(n):
        @pl.when(j != me)
        def _():
            pl.semaphore_signal(
                barrier, inc=1, device_id=_device(axis, j, other_axis, other),
                device_id_type=pl.DeviceIdType.MESH,
            )
    pl.semaphore_wait(barrier, n - 1)

    def scatter(j, slot):
        return pltpu.make_async_remote_copy(
            src_ref=x_ref.at[pl.ds(j * part, part)],
            dst_ref=rs.at[slot],
            send_sem=send_sem.at[j],
            recv_sem=rs_sem.at[slot],
            device_id=_device(axis, j, other_axis, other),
            device_id_type=pl.DeviceIdType.MESH,
        )

    def gather(j, slot):
        return pltpu.make_async_remote_copy(
            src_ref=mine,
            dst_ref=ag.at[slot],
            send_sem=send_sem.at[j],
            recv_sem=ag_sem.at[slot],
            device_id=_device(axis, j, other_axis, other),
            device_id_type=pl.DeviceIdType.MESH,
        )

    for j in range(n):
        @pl.when(j != me)
        def _():
            scatter(j, me).start()

    rs[me] = x_ref[pl.ds(pl.multiple_of(me * part, part), part)]
    for j in range(n):
        @pl.when(j != me)
        def _():
            scatter(j, me).wait_send()
            scatter(j, j).wait_recv()

    acc = rs[0]
    for j in range(1, n):
        acc = acc + rs[j]
    mine[...] = acc
    for j in range(n):
        @pl.when(j != me)
        def _():
            gather(j, me).start()
    ag[me] = acc
    for j in range(n):
        @pl.when(j != me)
        def _():
            gather(j, me).wait_send()
            gather(j, j).wait_recv()
    for j in range(n):
        o_ref[pl.ds(j * part, part)] = ag[j]


def allreduce_axis(x, axis, other_axis, collective_id):
    n = lax.axis_size(axis)
    part = x.shape[0] // n
    block = (part,) + x.shape[1:]
    return pl.pallas_call(
        lambda *refs: allreduce_kernel(axis, other_axis, n, *refs),
        out_shape=jax.ShapeDtypeStruct(x.shape, x.dtype),
        in_specs=[pl.BlockSpec(memory_space=pltpu.VMEM)],
        out_specs=pl.BlockSpec(memory_space=pltpu.VMEM),
        scratch_shapes=[
            pltpu.VMEM((n,) + block, x.dtype),
            pltpu.VMEM((n,) + block, x.dtype),
            pltpu.VMEM(block, x.dtype),
            pltpu.SemaphoreType.DMA((n,)),
            pltpu.SemaphoreType.DMA((n,)),
            pltpu.SemaphoreType.DMA((n,)),
        ],
        compiler_params=pltpu.CompilerParams(collective_id=collective_id, has_side_effects=True),
        name=f"allreduce_{axis}",
    )(x)


def gram_sum(local_gram):
    size = local_gram.shape[0]
    wide = jnp.pad(local_gram, ((0, 128 - size), (0, 128 - size)))
    partial = allreduce_axis(wide, "gy", "gx", 0)
    return allreduce_axis(partial, "gx", "gy", 1)[:size, :size]


def small_solve(gram_all):
    shift_matrix = jnp.eye(BASIS, BASIS - RHS, dtype=jnp.float32) + jnp.eye(
        BASIS, BASIS - RHS, k=-RHS, dtype=jnp.float32
    )
    first_block = jnp.eye(BASIS, RHS, dtype=jnp.float32)
    hp = lax.Precision.HIGHEST
    gram_shift = jnp.dot(gram_all, shift_matrix, precision=hp)
    normal = jnp.dot(shift_matrix.T, gram_shift, precision=hp)
    right_side = jnp.dot(gram_shift.T, first_block, precision=hp)
    lower = jnp.linalg.cholesky(normal)
    y = jax.scipy.linalg.cho_solve((lower, True), right_side)
    coeffs = first_block - jnp.dot(shift_matrix, y, precision=hp)
    return (y, coeffs)


def shards(pumping, conductivity, capacity):
    hp = lax.Precision.HIGHEST
    shape = pumping.shape
    cond_halo = padded_2(conductivity, (("gx", 1), ("gy", 2)), 1)
    cond_pad = jnp.pad(cond_halo, ((1, 1), (0, 0), (0, 0)))
    terms, diagonal = face_terms(cond_pad, capacity)
    solution = jnp.zeros(shape, jnp.float32)
    residual = pumping / diagonal
    for restart in range(CYCLES):
        stacked, gram_all = cycle_step(residual, terms, diagonal)
        y, coeffs = small_solve(gram_all)
        solution = solution + jnp.dot(y.T, stacked[: BASIS - RHS], precision=hp).reshape(shape)
        residual = jnp.dot(coeffs.T, stacked, precision=hp).reshape(shape)
    return (solution, residual)


def solution(mesh):
    return jax.shard_map(
        shards,
        mesh=mesh,
        in_specs=(P(None, None, "gx", "gy"), P(None, "gx", "gy"), P(None, "gx", "gy")),
        out_specs=(P(None, None, "gx", "gy"), P(None, None, "gx", "gy")),
        check_vma=False,
    )
```

```python
import jax
import jax.numpy as jnp
from jax import lax
from jax.sharding import PartitionSpec as P
from jax.experimental import pallas as pl
from jax.experimental.pallas import tpu as pltpu

RHS = 16
S = 4
CYCLES = 5
BASIS = 80


def padded_2(array, sides, width):
    for axis, dim in sides:
        devices, length = (lax.axis_size(axis), array.shape[dim])
        up = [(i, (i + 1) % devices) for i in range(devices - 1)]
        down = [(j, i) for i, j in up]
        last = lax.slice_in_dim(array, length - width, length, axis=dim)
        leading = lax.slice_in_dim(array, 0, width, axis=dim)
        before = lax.ppermute(last, axis, up)
        after = lax.ppermute(leading, axis, down)
        array = jnp.concatenate([before, array, after], axis=dim)
    return array


def exchange_reduce(axis, other_axis, n, src, mine, rs, ag, full, send_sem, rs_sem, ag_sem):
    me = lax.axis_index(axis)
    other = lax.axis_index(other_axis)
    part = src.shape[0] // n

    def scatter(j, slot):
        return pltpu.make_async_remote_copy(
            src_ref=src.at[pl.ds(j * part, part)], dst_ref=rs.at[slot], send_sem=send_sem.at[j],
            recv_sem=rs_sem.at[slot], device_id=_device(axis, j, other_axis, other),
            device_id_type=pl.DeviceIdType.MESH,
        )

    def gather(j, slot):
        return pltpu.make_async_remote_copy(
            src_ref=mine, dst_ref=ag.at[slot], send_sem=send_sem.at[j],
            recv_sem=ag_sem.at[slot], device_id=_device(axis, j, other_axis, other),
            device_id_type=pl.DeviceIdType.MESH,
        )

    for j in range(n):
        @pl.when(j != me)
        def _():
            scatter(j, me).start()
    rs[me] = src[pl.ds(pl.multiple_of(me * part, part), part)]
    for j in range(n):
        @pl.when(j != me)
        def _():
            scatter(j, me).wait_send()
            scatter(j, j).wait_recv()
    acc = rs[0]
    for j in range(1, n):
        acc = acc + rs[j]
    mine[...] = acc
    for j in range(n):
        @pl.when(j != me)
        def _():
            gather(j, me).start()
    ag[me] = acc
    for j in range(n):
        @pl.when(j != me)
        def _():
            gather(j, me).wait_send()
            gather(j, j).wait_recv()
    for j in range(n):
        full[pl.ds(j * part, part)] = ag[j]


def reduce_kernel(nx, ny, x_ref, o_ref, gy_full, mine_y, rs_y, ag_y, mine_x, rs_x, ag_x,
                  y_send, y_rs, y_ag, x_send, x_rs, x_ag):
    gx = lax.axis_index("gx")
    gy = lax.axis_index("gy")
    barrier = pltpu.get_barrier_semaphore()
    for j in range(nx):
        @pl.when(j != gx)
        def _():
            pl.semaphore_signal(barrier, inc=1, device_id={"gx": j, "gy": gy},
                                device_id_type=pl.DeviceIdType.MESH)
    for j in range(ny):
        @pl.when(j != gy)
        def _():
            pl.semaphore_signal(barrier, inc=1, device_id={"gx": gx, "gy": j},
                                device_id_type=pl.DeviceIdType.MESH)
    pl.semaphore_wait(barrier, nx + ny - 2)
    exchange_reduce("gy", "gx", ny, x_ref, mine_y, rs_y, ag_y, gy_full, y_send, y_rs, y_ag)
    exchange_reduce("gx", "gy", nx, gy_full, mine_x, rs_x, ag_x, o_ref, x_send, x_rs, x_ag)


def gram_sum(local_gram):
    size = local_gram.shape[0]
    nx, ny = lax.axis_size("gx"), lax.axis_size("gy")
    pad = 128
    py, px = pad // ny, pad // nx
    f32 = jnp.float32
    wide = jnp.pad(local_gram, ((0, pad - size), (0, pad - size)))
    vmem = pl.BlockSpec(memory_space=pltpu.VMEM)
    total = pl.pallas_call(
        lambda *refs: reduce_kernel(nx, ny, *refs),
        out_shape=jax.ShapeDtypeStruct((pad, pad), f32),
        in_specs=[vmem],
        out_specs=vmem,
        scratch_shapes=[
            pltpu.VMEM((pad, pad), f32),
            pltpu.VMEM((py, pad), f32),
            pltpu.VMEM((ny, py, pad), f32),
            pltpu.VMEM((ny, py, pad), f32),
            pltpu.VMEM((px, pad), f32),
            pltpu.VMEM((nx, px, pad), f32),
            pltpu.VMEM((nx, px, pad), f32),
            pltpu.SemaphoreType.DMA((ny,)),
            pltpu.SemaphoreType.DMA((ny,)),
            pltpu.SemaphoreType.DMA((ny,)),
            pltpu.SemaphoreType.DMA((nx,)),
            pltpu.SemaphoreType.DMA((nx,)),
            pltpu.SemaphoreType.DMA((nx,)),
        ],
        compiler_params=pltpu.CompilerParams(collective_id=4, has_side_effects=True),
        name="gram_allreduce",
    )(wide)
    return total[:size, :size]


def krylov_kernel(nx, ny, bx, v0_ref, terms_ref, diag_ref, out_ref,
                  halo_x, xsend, ysend, xr, yr, send_sem, recv_sem):
    gx = lax.axis_index("gx")
    gy = lax.axis_index("gy")
    rhs = out_ref.shape[1] // terms_ref.shape[1]
    rows, lanes = terms_ref.shape[1], terms_ref.shape[2]
    cells = out_ref.shape[1]
    zero_x = jnp.zeros(xr.shape[2:], jnp.float32)
    zero_y = jnp.zeros(yr.shape[2:], jnp.float32)
    for k in range(xr.shape[0]):
        for d in range(2):
            xr[k, d] = zero_x
            yr[k, d] = zero_y
    targets = (
        (gx < nx - 1, {"gx": gx + 1, "gy": gy}, gx > 0),
        (gx > 0, {"gx": gx - 1, "gy": gy}, gx < nx - 1),
        (gy < ny - 1, {"gx": gx, "gy": gy + 1}, gy > 0),
        (gy > 0, {"gx": gx, "gy": gy - 1}, gy < ny - 1),
    )
    barrier = pltpu.get_barrier_semaphore()
    for has_target, target, _ in targets:
        @pl.when(has_target)
        def _():
            pl.semaphore_signal(barrier, inc=1, device_id=target, device_id_type=pl.DeviceIdType.MESH)
    peers = (gx + nx - 1) // nx + (2 * nx - 2 - gx) // nx + (gy + ny - 1) // ny + (2 * ny - 2 - gy) // ny
    pl.semaphore_wait(barrier, peers)

    row = lax.broadcasted_iota(jnp.int32, (rhs, rows, lanes), 1)
    lane = lax.broadcasted_iota(jnp.int32, (rhs, rows, lanes), 2)
    xpos = row % bx
    zpos = row // bx
    nzp = rows // bx
    t = [terms_ref[i][None] for i in range(6)]
    diag = diag_ref[...][None]
    trow = lax.broadcasted_iota(jnp.int32, (lanes, cells), 0)

    out_ref[0] = v0_ref[...]
    for k in range(xr.shape[0]):
        flat = out_ref[k]
        xsend[0] = out_ref[k, pl.ds(0, cells // bx, stride=bx), :]
        xsend[1] = out_ref[k, pl.ds(bx - 1, cells // bx, stride=bx), :]
        tr = flat.T
        ysend[...] = jnp.where(trow[:8] == 0, tr[0:1], jnp.where(trow[:8] == 1, tr[lanes - 1:lanes], 0.0))
        plan = (
            (xsend.at[1], xr.at[k, 0]),
            (xsend.at[0], xr.at[k, 1]),
            (ysend, yr.at[k, 0]),
            (ysend, yr.at[k, 1]),
        )

        def copy(d):
            return pltpu.make_async_remote_copy(
                src_ref=plan[d][0], dst_ref=plan[d][1], send_sem=send_sem.at[d],
                recv_sem=recv_sem.at[k, d], device_id=targets[d][1],
                device_id_type=pl.DeviceIdType.MESH,
            )

        for d in range(4):
            @pl.when(targets[d][0])
            def _():
                copy(d).start()
        for d in range(4):
            @pl.when(targets[d][0])
            def _():
                copy(d).wait_send()

            @pl.when(targets[d][2])
            def _():
                copy(d).wait_recv()

        halo_x[pl.ds(0, cells // bx, stride=bx), :] = xr[k, 0]
        halo_x[pl.ds(bx - 1, cells // bx, stride=bx), :] = xr[k, 1]
        before = yr[k, 0][1:2]
        after = yr[k, 1][0:1]
        ycols = jnp.where(trow == 0, before, jnp.where(trow == lanes - 1, after, 0.0)).T
        v = flat.reshape(rhs, rows, lanes)
        hx = halo_x[...].reshape(rhs, rows, lanes)
        hy = ycols.reshape(rhs, rows, lanes)
        zm = jnp.where(zpos == 0, 0.0, pltpu.roll(v, bx, 1))
        zp = jnp.where(zpos == nzp - 1, 0.0, pltpu.roll(v, rows - bx, 1))
        xm = jnp.where(xpos == 0, hx, pltpu.roll(v, 1, 1))
        xp = jnp.where(xpos == bx - 1, hx, pltpu.roll(v, rows - 1, 1))
        ym = jnp.where(lane == 0, hy, pltpu.roll(v, 1, 2))
        yp = jnp.where(lane == lanes - 1, hy, pltpu.roll(v, lanes - 1, 2))
        total = t[0] * zm + t[1] * zp
        total = total + t[2] * xm + t[3] * xp
        total = total + t[4] * ym + t[5] * yp
        out_ref[k + 1] = (-total / diag).reshape(cells, lanes)


def krylov_basis(v0, terms, diagonal):
    rhs, nz, bx, by = v0.shape
    nx, ny = lax.axis_size("gx"), lax.axis_size("gy")
    cells = rhs * nz * bx
    vmem = pl.BlockSpec(memory_space=pltpu.VMEM)
    out = pl.pallas_call(
        lambda *refs: krylov_kernel(nx, ny, bx, *refs),
        out_shape=jax.ShapeDtypeStruct((S + 1, cells, by), jnp.float32),
        in_specs=[vmem] * 3,
        out_specs=vmem,
        scratch_shapes=[
            pltpu.VMEM((cells, by), jnp.float32),
            pltpu.VMEM((2, cells // bx, by), jnp.float32),
            pltpu.VMEM((8, cells), jnp.float32),
            pltpu.VMEM((S, 2, cells // bx, by), jnp.float32),
            pltpu.VMEM((S, 2, 8, cells), jnp.float32),
            pltpu.SemaphoreType.DMA((4,)),
            pltpu.SemaphoreType.DMA((S, 4)),
        ],
        compiler_params=pltpu.CompilerParams(collective_id=3, has_side_effects=True),
        name="krylov_basis",
    )(v0.reshape(cells, by), jnp.stack(terms).reshape(6, nz * bx, by), diagonal.reshape(nz * bx, by))
    return out.reshape(S + 1, rhs, nz, bx, by)


def face_terms(padded, storage):
    core = padded[1:-1, 1:-1, 1:-1]
    terms = (
        (core + padded[:-2, 1:-1, 1:-1]) * 0.5,
        (core + padded[2:, 1:-1, 1:-1]) * 0.5,
        (core + padded[1:-1, :-2, 1:-1]) * 0.5,
        (core + padded[1:-1, 2:, 1:-1]) * 0.5,
        (core + padded[1:-1, 1:-1, :-2]) * 0.5,
        (core + padded[1:-1, 1:-1, 2:]) * 0.5,
    )
    diagonal = storage + terms[0] + terms[1] + terms[2] + terms[3] + terms[4] + terms[5]
    return (terms, diagonal)


def _device(axis, index, other_axis, other_index):
    return {axis: index, other_axis: other_index}


def small_solve(gram_all):
    shift_matrix = jnp.eye(BASIS, BASIS - RHS, dtype=jnp.float32) + jnp.eye(
        BASIS, BASIS - RHS, k=-RHS, dtype=jnp.float32
    )
    first_block = jnp.eye(BASIS, RHS, dtype=jnp.float32)
    hp = lax.Precision.HIGHEST
    gram_shift = jnp.dot(gram_all, shift_matrix, precision=hp)
    normal = jnp.dot(shift_matrix.T, gram_shift, precision=hp)
    right_side = jnp.dot(gram_shift.T, first_block, precision=hp)
    lower = jnp.linalg.cholesky(normal)
    y = jax.scipy.linalg.cho_solve((lower, True), right_side)
    coeffs = first_block - jnp.dot(shift_matrix, y, precision=hp)
    return (y, coeffs)


def shards(pumping, conductivity, capacity):
    hp = lax.Precision.HIGHEST
    shape = pumping.shape
    cond_halo = padded_2(conductivity, (("gx", 1), ("gy", 2)), 1)
    cond_pad = jnp.pad(cond_halo, ((1, 1), (0, 0), (0, 0)))
    terms, diagonal = face_terms(cond_pad, capacity)
    solution = jnp.zeros(shape, jnp.float32)
    residual = pumping / diagonal
    for restart in range(CYCLES):
        stacked = krylov_basis(residual, terms, diagonal).reshape(BASIS, -1)
        local_gram = jnp.dot(stacked, stacked.T, precision=hp)
        gram_all = gram_sum(local_gram)
        y, coeffs = small_solve(gram_all)
        y_full = jnp.concatenate([y, jnp.zeros((RHS, RHS), jnp.float32)], axis=0)
        both = jnp.dot(jnp.concatenate([y_full, coeffs], axis=1).T, stacked, precision=hp)
        solution = solution + both[:RHS].reshape(shape)
        residual = both[RHS:].reshape(shape)
    return (solution, residual)


def solution(mesh):
    return jax.shard_map(
        shards,
        mesh=mesh,
        in_specs=(P(None, None, "gx", "gy"), P(None, "gx", "gy"), P(None, "gx", "gy")),
        out_specs=(P(None, None, "gx", "gy"), P(None, None, "gx", "gy")),
        check_vma=False,
    )
```

```python
import jax
import jax.numpy as jnp
from jax import lax
from jax.sharding import PartitionSpec as P
from jax.experimental import pallas as pl
from jax.experimental.pallas import tpu as pltpu

RHS = 16
S = 4
CYCLES = 5
BASIS = 80


def padded_2(array, sides, width):
    for axis, dim in sides:
        devices, length = (lax.axis_size(axis), array.shape[dim])
        up = [(i, (i + 1) % devices) for i in range(devices - 1)]
        down = [(j, i) for i, j in up]
        last = lax.slice_in_dim(array, length - width, length, axis=dim)
        leading = lax.slice_in_dim(array, 0, width, axis=dim)
        before = lax.ppermute(last, axis, up)
        after = lax.ppermute(leading, axis, down)
        array = jnp.concatenate([before, array, after], axis=dim)
    return array


def exchange_reduce(axis, other_axis, n, src, mine, rs, ag, full, send_sem, rs_sem, ag_sem):
    me = lax.axis_index(axis)
    other = lax.axis_index(other_axis)
    part = src.shape[0] // n

    def scatter(j, slot):
        return pltpu.make_async_remote_copy(
            src_ref=src.at[pl.ds(j * part, part)], dst_ref=rs.at[slot], send_sem=send_sem.at[j],
            recv_sem=rs_sem.at[slot], device_id=_device(axis, j, other_axis, other),
            device_id_type=pl.DeviceIdType.MESH,
        )

    def gather(j, slot):
        return pltpu.make_async_remote_copy(
            src_ref=mine, dst_ref=ag.at[slot], send_sem=send_sem.at[j],
            recv_sem=ag_sem.at[slot], device_id=_device(axis, j, other_axis, other),
            device_id_type=pl.DeviceIdType.MESH,
        )

    for j in range(n):
        @pl.when(j != me)
        def _():
            scatter(j, me).start()
    rs[me] = src[pl.ds(pl.multiple_of(me * part, part), part)]
    for j in range(n):
        @pl.when(j != me)
        def _():
            scatter(j, me).wait_send()
            scatter(j, j).wait_recv()
    acc = rs[0]
    for j in range(1, n):
        acc = acc + rs[j]
    mine[...] = acc
    for j in range(n):
        @pl.when(j != me)
        def _():
            gather(j, me).start()
    ag[me] = acc
    for j in range(n):
        @pl.when(j != me)
        def _():
            gather(j, me).wait_send()
            gather(j, j).wait_recv()
    for j in range(n):
        full[pl.ds(j * part, part)] = ag[j]


def reduce_kernel(nx, ny, x_ref, o_ref, gy_full, mine_y, rs_y, ag_y, mine_x, rs_x, ag_x,
                  y_send, y_rs, y_ag, x_send, x_rs, x_ag):
    gx = lax.axis_index("gx")
    gy = lax.axis_index("gy")
    barrier = pltpu.get_barrier_semaphore()
    for j in range(nx):
        @pl.when(j != gx)
        def _():
            pl.semaphore_signal(barrier, inc=1, device_id={"gx": j, "gy": gy},
                                device_id_type=pl.DeviceIdType.MESH)
    for j in range(ny):
        @pl.when(j != gy)
        def _():
            pl.semaphore_signal(barrier, inc=1, device_id={"gx": gx, "gy": j},
                                device_id_type=pl.DeviceIdType.MESH)
    pl.semaphore_wait(barrier, nx + ny - 2)
    exchange_reduce("gy", "gx", ny, x_ref, mine_y, rs_y, ag_y, gy_full, y_send, y_rs, y_ag)
    exchange_reduce("gx", "gy", nx, gy_full, mine_x, rs_x, ag_x, o_ref, x_send, x_rs, x_ag)


def gram_sum(local_gram):
    size = local_gram.shape[0]
    nx, ny = lax.axis_size("gx"), lax.axis_size("gy")
    pad = 128
    py, px = pad // ny, pad // nx
    f32 = jnp.float32
    wide = jnp.pad(local_gram, ((0, pad - size), (0, pad - size)))
    vmem = pl.BlockSpec(memory_space=pltpu.VMEM)
    total = pl.pallas_call(
        lambda *refs: reduce_kernel(nx, ny, *refs),
        out_shape=jax.ShapeDtypeStruct((pad, pad), f32),
        in_specs=[vmem],
        out_specs=vmem,
        scratch_shapes=[
            pltpu.VMEM((pad, pad), f32),
            pltpu.VMEM((py, pad), f32),
            pltpu.VMEM((ny, py, pad), f32),
            pltpu.VMEM((ny, py, pad), f32),
            pltpu.VMEM((px, pad), f32),
            pltpu.VMEM((nx, px, pad), f32),
            pltpu.VMEM((nx, px, pad), f32),
            pltpu.SemaphoreType.DMA((ny,)),
            pltpu.SemaphoreType.DMA((ny,)),
            pltpu.SemaphoreType.DMA((ny,)),
            pltpu.SemaphoreType.DMA((nx,)),
            pltpu.SemaphoreType.DMA((nx,)),
            pltpu.SemaphoreType.DMA((nx,)),
        ],
        compiler_params=pltpu.CompilerParams(collective_id=4, has_side_effects=True),
        name="gram_allreduce",
    )(wide)
    return total


def solve_kernel(g_ref, y_ref):
    n, r = BASIS - RHS, RHS
    g = g_ref[...]
    lanes = g.shape[1]
    a1 = g[0:n] + g[r:r + n]
    lane = lax.broadcasted_iota(jnp.int32, (n, lanes), 1)
    row = lax.broadcasted_iota(jnp.int32, (n, lanes), 0)
    normal = a1 + pltpu.roll(a1, lanes - r, 1)
    m = jnp.where(lane < n, normal, jnp.where(lane < n + r, pltpu.roll(a1, n, 1), 0.0))
    upper = []
    for j in range(n):
        rowj = m[j:j + 1, :]
        d = jnp.sqrt(rowj[:, j:j + 1])
        urow = rowj / d
        upper.append(urow)
        col = jnp.where(row > j, m[:, j:j + 1] / d, 0.0)
        m = m - col * urow
    w = jnp.concatenate(upper, axis=0)
    rhs_lane = jnp.logical_and(lane >= n, lane < n + r)
    ys = [None] * n
    for j in reversed(range(n)):
        yj = jnp.where(rhs_lane[0:1], w[j:j + 1, :] / w[j:j + 1, j:j + 1], 0.0)
        ys[j] = yj
        col = jnp.where(row < j, w[:, j:j + 1], 0.0)
        w = w - col * yj
    y = jnp.concatenate(ys, axis=0)
    y_ref[...] = pltpu.roll(y, lanes - n, 1)[:, 0:r]


def small_solve_fast(gram_pad):
    y = pl.pallas_call(
        solve_kernel,
        out_shape=jax.ShapeDtypeStruct((BASIS - RHS, RHS), jnp.float32),
        in_specs=[pl.BlockSpec(memory_space=pltpu.VMEM)],
        out_specs=pl.BlockSpec(memory_space=pltpu.VMEM),
        name="small_solve",
    )(gram_pad)
    shift_matrix = jnp.eye(BASIS, BASIS - RHS, dtype=jnp.float32) + jnp.eye(
        BASIS, BASIS - RHS, k=-RHS, dtype=jnp.float32
    )
    first_block = jnp.eye(BASIS, RHS, dtype=jnp.float32)
    coeffs = first_block - jnp.dot(shift_matrix, y, precision=lax.Precision.HIGHEST)
    return (y, coeffs)


def krylov_kernel(nx, ny, bx, v0_ref, terms_ref, diag_ref, out_ref,
                  halo_x, xsend, ysend, xr, yr, send_sem, recv_sem):
    gx = lax.axis_index("gx")
    gy = lax.axis_index("gy")
    rhs = out_ref.shape[1] // terms_ref.shape[1]
    rows, lanes = terms_ref.shape[1], terms_ref.shape[2]
    cells = out_ref.shape[1]
    zero_x = jnp.zeros(xr.shape[2:], jnp.float32)
    zero_y = jnp.zeros(yr.shape[2:], jnp.float32)
    for k in range(xr.shape[0]):
        for d in range(2):
            xr[k, d] = zero_x
            yr[k, d] = zero_y
    targets = (
        (gx < nx - 1, {"gx": gx + 1, "gy": gy}, gx > 0),
        (gx > 0, {"gx": gx - 1, "gy": gy}, gx < nx - 1),
        (gy < ny - 1, {"gx": gx, "gy": gy + 1}, gy > 0),
        (gy > 0, {"gx": gx, "gy": gy - 1}, gy < ny - 1),
    )
    barrier = pltpu.get_barrier_semaphore()
    for has_target, target, _ in targets:
        @pl.when(has_target)
        def _():
            pl.semaphore_signal(barrier, inc=1, device_id=target, device_id_type=pl.DeviceIdType.MESH)
    peers = (gx + nx - 1) // nx + (2 * nx - 2 - gx) // nx + (gy + ny - 1) // ny + (2 * ny - 2 - gy) // ny
    pl.semaphore_wait(barrier, peers)

    row = lax.broadcasted_iota(jnp.int32, (rhs, rows, lanes), 1)
    lane = lax.broadcasted_iota(jnp.int32, (rhs, rows, lanes), 2)
    xpos = row % bx
    zpos = row // bx
    nzp = rows // bx
    t = [terms_ref[i][None] for i in range(6)]
    diag = diag_ref[...][None]
    trow = lax.broadcasted_iota(jnp.int32, (lanes, cells), 0)

    out_ref[0] = v0_ref[...]
    for k in range(xr.shape[0]):
        flat = out_ref[k]
        xsend[0] = out_ref[k, pl.ds(0, cells // bx, stride=bx), :]
        xsend[1] = out_ref[k, pl.ds(bx - 1, cells // bx, stride=bx), :]
        tr = flat.T
        ysend[...] = jnp.where(trow[:8] == 0, tr[0:1], jnp.where(trow[:8] == 1, tr[lanes - 1:lanes], 0.0))
        plan = (
            (xsend.at[1], xr.at[k, 0]),
            (xsend.at[0], xr.at[k, 1]),
            (ysend, yr.at[k, 0]),
            (ysend, yr.at[k, 1]),
        )

        def copy(d):
            return pltpu.make_async_remote_copy(
                src_ref=plan[d][0], dst_ref=plan[d][1], send_sem=send_sem.at[d],
                recv_sem=recv_sem.at[k, d], device_id=targets[d][1],
                device_id_type=pl.DeviceIdType.MESH,
            )

        for d in range(4):
            @pl.when(targets[d][0])
            def _():
                copy(d).start()
        for d in range(4):
            @pl.when(targets[d][0])
            def _():
                copy(d).wait_send()

            @pl.when(targets[d][2])
            def _():
                copy(d).wait_recv()

        halo_x[pl.ds(0, cells // bx, stride=bx), :] = xr[k, 0]
        halo_x[pl.ds(bx - 1, cells // bx, stride=bx), :] = xr[k, 1]
        before = yr[k, 0][1:2]
        after = yr[k, 1][0:1]
        ycols = jnp.where(trow == 0, before, jnp.where(trow == lanes - 1, after, 0.0)).T
        v = flat.reshape(rhs, rows, lanes)
        hx = halo_x[...].reshape(rhs, rows, lanes)
        hy = ycols.reshape(rhs, rows, lanes)
        zm = jnp.where(zpos == 0, 0.0, pltpu.roll(v, bx, 1))
        zp = jnp.where(zpos == nzp - 1, 0.0, pltpu.roll(v, rows - bx, 1))
        xm = jnp.where(xpos == 0, hx, pltpu.roll(v, 1, 1))
        xp = jnp.where(xpos == bx - 1, hx, pltpu.roll(v, rows - 1, 1))
        ym = jnp.where(lane == 0, hy, pltpu.roll(v, 1, 2))
        yp = jnp.where(lane == lanes - 1, hy, pltpu.roll(v, lanes - 1, 2))
        total = t[0] * zm + t[1] * zp
        total = total + t[2] * xm + t[3] * xp
        total = total + t[4] * ym + t[5] * yp
        out_ref[k + 1] = (-total / diag).reshape(cells, lanes)


def krylov_basis(v0, terms, diagonal):
    rhs, nz, bx, by = v0.shape
    nx, ny = lax.axis_size("gx"), lax.axis_size("gy")
    cells = rhs * nz * bx
    vmem = pl.BlockSpec(memory_space=pltpu.VMEM)
    out = pl.pallas_call(
        lambda *refs: krylov_kernel(nx, ny, bx, *refs),
        out_shape=jax.ShapeDtypeStruct((S + 1, cells, by), jnp.float32),
        in_specs=[vmem] * 3,
        out_specs=vmem,
        scratch_shapes=[
            pltpu.VMEM((cells, by), jnp.float32),
            pltpu.VMEM((2, cells // bx, by), jnp.float32),
            pltpu.VMEM((8, cells), jnp.float32),
            pltpu.VMEM((S, 2, cells // bx, by), jnp.float32),
            pltpu.VMEM((S, 2, 8, cells), jnp.float32),
            pltpu.SemaphoreType.DMA((4,)),
            pltpu.SemaphoreType.DMA((S, 4)),
        ],
        compiler_params=pltpu.CompilerParams(collective_id=3, has_side_effects=True),
        name="krylov_basis",
    )(v0.reshape(cells, by), jnp.stack(terms).reshape(6, nz * bx, by), diagonal.reshape(nz * bx, by))
    return out.reshape(S + 1, rhs, nz, bx, by)


def face_terms(padded, storage):
    core = padded[1:-1, 1:-1, 1:-1]
    terms = (
        (core + padded[:-2, 1:-1, 1:-1]) * 0.5,
        (core + padded[2:, 1:-1, 1:-1]) * 0.5,
        (core + padded[1:-1, :-2, 1:-1]) * 0.5,
        (core + padded[1:-1, 2:, 1:-1]) * 0.5,
        (core + padded[1:-1, 1:-1, :-2]) * 0.5,
        (core + padded[1:-1, 1:-1, 2:]) * 0.5,
    )
    diagonal = storage + terms[0] + terms[1] + terms[2] + terms[3] + terms[4] + terms[5]
    return (terms, diagonal)


def _device(axis, index, other_axis, other_index):
    return {axis: index, other_axis: other_index}


def small_solve(gram_all):
    shift_matrix = jnp.eye(BASIS, BASIS - RHS, dtype=jnp.float32) + jnp.eye(
        BASIS, BASIS - RHS, k=-RHS, dtype=jnp.float32
    )
    first_block = jnp.eye(BASIS, RHS, dtype=jnp.float32)
    hp = lax.Precision.HIGHEST
    gram_shift = jnp.dot(gram_all, shift_matrix, precision=hp)
    normal = jnp.dot(shift_matrix.T, gram_shift, precision=hp)
    right_side = jnp.dot(gram_shift.T, first_block, precision=hp)
    lower = jnp.linalg.cholesky(normal)
    y = jax.scipy.linalg.cho_solve((lower, True), right_side)
    coeffs = first_block - jnp.dot(shift_matrix, y, precision=hp)
    return (y, coeffs)


def shards(pumping, conductivity, capacity):
    hp = lax.Precision.HIGHEST
    shape = pumping.shape
    cond_halo = padded_2(conductivity, (("gx", 1), ("gy", 2)), 1)
    cond_pad = jnp.pad(cond_halo, ((1, 1), (0, 0), (0, 0)))
    terms, diagonal = face_terms(cond_pad, capacity)
    solution = jnp.zeros(shape, jnp.float32)
    residual = pumping / diagonal
    for restart in range(CYCLES):
        stacked = krylov_basis(residual, terms, diagonal).reshape(BASIS, -1)
        local_gram = jnp.dot(stacked, stacked.T, precision=hp)
        y, coeffs = small_solve_fast(gram_sum(local_gram))
        y_full = jnp.concatenate([y, jnp.zeros((RHS, RHS), jnp.float32)], axis=0)
        both = jnp.dot(jnp.concatenate([y_full, coeffs], axis=1).T, stacked, precision=hp)
        solution = solution + both[:RHS].reshape(shape)
        residual = both[RHS:].reshape(shape)
    return (solution, residual)


def solution(mesh):
    return jax.shard_map(
        shards,
        mesh=mesh,
        in_specs=(P(None, None, "gx", "gy"), P(None, "gx", "gy"), P(None, "gx", "gy")),
        out_specs=(P(None, None, "gx", "gy"), P(None, None, "gx", "gy")),
        check_vma=False,
    )
```

```python
import jax
import jax.numpy as jnp
from jax import lax
from jax.sharding import PartitionSpec as P
from jax.experimental import pallas as pl
from jax.experimental.pallas import tpu as pltpu

RHS = 16
S = 4
CYCLES = 5
BASIS = 80


def padded_2(array, sides, width):
    for axis, dim in sides:
        devices, length = (lax.axis_size(axis), array.shape[dim])
        up = [(i, (i + 1) % devices) for i in range(devices - 1)]
        down = [(j, i) for i, j in up]
        last = lax.slice_in_dim(array, length - width, length, axis=dim)
        leading = lax.slice_in_dim(array, 0, width, axis=dim)
        before = lax.ppermute(last, axis, up)
        after = lax.ppermute(leading, axis, down)
        array = jnp.concatenate([before, array, after], axis=dim)
    return array


def exchange_reduce(axis, other_axis, n, src, mine, rs, ag, full, send_sem, rs_sem, ag_sem):
    me = lax.axis_index(axis)
    other = lax.axis_index(other_axis)
    part = src.shape[0] // n

    def scatter(j, slot):
        return pltpu.make_async_remote_copy(
            src_ref=src.at[pl.ds(j * part, part)], dst_ref=rs.at[slot], send_sem=send_sem.at[j],
            recv_sem=rs_sem.at[slot], device_id=_device(axis, j, other_axis, other),
            device_id_type=pl.DeviceIdType.MESH,
        )

    def gather(j, slot):
        return pltpu.make_async_remote_copy(
            src_ref=mine, dst_ref=ag.at[slot], send_sem=send_sem.at[j],
            recv_sem=ag_sem.at[slot], device_id=_device(axis, j, other_axis, other),
            device_id_type=pl.DeviceIdType.MESH,
        )

    for j in range(n):
        @pl.when(j != me)
        def _():
            scatter(j, me).start()
    rs[me] = src[pl.ds(pl.multiple_of(me * part, part), part)]
    for j in range(n):
        @pl.when(j != me)
        def _():
            scatter(j, me).wait_send()
            scatter(j, j).wait_recv()
    acc = rs[0]
    for j in range(1, n):
        acc = acc + rs[j]
    mine[...] = acc
    for j in range(n):
        @pl.when(j != me)
        def _():
            gather(j, me).start()
    ag[me] = acc
    for j in range(n):
        @pl.when(j != me)
        def _():
            gather(j, me).wait_send()
            gather(j, j).wait_recv()
    for j in range(n):
        full[pl.ds(j * part, part)] = ag[j]


def reduce_kernel(nx, ny, x_ref, o_ref, gy_full, mine_y, rs_y, ag_y, mine_x, rs_x, ag_x,
                  y_send, y_rs, y_ag, x_send, x_rs, x_ag):
    gx = lax.axis_index("gx")
    gy = lax.axis_index("gy")
    barrier = pltpu.get_barrier_semaphore()
    for j in range(nx):
        @pl.when(j != gx)
        def _():
            pl.semaphore_signal(barrier, inc=1, device_id={"gx": j, "gy": gy},
                                device_id_type=pl.DeviceIdType.MESH)
    for j in range(ny):
        @pl.when(j != gy)
        def _():
            pl.semaphore_signal(barrier, inc=1, device_id={"gx": gx, "gy": j},
                                device_id_type=pl.DeviceIdType.MESH)
    pl.semaphore_wait(barrier, nx + ny - 2)
    part = x_ref.shape[0] // ny

    def to_y(j, src, dst, slot, sem):
        return pltpu.make_async_remote_copy(
            src_ref=src, dst_ref=dst.at[slot], send_sem=y_send.at[j], recv_sem=sem.at[slot],
            device_id={"gx": gx, "gy": j}, device_id_type=pl.DeviceIdType.MESH,
        )

    def to_x(j, slot):
        return pltpu.make_async_remote_copy(
            src_ref=mine_y, dst_ref=rs_x.at[slot], send_sem=x_send.at[j], recv_sem=x_rs.at[slot],
            device_id={"gx": j, "gy": gy}, device_id_type=pl.DeviceIdType.MESH,
        )

    for j in range(ny):
        @pl.when(j != gy)
        def _():
            to_y(j, x_ref.at[pl.ds(j * part, part)], rs_y, gy, y_rs).start()
    rs_y[gy] = x_ref[pl.ds(pl.multiple_of(gy * part, part), part)]
    for j in range(ny):
        @pl.when(j != gy)
        def _():
            to_y(j, x_ref.at[pl.ds(j * part, part)], rs_y, gy, y_rs).wait_send()
            to_y(j, x_ref.at[pl.ds(j * part, part)], rs_y, j, y_rs).wait_recv()
    acc = rs_y[0]
    for j in range(1, ny):
        acc = acc + rs_y[j]
    mine_y[...] = acc
    for j in range(nx):
        @pl.when(j != gx)
        def _():
            to_x(j, gx).start()
    rs_x[gx] = acc
    for j in range(nx):
        @pl.when(j != gx)
        def _():
            to_x(j, gx).wait_send()
            to_x(j, j).wait_recv()
    acc = rs_x[0]
    for j in range(1, nx):
        acc = acc + rs_x[j]
    mine_x[...] = acc
    for j in range(ny):
        @pl.when(j != gy)
        def _():
            to_y(j, mine_x, ag_y, gy, y_ag).start()
    ag_y[gy] = acc
    for j in range(ny):
        @pl.when(j != gy)
        def _():
            to_y(j, mine_x, ag_y, gy, y_ag).wait_send()
            to_y(j, mine_x, ag_y, j, y_ag).wait_recv()
    for j in range(ny):
        o_ref[pl.ds(j * part, part)] = ag_y[j]


def gram_sum(local_gram):
    size = local_gram.shape[0]
    nx, ny = lax.axis_size("gx"), lax.axis_size("gy")
    pad = 128
    py, px = pad // ny, pad // nx
    f32 = jnp.float32
    wide = jnp.pad(local_gram, ((0, pad - size), (0, pad - size)))
    vmem = pl.BlockSpec(memory_space=pltpu.VMEM)
    total = pl.pallas_call(
        lambda *refs: reduce_kernel(nx, ny, *refs),
        out_shape=jax.ShapeDtypeStruct((pad, pad), f32),
        in_specs=[vmem],
        out_specs=vmem,
        scratch_shapes=[
            pltpu.VMEM((pad, pad), f32),
            pltpu.VMEM((py, pad), f32),
            pltpu.VMEM((ny, py, pad), f32),
            pltpu.VMEM((ny, py, pad), f32),
            pltpu.VMEM((py, pad), f32),
            pltpu.VMEM((nx, py, pad), f32),
            pltpu.VMEM((nx, py, pad), f32),
            pltpu.SemaphoreType.DMA((ny,)),
            pltpu.SemaphoreType.DMA((ny,)),
            pltpu.SemaphoreType.DMA((ny,)),
            pltpu.SemaphoreType.DMA((nx,)),
            pltpu.SemaphoreType.DMA((nx,)),
            pltpu.SemaphoreType.DMA((nx,)),
        ],
        compiler_params=pltpu.CompilerParams(collective_id=4, has_side_effects=True),
        name="gram_allreduce",
    )(wide)
    return total[:size, :size]


def krylov_kernel(nx, ny, bx, v0_ref, terms_ref, diag_ref, out_ref,
                  halo_x, xsend, ysend, xr, yr, send_sem, recv_sem):
    gx = lax.axis_index("gx")
    gy = lax.axis_index("gy")
    rhs = out_ref.shape[1] // terms_ref.shape[1]
    rows, lanes = terms_ref.shape[1], terms_ref.shape[2]
    cells = out_ref.shape[1]
    zero_x = jnp.zeros(xr.shape[2:], jnp.float32)
    zero_y = jnp.zeros(yr.shape[2:], jnp.float32)
    for k in range(xr.shape[0]):
        for d in range(2):
            xr[k, d] = zero_x
            yr[k, d] = zero_y
    targets = (
        (gx < nx - 1, {"gx": gx + 1, "gy": gy}, gx > 0),
        (gx > 0, {"gx": gx - 1, "gy": gy}, gx < nx - 1),
        (gy < ny - 1, {"gx": gx, "gy": gy + 1}, gy > 0),
        (gy > 0, {"gx": gx, "gy": gy - 1}, gy < ny - 1),
    )
    barrier = pltpu.get_barrier_semaphore()
    for has_target, target, _ in targets:
        @pl.when(has_target)
        def _():
            pl.semaphore_signal(barrier, inc=1, device_id=target, device_id_type=pl.DeviceIdType.MESH)
    peers = (gx + nx - 1) // nx + (2 * nx - 2 - gx) // nx + (gy + ny - 1) // ny + (2 * ny - 2 - gy) // ny
    pl.semaphore_wait(barrier, peers)

    row = lax.broadcasted_iota(jnp.int32, (rhs, rows, lanes), 1)
    lane = lax.broadcasted_iota(jnp.int32, (rhs, rows, lanes), 2)
    xpos = row % bx
    zpos = row // bx
    nzp = rows // bx
    t = [terms_ref[i][None] for i in range(6)]
    diag = diag_ref[...][None]
    trow = lax.broadcasted_iota(jnp.int32, (lanes, cells), 0)

    out_ref[0] = v0_ref[...]
    for k in range(xr.shape[0]):
        flat = out_ref[k]
        xsend[0] = out_ref[k, pl.ds(0, cells // bx, stride=bx), :]
        xsend[1] = out_ref[k, pl.ds(bx - 1, cells // bx, stride=bx), :]
        tr = flat.T
        ysend[...] = jnp.where(trow[:8] == 0, tr[0:1], jnp.where(trow[:8] == 1, tr[lanes - 1:lanes], 0.0))
        plan = (
            (xsend.at[1], xr.at[k, 0]),
            (xsend.at[0], xr.at[k, 1]),
            (ysend, yr.at[k, 0]),
            (ysend, yr.at[k, 1]),
        )

        def copy(d):
            return pltpu.make_async_remote_copy(
                src_ref=plan[d][0], dst_ref=plan[d][1], send_sem=send_sem.at[d],
                recv_sem=recv_sem.at[k, d], device_id=targets[d][1],
                device_id_type=pl.DeviceIdType.MESH,
            )

        for d in range(4):
            @pl.when(targets[d][0])
            def _():
                copy(d).start()
        for d in range(4):
            @pl.when(targets[d][0])
            def _():
                copy(d).wait_send()

            @pl.when(targets[d][2])
            def _():
                copy(d).wait_recv()

        halo_x[pl.ds(0, cells // bx, stride=bx), :] = xr[k, 0]
        halo_x[pl.ds(bx - 1, cells // bx, stride=bx), :] = xr[k, 1]
        before = yr[k, 0][1:2]
        after = yr[k, 1][0:1]
        ycols = jnp.where(trow == 0, before, jnp.where(trow == lanes - 1, after, 0.0)).T
        v = flat.reshape(rhs, rows, lanes)
        hx = halo_x[...].reshape(rhs, rows, lanes)
        hy = ycols.reshape(rhs, rows, lanes)
        zm = jnp.where(zpos == 0, 0.0, pltpu.roll(v, bx, 1))
        zp = jnp.where(zpos == nzp - 1, 0.0, pltpu.roll(v, rows - bx, 1))
        xm = jnp.where(xpos == 0, hx, pltpu.roll(v, 1, 1))
        xp = jnp.where(xpos == bx - 1, hx, pltpu.roll(v, rows - 1, 1))
        ym = jnp.where(lane == 0, hy, pltpu.roll(v, 1, 2))
        yp = jnp.where(lane == lanes - 1, hy, pltpu.roll(v, lanes - 1, 2))
        total = t[0] * zm + t[1] * zp
        total = total + t[2] * xm + t[3] * xp
        total = total + t[4] * ym + t[5] * yp
        out_ref[k + 1] = (-total / diag).reshape(cells, lanes)


def krylov_basis(v0, terms, diagonal):
    rhs, nz, bx, by = v0.shape
    nx, ny = lax.axis_size("gx"), lax.axis_size("gy")
    cells = rhs * nz * bx
    vmem = pl.BlockSpec(memory_space=pltpu.VMEM)
    out = pl.pallas_call(
        lambda *refs: krylov_kernel(nx, ny, bx, *refs),
        out_shape=jax.ShapeDtypeStruct((S + 1, cells, by), jnp.float32),
        in_specs=[vmem] * 3,
        out_specs=vmem,
        scratch_shapes=[
            pltpu.VMEM((cells, by), jnp.float32),
            pltpu.VMEM((2, cells // bx, by), jnp.float32),
            pltpu.VMEM((8, cells), jnp.float32),
            pltpu.VMEM((S, 2, cells // bx, by), jnp.float32),
            pltpu.VMEM((S, 2, 8, cells), jnp.float32),
            pltpu.SemaphoreType.DMA((4,)),
            pltpu.SemaphoreType.DMA((S, 4)),
        ],
        compiler_params=pltpu.CompilerParams(collective_id=3, has_side_effects=True),
        name="krylov_basis",
    )(v0.reshape(cells, by), jnp.stack(terms).reshape(6, nz * bx, by), diagonal.reshape(nz * bx, by))
    return out.reshape(S + 1, rhs, nz, bx, by)


def face_terms(padded, storage):
    core = padded[1:-1, 1:-1, 1:-1]
    terms = (
        (core + padded[:-2, 1:-1, 1:-1]) * 0.5,
        (core + padded[2:, 1:-1, 1:-1]) * 0.5,
        (core + padded[1:-1, :-2, 1:-1]) * 0.5,
        (core + padded[1:-1, 2:, 1:-1]) * 0.5,
        (core + padded[1:-1, 1:-1, :-2]) * 0.5,
        (core + padded[1:-1, 1:-1, 2:]) * 0.5,
    )
    diagonal = storage + terms[0] + terms[1] + terms[2] + terms[3] + terms[4] + terms[5]
    return (terms, diagonal)


def _device(axis, index, other_axis, other_index):
    return {axis: index, other_axis: other_index}


def small_solve(gram_all):
    shift_matrix = jnp.eye(BASIS, BASIS - RHS, dtype=jnp.float32) + jnp.eye(
        BASIS, BASIS - RHS, k=-RHS, dtype=jnp.float32
    )
    first_block = jnp.eye(BASIS, RHS, dtype=jnp.float32)
    hp = lax.Precision.HIGHEST
    gram_shift = jnp.dot(gram_all, shift_matrix, precision=hp)
    normal = jnp.dot(shift_matrix.T, gram_shift, precision=hp)
    right_side = jnp.dot(gram_shift.T, first_block, precision=hp)
    lower = jnp.linalg.cholesky(normal)
    y = jax.scipy.linalg.cho_solve((lower, True), right_side)
    coeffs = first_block - jnp.dot(shift_matrix, y, precision=hp)
    return (y, coeffs)


def shards(pumping, conductivity, capacity):
    hp = lax.Precision.HIGHEST
    shape = pumping.shape
    cond_halo = padded_2(conductivity, (("gx", 1), ("gy", 2)), 1)
    cond_pad = jnp.pad(cond_halo, ((1, 1), (0, 0), (0, 0)))
    terms, diagonal = face_terms(cond_pad, capacity)
    solution = jnp.zeros(shape, jnp.float32)
    residual = pumping / diagonal
    for restart in range(CYCLES):
        stacked = krylov_basis(residual, terms, diagonal).reshape(BASIS, -1)
        local_gram = jnp.dot(stacked, stacked.T, precision=hp)
        gram_all = gram_sum(local_gram)
        y, coeffs = small_solve(gram_all)
        y_full = jnp.concatenate([y, jnp.zeros((RHS, RHS), jnp.float32)], axis=0)
        both = jnp.dot(jnp.concatenate([y_full, coeffs], axis=1).T, stacked, precision=hp)
        solution = solution + both[:RHS].reshape(shape)
        residual = both[RHS:].reshape(shape)
    return (solution, residual)


def solution(mesh):
    return jax.shard_map(
        shards,
        mesh=mesh,
        in_specs=(P(None, None, "gx", "gy"), P(None, "gx", "gy"), P(None, "gx", "gy")),
        out_specs=(P(None, None, "gx", "gy"), P(None, None, "gx", "gy")),
        check_vma=False,
    )
```

```python
import jax
import jax.numpy as jnp
from jax import lax
from jax.sharding import PartitionSpec as P
from jax.experimental import pallas as pl
from jax.experimental.pallas import tpu as pltpu

RHS = 16
S = 4
CYCLES = 5
BASIS = 80


def padded_2(array, sides, width):
    for axis, dim in sides:
        devices, length = (lax.axis_size(axis), array.shape[dim])
        up = [(i, (i + 1) % devices) for i in range(devices - 1)]
        down = [(j, i) for i, j in up]
        last = lax.slice_in_dim(array, length - width, length, axis=dim)
        leading = lax.slice_in_dim(array, 0, width, axis=dim)
        before = lax.ppermute(last, axis, up)
        after = lax.ppermute(leading, axis, down)
        array = jnp.concatenate([before, array, after], axis=dim)
    return array


def exchange_reduce(axis, other_axis, n, src, mine, rs, ag, full, send_sem, rs_sem, ag_sem):
    me = lax.axis_index(axis)
    other = lax.axis_index(other_axis)
    part = src.shape[0] // n

    def scatter(j, slot):
        return pltpu.make_async_remote_copy(
            src_ref=src.at[pl.ds(j * part, part)], dst_ref=rs.at[slot], send_sem=send_sem.at[j],
            recv_sem=rs_sem.at[slot], device_id=_device(axis, j, other_axis, other),
            device_id_type=pl.DeviceIdType.MESH,
        )

    def gather(j, slot):
        return pltpu.make_async_remote_copy(
            src_ref=mine, dst_ref=ag.at[slot], send_sem=send_sem.at[j],
            recv_sem=ag_sem.at[slot], device_id=_device(axis, j, other_axis, other),
            device_id_type=pl.DeviceIdType.MESH,
        )

    for j in range(n):
        @pl.when(j != me)
        def _():
            scatter(j, me).start()
    rs[me] = src[pl.ds(pl.multiple_of(me * part, part), part)]
    for j in range(n):
        @pl.when(j != me)
        def _():
            scatter(j, me).wait_send()
            scatter(j, j).wait_recv()
    acc = rs[0]
    for j in range(1, n):
        acc = acc + rs[j]
    mine[...] = acc
    for j in range(n):
        @pl.when(j != me)
        def _():
            gather(j, me).start()
    ag[me] = acc
    for j in range(n):
        @pl.when(j != me)
        def _():
            gather(j, me).wait_send()
            gather(j, j).wait_recv()
    for j in range(n):
        full[pl.ds(j * part, part)] = ag[j]


def reduce_kernel(nx, ny, x_ref, o_ref, gy_full, mine_y, rs_y, ag_y, mine_x, rs_x, ag_x,
                  y_send, y_rs, y_ag, x_send, x_rs, x_ag):
    gx = lax.axis_index("gx")
    gy = lax.axis_index("gy")
    part = x_ref.shape[0] // ny

    def to_y(j, src, dst, slot, sem):
        return pltpu.make_async_remote_copy(
            src_ref=src, dst_ref=dst.at[slot], send_sem=y_send.at[j], recv_sem=sem.at[slot],
            device_id={"gx": gx, "gy": j}, device_id_type=pl.DeviceIdType.MESH,
        )

    def to_x(j, slot):
        return pltpu.make_async_remote_copy(
            src_ref=mine_y, dst_ref=rs_x.at[slot], send_sem=x_send.at[j], recv_sem=x_rs.at[slot],
            device_id={"gx": j, "gy": gy}, device_id_type=pl.DeviceIdType.MESH,
        )

    for j in range(ny):
        @pl.when(j != gy)
        def _():
            to_y(j, x_ref.at[pl.ds(j * part, part)], rs_y, gy, y_rs).start()
    rs_y[gy] = x_ref[pl.ds(pl.multiple_of(gy * part, part), part)]
    for j in range(ny):
        @pl.when(j != gy)
        def _():
            to_y(j, x_ref.at[pl.ds(j * part, part)], rs_y, gy, y_rs).wait_send()
            to_y(j, x_ref.at[pl.ds(j * part, part)], rs_y, j, y_rs).wait_recv()
    acc = rs_y[0]
    for j in range(1, ny):
        acc = acc + rs_y[j]
    mine_y[...] = acc
    for j in range(nx):
        @pl.when(j != gx)
        def _():
            to_x(j, gx).start()
    rs_x[gx] = acc
    for j in range(nx):
        @pl.when(j != gx)
        def _():
            to_x(j, gx).wait_send()
            to_x(j, j).wait_recv()
    acc = rs_x[0]
    for j in range(1, nx):
        acc = acc + rs_x[j]
    mine_x[...] = acc
    for j in range(ny):
        @pl.when(j != gy)
        def _():
            to_y(j, mine_x, ag_y, gy, y_ag).start()
    ag_y[gy] = acc
    for j in range(ny):
        @pl.when(j != gy)
        def _():
            to_y(j, mine_x, ag_y, gy, y_ag).wait_send()
            to_y(j, mine_x, ag_y, j, y_ag).wait_recv()
    for j in range(ny):
        o_ref[pl.ds(j * part, part)] = ag_y[j]


def gram_sum(local_gram):
    size = local_gram.shape[0]
    nx, ny = lax.axis_size("gx"), lax.axis_size("gy")
    pad = 128
    py, px = pad // ny, pad // nx
    f32 = jnp.float32
    wide = jnp.pad(local_gram, ((0, pad - size), (0, pad - size)))
    vmem = pl.BlockSpec(memory_space=pltpu.VMEM)
    total = pl.pallas_call(
        lambda *refs: reduce_kernel(nx, ny, *refs),
        out_shape=jax.ShapeDtypeStruct((pad, pad), f32),
        in_specs=[vmem],
        out_specs=vmem,
        scratch_shapes=[
            pltpu.VMEM((pad, pad), f32),
            pltpu.VMEM((py, pad), f32),
            pltpu.VMEM((ny, py, pad), f32),
            pltpu.VMEM((ny, py, pad), f32),
            pltpu.VMEM((py, pad), f32),
            pltpu.VMEM((nx, py, pad), f32),
            pltpu.VMEM((nx, py, pad), f32),
            pltpu.SemaphoreType.DMA((ny,)),
            pltpu.SemaphoreType.DMA((ny,)),
            pltpu.SemaphoreType.DMA((ny,)),
            pltpu.SemaphoreType.DMA((nx,)),
            pltpu.SemaphoreType.DMA((nx,)),
            pltpu.SemaphoreType.DMA((nx,)),
        ],
        compiler_params=pltpu.CompilerParams(has_side_effects=True),
        name="gram_allreduce",
    )(wide)
    return total[:size, :size]


def krylov_kernel(nx, ny, bx, v0_ref, terms_ref, diag_ref, out_ref,
                  halo_x, xsend, ysend, xr, yr, send_sem, recv_sem, ybuf):
    gx = lax.axis_index("gx")
    gy = lax.axis_index("gy")
    rhs = out_ref.shape[1] // terms_ref.shape[1]
    rows, lanes = terms_ref.shape[1], terms_ref.shape[2]
    cells = out_ref.shape[1]
    zero_x = jnp.zeros(xr.shape[2:], jnp.float32)
    zero_row = jnp.zeros((1, yr.shape[3]), jnp.float32)
    targets = (
        (gx < nx - 1, {"gx": gx + 1, "gy": gy}, gx > 0),
        (gx > 0, {"gx": gx - 1, "gy": gy}, gx < nx - 1),
        (gy < ny - 1, {"gx": gx, "gy": gy + 1}, gy > 0),
        (gy > 0, {"gx": gx, "gy": gy - 1}, gy < ny - 1),
    )

    row = lax.broadcasted_iota(jnp.int32, (rhs, rows, lanes), 1)
    lane = lax.broadcasted_iota(jnp.int32, (rhs, rows, lanes), 2)
    xpos = row % bx
    zpos = row // bx
    nzp = rows // bx
    t = [terms_ref[i][None] for i in range(6)]
    diag = diag_ref[...][None]
    trow = lax.broadcasted_iota(jnp.int32, (lanes, cells), 0)

    out_ref[0] = v0_ref[...]
    for k in range(xr.shape[0]):
        flat = out_ref[k]
        xsend[0] = out_ref[k, pl.ds(0, cells // bx, stride=bx), :]
        xsend[1] = out_ref[k, pl.ds(bx - 1, cells // bx, stride=bx), :]
        tr = flat.T
        ysend[...] = jnp.where(trow[:8] == 0, tr[0:1], jnp.where(trow[:8] == 1, tr[lanes - 1:lanes], 0.0))
        plan = (
            (xsend.at[1], xr.at[k, 0]),
            (xsend.at[0], xr.at[k, 1]),
            (ysend, yr.at[k, 0]),
            (ysend, yr.at[k, 1]),
        )

        def copy(d):
            return pltpu.make_async_remote_copy(
                src_ref=plan[d][0], dst_ref=plan[d][1], send_sem=send_sem.at[d],
                recv_sem=recv_sem.at[k, d], device_id=targets[d][1],
                device_id_type=pl.DeviceIdType.MESH,
            )

        for d in range(4):
            @pl.when(targets[d][0])
            def _():
                copy(d).start()
        for d in range(4):
            @pl.when(targets[d][0])
            def _():
                copy(d).wait_send()

            @pl.when(targets[d][2])
            def _():
                copy(d).wait_recv()

        for side, start in ((0, 0), (1, bx - 1)):
            has_x = targets[side][2]
            has_y = targets[2 + side][2]

            @pl.when(has_x)
            def _():
                halo_x[pl.ds(start, cells // bx, stride=bx), :] = xr[k, side]

            @pl.when(jnp.logical_not(has_x))
            def _():
                halo_x[pl.ds(start, cells // bx, stride=bx), :] = zero_x

            @pl.when(has_y)
            def _():
                ybuf[side:side + 1] = yr[k, side][1 - side:2 - side]

            @pl.when(jnp.logical_not(has_y))
            def _():
                ybuf[side:side + 1] = zero_row

        before = ybuf[0:1]
        after = ybuf[1:2]
        ycols = jnp.where(trow == 0, before, jnp.where(trow == lanes - 1, after, 0.0)).T
        v = flat.reshape(rhs, rows, lanes)
        hx = halo_x[...].reshape(rhs, rows, lanes)
        hy = ycols.reshape(rhs, rows, lanes)
        zm = jnp.where(zpos == 0, 0.0, pltpu.roll(v, bx, 1))
        zp = jnp.where(zpos == nzp - 1, 0.0, pltpu.roll(v, rows - bx, 1))
        xm = jnp.where(xpos == 0, hx, pltpu.roll(v, 1, 1))
        xp = jnp.where(xpos == bx - 1, hx, pltpu.roll(v, rows - 1, 1))
        ym = jnp.where(lane == 0, hy, pltpu.roll(v, 1, 2))
        yp = jnp.where(lane == lanes - 1, hy, pltpu.roll(v, lanes - 1, 2))
        total = t[0] * zm + t[1] * zp
        total = total + t[2] * xm + t[3] * xp
        total = total + t[4] * ym + t[5] * yp
        out_ref[k + 1] = (-total / diag).reshape(cells, lanes)


def krylov_basis(v0, terms, diagonal):
    rhs, nz, bx, by = v0.shape
    nx, ny = lax.axis_size("gx"), lax.axis_size("gy")
    cells = rhs * nz * bx
    vmem = pl.BlockSpec(memory_space=pltpu.VMEM)
    out = pl.pallas_call(
        lambda *refs: krylov_kernel(nx, ny, bx, *refs),
        out_shape=jax.ShapeDtypeStruct((S + 1, cells, by), jnp.float32),
        in_specs=[vmem] * 3,
        out_specs=vmem,
        scratch_shapes=[
            pltpu.VMEM((cells, by), jnp.float32),
            pltpu.VMEM((2, cells // bx, by), jnp.float32),
            pltpu.VMEM((8, cells), jnp.float32),
            pltpu.VMEM((S, 2, cells // bx, by), jnp.float32),
            pltpu.VMEM((S, 2, 8, cells), jnp.float32),
            pltpu.SemaphoreType.DMA((4,)),
            pltpu.SemaphoreType.DMA((S, 4)),
            pltpu.VMEM((8, cells), jnp.float32),
        ],
        compiler_params=pltpu.CompilerParams(has_side_effects=True),
        name="krylov_basis",
    )(v0.reshape(cells, by), jnp.stack(terms).reshape(6, nz * bx, by), diagonal.reshape(nz * bx, by))
    return out.reshape(S + 1, rhs, nz, bx, by)


def face_terms(padded, storage):
    core = padded[1:-1, 1:-1, 1:-1]
    terms = (
        (core + padded[:-2, 1:-1, 1:-1]) * 0.5,
        (core + padded[2:, 1:-1, 1:-1]) * 0.5,
        (core + padded[1:-1, :-2, 1:-1]) * 0.5,
        (core + padded[1:-1, 2:, 1:-1]) * 0.5,
        (core + padded[1:-1, 1:-1, :-2]) * 0.5,
        (core + padded[1:-1, 1:-1, 2:]) * 0.5,
    )
    diagonal = storage + terms[0] + terms[1] + terms[2] + terms[3] + terms[4] + terms[5]
    return (terms, diagonal)


def _device(axis, index, other_axis, other_index):
    return {axis: index, other_axis: other_index}


def small_solve(gram_all):
    shift_matrix = jnp.eye(BASIS, BASIS - RHS, dtype=jnp.float32) + jnp.eye(
        BASIS, BASIS - RHS, k=-RHS, dtype=jnp.float32
    )
    first_block = jnp.eye(BASIS, RHS, dtype=jnp.float32)
    hp = lax.Precision.HIGHEST
    gram_shift = jnp.dot(gram_all, shift_matrix, precision=hp)
    normal = jnp.dot(shift_matrix.T, gram_shift, precision=hp)
    right_side = jnp.dot(gram_shift.T, first_block, precision=hp)
    lower = jnp.linalg.cholesky(normal)
    y = jax.scipy.linalg.cho_solve((lower, True), right_side)
    coeffs = first_block - jnp.dot(shift_matrix, y, precision=hp)
    return (y, coeffs)


def shards(pumping, conductivity, capacity):
    hp = lax.Precision.HIGHEST
    shape = pumping.shape
    cond_halo = padded_2(conductivity, (("gx", 1), ("gy", 2)), 1)
    cond_pad = jnp.pad(cond_halo, ((1, 1), (0, 0), (0, 0)))
    terms, diagonal = face_terms(cond_pad, capacity)
    solution = jnp.zeros(shape, jnp.float32)
    residual = pumping / diagonal
    for restart in range(CYCLES):
        stacked = krylov_basis(residual, terms, diagonal).reshape(BASIS, -1)
        local_gram = jnp.dot(stacked, stacked.T, precision=hp)
        gram_all = gram_sum(local_gram)
        y, coeffs = small_solve(gram_all)
        y_full = jnp.concatenate([y, jnp.zeros((RHS, RHS), jnp.float32)], axis=0)
        both = jnp.dot(jnp.concatenate([y_full, coeffs], axis=1).T, stacked, precision=hp)
        solution = solution + both[:RHS].reshape(shape)
        residual = both[RHS:].reshape(shape)
    return (solution, residual)


def solution(mesh):
    return jax.shard_map(
        shards,
        mesh=mesh,
        in_specs=(P(None, None, "gx", "gy"), P(None, "gx", "gy"), P(None, "gx", "gy")),
        out_specs=(P(None, None, "gx", "gy"), P(None, None, "gx", "gy")),
        check_vma=False,
    )
```

```python
import jax
import jax.numpy as jnp
from jax import lax
from jax.sharding import PartitionSpec as P
from jax.experimental import pallas as pl
from jax.experimental.pallas import tpu as pltpu

RHS = 16
S = 4
CYCLES = 5
BASIS = 80


def padded_2(array, sides, width):
    for axis, dim in sides:
        devices, length = (lax.axis_size(axis), array.shape[dim])
        up = [(i, (i + 1) % devices) for i in range(devices - 1)]
        down = [(j, i) for i, j in up]
        last = lax.slice_in_dim(array, length - width, length, axis=dim)
        leading = lax.slice_in_dim(array, 0, width, axis=dim)
        before = lax.ppermute(last, axis, up)
        after = lax.ppermute(leading, axis, down)
        array = jnp.concatenate([before, array, after], axis=dim)
    return array


def exchange_reduce(axis, other_axis, n, src, mine, rs, ag, full, send_sem, rs_sem, ag_sem):
    me = lax.axis_index(axis)
    other = lax.axis_index(other_axis)
    part = src.shape[0] // n

    def scatter(j, slot):
        return pltpu.make_async_remote_copy(
            src_ref=src.at[pl.ds(j * part, part)], dst_ref=rs.at[slot], send_sem=send_sem.at[j],
            recv_sem=rs_sem.at[slot], device_id=_device(axis, j, other_axis, other),
            device_id_type=pl.DeviceIdType.MESH,
        )

    def gather(j, slot):
        return pltpu.make_async_remote_copy(
            src_ref=mine, dst_ref=ag.at[slot], send_sem=send_sem.at[j],
            recv_sem=ag_sem.at[slot], device_id=_device(axis, j, other_axis, other),
            device_id_type=pl.DeviceIdType.MESH,
        )

    for j in range(n):
        @pl.when(j != me)
        def _():
            scatter(j, me).start()
    rs[me] = src[pl.ds(pl.multiple_of(me * part, part), part)]
    for j in range(n):
        @pl.when(j != me)
        def _():
            scatter(j, me).wait_send()
            scatter(j, j).wait_recv()
    acc = rs[0]
    for j in range(1, n):
        acc = acc + rs[j]
    mine[...] = acc
    for j in range(n):
        @pl.when(j != me)
        def _():
            gather(j, me).start()
    ag[me] = acc
    for j in range(n):
        @pl.when(j != me)
        def _():
            gather(j, me).wait_send()
            gather(j, j).wait_recv()
    for j in range(n):
        full[pl.ds(j * part, part)] = ag[j]


def reduce_kernel(nx, ny, x_ref, o_ref, gy_full, mine_y, rs_y, ag_y, mine_x, rs_x, ag_x,
                  y_send, y_rs, y_ag, x_send, x_rs, x_ag):
    gx = lax.axis_index("gx")
    gy = lax.axis_index("gy")
    barrier = pltpu.get_barrier_semaphore()
    for j in range(nx):
        @pl.when(j != gx)
        def _():
            pl.semaphore_signal(barrier, inc=1, device_id={"gx": j, "gy": gy},
                                device_id_type=pl.DeviceIdType.MESH)
    for j in range(ny):
        @pl.when(j != gy)
        def _():
            pl.semaphore_signal(barrier, inc=1, device_id={"gx": gx, "gy": j},
                                device_id_type=pl.DeviceIdType.MESH)
    pl.semaphore_wait(barrier, nx + ny - 2)
    part = x_ref.shape[0] // ny

    def to_y(j, src, dst, slot, sem):
        return pltpu.make_async_remote_copy(
            src_ref=src, dst_ref=dst.at[slot], send_sem=y_send.at[j], recv_sem=sem.at[slot],
            device_id={"gx": gx, "gy": j}, device_id_type=pl.DeviceIdType.MESH,
        )

    def to_x(j, slot):
        return pltpu.make_async_remote_copy(
            src_ref=mine_y, dst_ref=rs_x.at[slot], send_sem=x_send.at[j], recv_sem=x_rs.at[slot],
            device_id={"gx": j, "gy": gy}, device_id_type=pl.DeviceIdType.MESH,
        )

    for j in range(ny):
        @pl.when(j != gy)
        def _():
            to_y(j, x_ref.at[pl.ds(j * part, part)], rs_y, gy, y_rs).start()
    rs_y[gy] = x_ref[pl.ds(pl.multiple_of(gy * part, part), part)]
    for j in range(ny):
        @pl.when(j != gy)
        def _():
            to_y(j, x_ref.at[pl.ds(j * part, part)], rs_y, gy, y_rs).wait_send()
            to_y(j, x_ref.at[pl.ds(j * part, part)], rs_y, j, y_rs).wait_recv()
    acc = rs_y[0]
    for j in range(1, ny):
        acc = acc + rs_y[j]
    mine_y[...] = acc
    for j in range(nx):
        @pl.when(j != gx)
        def _():
            to_x(j, gx).start()
    rs_x[gx] = acc
    for j in range(nx):
        @pl.when(j != gx)
        def _():
            to_x(j, gx).wait_send()
            to_x(j, j).wait_recv()
    acc = rs_x[0]
    for j in range(1, nx):
        acc = acc + rs_x[j]
    mine_x[...] = acc
    for j in range(ny):
        @pl.when(j != gy)
        def _():
            to_y(j, mine_x, ag_y, gy, y_ag).start()
    ag_y[gy] = acc
    for j in range(ny):
        @pl.when(j != gy)
        def _():
            to_y(j, mine_x, ag_y, gy, y_ag).wait_send()
            to_y(j, mine_x, ag_y, j, y_ag).wait_recv()
    for j in range(ny):
        o_ref[pl.ds(j * part, part)] = ag_y[j]


def gram_sum(local_gram):
    size = local_gram.shape[0]
    nx, ny = lax.axis_size("gx"), lax.axis_size("gy")
    pad = 128
    py, px = pad // ny, pad // nx
    f32 = jnp.float32
    wide = jnp.pad(local_gram, ((0, pad - size), (0, pad - size)))
    vmem = pl.BlockSpec(memory_space=pltpu.VMEM)
    total = pl.pallas_call(
        lambda *refs: reduce_kernel(nx, ny, *refs),
        out_shape=jax.ShapeDtypeStruct((pad, pad), f32),
        in_specs=[vmem],
        out_specs=vmem,
        scratch_shapes=[
            pltpu.VMEM((pad, pad), f32),
            pltpu.VMEM((py, pad), f32),
            pltpu.VMEM((ny, py, pad), f32),
            pltpu.VMEM((ny, py, pad), f32),
            pltpu.VMEM((py, pad), f32),
            pltpu.VMEM((nx, py, pad), f32),
            pltpu.VMEM((nx, py, pad), f32),
            pltpu.SemaphoreType.DMA((ny,)),
            pltpu.SemaphoreType.DMA((ny,)),
            pltpu.SemaphoreType.DMA((ny,)),
            pltpu.SemaphoreType.DMA((nx,)),
            pltpu.SemaphoreType.DMA((nx,)),
            pltpu.SemaphoreType.DMA((nx,)),
        ],
        compiler_params=pltpu.CompilerParams(collective_id=4, has_side_effects=True),
        name="gram_allreduce",
    )(wide)
    return total[:size, :size]


def krylov_kernel(nx, ny, bx, v0_ref, terms_ref, diag_ref, out_ref,
                  halo_x, xsend, ysend, xr, yr, send_sem, recv_sem):
    gx = lax.axis_index("gx")
    gy = lax.axis_index("gy")
    rhs = out_ref.shape[1] // terms_ref.shape[1]
    rows, lanes = terms_ref.shape[1], terms_ref.shape[2]
    cells = out_ref.shape[1]
    zero_x = jnp.zeros(xr.shape[2:], jnp.float32)
    zero_y = jnp.zeros(yr.shape[2:], jnp.float32)
    for k in range(xr.shape[0]):
        for d in range(2):
            xr[k, d] = zero_x
            yr[k, d] = zero_y
    targets = (
        (gx < nx - 1, {"gx": gx + 1, "gy": gy}, gx > 0),
        (gx > 0, {"gx": gx - 1, "gy": gy}, gx < nx - 1),
        (gy < ny - 1, {"gx": gx, "gy": gy + 1}, gy > 0),
        (gy > 0, {"gx": gx, "gy": gy - 1}, gy < ny - 1),
    )
    barrier = pltpu.get_barrier_semaphore()
    for has_target, target, _ in targets:
        @pl.when(has_target)
        def _():
            pl.semaphore_signal(barrier, inc=1, device_id=target, device_id_type=pl.DeviceIdType.MESH)
    peers = (gx + nx - 1) // nx + (2 * nx - 2 - gx) // nx + (gy + ny - 1) // ny + (2 * ny - 2 - gy) // ny
    pl.semaphore_wait(barrier, peers)

    row = lax.broadcasted_iota(jnp.int32, (rhs, rows, lanes), 1)
    lane = lax.broadcasted_iota(jnp.int32, (rhs, rows, lanes), 2)
    xpos = row % bx
    zpos = row // bx
    nzp = rows // bx
    t = [terms_ref[i][None] for i in range(6)]
    diag = diag_ref[...][None]
    trow = lax.broadcasted_iota(jnp.int32, (lanes, cells), 0)

    out_ref[0] = v0_ref[...]
    for k in range(xr.shape[0]):
        flat = out_ref[k]
        xsend[0] = out_ref[k, pl.ds(0, cells // bx, stride=bx), :]
        xsend[1] = out_ref[k, pl.ds(bx - 1, cells // bx, stride=bx), :]
        tr = flat.T
        ysend[...] = jnp.where(trow[:8] == 0, tr[0:1], jnp.where(trow[:8] == 1, tr[lanes - 1:lanes], 0.0))
        plan = (
            (xsend.at[1], xr.at[k, 0]),
            (xsend.at[0], xr.at[k, 1]),
            (ysend, yr.at[k, 0]),
            (ysend, yr.at[k, 1]),
        )

        def copy(d):
            return pltpu.make_async_remote_copy(
                src_ref=plan[d][0], dst_ref=plan[d][1], send_sem=send_sem.at[d],
                recv_sem=recv_sem.at[k, d], device_id=targets[d][1],
                device_id_type=pl.DeviceIdType.MESH,
            )

        for d in range(4):
            @pl.when(targets[d][0])
            def _():
                copy(d).start()
        for d in range(4):
            @pl.when(targets[d][0])
            def _():
                copy(d).wait_send()

            @pl.when(targets[d][2])
            def _():
                copy(d).wait_recv()

        halo_x[pl.ds(0, cells // bx, stride=bx), :] = xr[k, 0]
        halo_x[pl.ds(bx - 1, cells // bx, stride=bx), :] = xr[k, 1]
        before = yr[k, 0][1:2]
        after = yr[k, 1][0:1]
        ycols = jnp.where(trow == 0, before, jnp.where(trow == lanes - 1, after, 0.0)).T
        v = flat.reshape(rhs, rows, lanes)
        hx = halo_x[...].reshape(rhs, rows, lanes)
        hy = ycols.reshape(rhs, rows, lanes)
        zm = jnp.where(zpos == 0, 0.0, pltpu.roll(v, bx, 1))
        zp = jnp.where(zpos == nzp - 1, 0.0, pltpu.roll(v, rows - bx, 1))
        xm = jnp.where(xpos == 0, hx, pltpu.roll(v, 1, 1))
        xp = jnp.where(xpos == bx - 1, hx, pltpu.roll(v, rows - 1, 1))
        ym = jnp.where(lane == 0, hy, pltpu.roll(v, 1, 2))
        yp = jnp.where(lane == lanes - 1, hy, pltpu.roll(v, lanes - 1, 2))
        total = t[0] * zm + t[1] * zp
        total = total + t[2] * xm + t[3] * xp
        total = total + t[4] * ym + t[5] * yp
        out_ref[k + 1] = (-total / diag).reshape(cells, lanes)


def krylov_basis(v0, terms, diagonal):
    rhs, nz, bx, by = v0.shape
    nx, ny = lax.axis_size("gx"), lax.axis_size("gy")
    cells = rhs * nz * bx
    vmem = pl.BlockSpec(memory_space=pltpu.VMEM)
    out = pl.pallas_call(
        lambda *refs: krylov_kernel(nx, ny, bx, *refs),
        out_shape=jax.ShapeDtypeStruct((S + 1, cells, by), jnp.float32),
        in_specs=[vmem] * 3,
        out_specs=vmem,
        scratch_shapes=[
            pltpu.VMEM((cells, by), jnp.float32),
            pltpu.VMEM((2, cells // bx, by), jnp.float32),
            pltpu.VMEM((8, cells), jnp.float32),
            pltpu.VMEM((S, 2, cells // bx, by), jnp.float32),
            pltpu.VMEM((S, 2, 8, cells), jnp.float32),
            pltpu.SemaphoreType.DMA((4,)),
            pltpu.SemaphoreType.DMA((S, 4)),
        ],
        compiler_params=pltpu.CompilerParams(collective_id=3, has_side_effects=True),
        name="krylov_basis",
    )(v0.reshape(cells, by), jnp.stack(terms).reshape(6, nz * bx, by), diagonal.reshape(nz * bx, by))
    return out.reshape(S + 1, rhs, nz, bx, by)


def face_terms(padded, storage):
    core = padded[1:-1, 1:-1, 1:-1]
    terms = (
        (core + padded[:-2, 1:-1, 1:-1]) * 0.5,
        (core + padded[2:, 1:-1, 1:-1]) * 0.5,
        (core + padded[1:-1, :-2, 1:-1]) * 0.5,
        (core + padded[1:-1, 2:, 1:-1]) * 0.5,
        (core + padded[1:-1, 1:-1, :-2]) * 0.5,
        (core + padded[1:-1, 1:-1, 2:]) * 0.5,
    )
    diagonal = storage + terms[0] + terms[1] + terms[2] + terms[3] + terms[4] + terms[5]
    return (terms, diagonal)


def _device(axis, index, other_axis, other_index):
    return {axis: index, other_axis: other_index}


def small_solve(gram_all):
    shift_matrix = jnp.eye(BASIS, BASIS - RHS, dtype=jnp.float32) + jnp.eye(
        BASIS, BASIS - RHS, k=-RHS, dtype=jnp.float32
    )
    first_block = jnp.eye(BASIS, RHS, dtype=jnp.float32)
    hp = lax.Precision.HIGHEST
    gram_shift = jnp.dot(gram_all, shift_matrix, precision=hp)
    normal = jnp.dot(shift_matrix.T, gram_shift, precision=hp)
    right_side = jnp.dot(gram_shift.T, first_block, precision=hp)
    lower = lax.linalg.cholesky(normal, symmetrize_input=False)
    forward = lax.linalg.triangular_solve(lower, right_side, left_side=True, lower=True)
    y = lax.linalg.triangular_solve(lower, forward, left_side=True, lower=True, transpose_a=True)
    coeffs = first_block - jnp.dot(shift_matrix, y, precision=hp)
    return (y, coeffs)


def shards(pumping, conductivity, capacity):
    hp = lax.Precision.HIGHEST
    shape = pumping.shape
    cond_halo = padded_2(conductivity, (("gx", 1), ("gy", 2)), 1)
    cond_pad = jnp.pad(cond_halo, ((1, 1), (0, 0), (0, 0)))
    terms, diagonal = face_terms(cond_pad, capacity)
    solution = jnp.zeros(shape, jnp.float32)
    residual = pumping / diagonal
    for restart in range(CYCLES):
        stacked = krylov_basis(residual, terms, diagonal).reshape(BASIS, -1)
        local_gram = jnp.dot(stacked, stacked.T, precision=hp)
        gram_all = gram_sum(local_gram)
        y, coeffs = small_solve(gram_all)
        y_full = jnp.concatenate([y, jnp.zeros((RHS, RHS), jnp.float32)], axis=0)
        both = jnp.dot(jnp.concatenate([y_full, coeffs], axis=1).T, stacked, precision=hp)
        solution = solution + both[:RHS].reshape(shape)
        residual = both[RHS:].reshape(shape)
    return (solution, residual)


def solution(mesh):
    return jax.shard_map(
        shards,
        mesh=mesh,
        in_specs=(P(None, None, "gx", "gy"), P(None, "gx", "gy"), P(None, "gx", "gy")),
        out_specs=(P(None, None, "gx", "gy"), P(None, None, "gx", "gy")),
        check_vma=False,
    )
```

```python
import jax
import jax.numpy as jnp
from jax import lax
from jax.sharding import PartitionSpec as P
from jax.experimental import pallas as pl
from jax.experimental.pallas import tpu as pltpu

RHS = 16
S = 4
CYCLES = 5
BASIS = 80


def padded_2(array, sides, width):
    for axis, dim in sides:
        devices, length = (lax.axis_size(axis), array.shape[dim])
        up = [(i, (i + 1) % devices) for i in range(devices - 1)]
        down = [(j, i) for i, j in up]
        last = lax.slice_in_dim(array, length - width, length, axis=dim)
        leading = lax.slice_in_dim(array, 0, width, axis=dim)
        before = lax.ppermute(last, axis, up)
        after = lax.ppermute(leading, axis, down)
        array = jnp.concatenate([before, array, after], axis=dim)
    return array


def exchange_reduce(axis, other_axis, n, src, mine, rs, ag, full, send_sem, rs_sem, ag_sem):
    me = lax.axis_index(axis)
    other = lax.axis_index(other_axis)
    part = src.shape[0] // n

    def scatter(j, slot):
        return pltpu.make_async_remote_copy(
            src_ref=src.at[pl.ds(j * part, part)], dst_ref=rs.at[slot], send_sem=send_sem.at[j],
            recv_sem=rs_sem.at[slot], device_id=_device(axis, j, other_axis, other),
            device_id_type=pl.DeviceIdType.MESH,
        )

    def gather(j, slot):
        return pltpu.make_async_remote_copy(
            src_ref=mine, dst_ref=ag.at[slot], send_sem=send_sem.at[j],
            recv_sem=ag_sem.at[slot], device_id=_device(axis, j, other_axis, other),
            device_id_type=pl.DeviceIdType.MESH,
        )

    for j in range(n):
        @pl.when(j != me)
        def _():
            scatter(j, me).start()
    rs[me] = src[pl.ds(pl.multiple_of(me * part, part), part)]
    for j in range(n):
        @pl.when(j != me)
        def _():
            scatter(j, me).wait_send()
            scatter(j, j).wait_recv()
    acc = rs[0]
    for j in range(1, n):
        acc = acc + rs[j]
    mine[...] = acc
    for j in range(n):
        @pl.when(j != me)
        def _():
            gather(j, me).start()
    ag[me] = acc
    for j in range(n):
        @pl.when(j != me)
        def _():
            gather(j, me).wait_send()
            gather(j, j).wait_recv()
    for j in range(n):
        full[pl.ds(j * part, part)] = ag[j]


def reduce_kernel(nx, ny, x_ref, o_ref, gy_full, mine_y, rs_y, ag_y, mine_x, rs_x, ag_x,
                  y_send, y_rs, y_ag, x_send, x_rs, x_ag):
    gx = lax.axis_index("gx")
    gy = lax.axis_index("gy")
    barrier = pltpu.get_barrier_semaphore()
    for j in range(nx):
        @pl.when(j != gx)
        def _():
            pl.semaphore_signal(barrier, inc=1, device_id={"gx": j, "gy": gy},
                                device_id_type=pl.DeviceIdType.MESH)
    for j in range(ny):
        @pl.when(j != gy)
        def _():
            pl.semaphore_signal(barrier, inc=1, device_id={"gx": gx, "gy": j},
                                device_id_type=pl.DeviceIdType.MESH)
    pl.semaphore_wait(barrier, nx + ny - 2)
    part = x_ref.shape[0] // ny

    def to_y(j, src, dst, slot, sem):
        return pltpu.make_async_remote_copy(
            src_ref=src, dst_ref=dst.at[slot], send_sem=y_send.at[j], recv_sem=sem.at[slot],
            device_id={"gx": gx, "gy": j}, device_id_type=pl.DeviceIdType.MESH,
        )

    def to_x(j, slot):
        return pltpu.make_async_remote_copy(
            src_ref=mine_y, dst_ref=rs_x.at[slot], send_sem=x_send.at[j], recv_sem=x_rs.at[slot],
            device_id={"gx": j, "gy": gy}, device_id_type=pl.DeviceIdType.MESH,
        )

    for j in range(ny):
        @pl.when(j != gy)
        def _():
            to_y(j, x_ref.at[pl.ds(j * part, part)], rs_y, gy, y_rs).start()
    rs_y[gy] = x_ref[pl.ds(pl.multiple_of(gy * part, part), part)]
    for j in range(ny):
        @pl.when(j != gy)
        def _():
            to_y(j, x_ref.at[pl.ds(j * part, part)], rs_y, gy, y_rs).wait_send()
            to_y(j, x_ref.at[pl.ds(j * part, part)], rs_y, j, y_rs).wait_recv()
    acc = rs_y[0]
    for j in range(1, ny):
        acc = acc + rs_y[j]
    mine_y[...] = acc
    for j in range(nx):
        @pl.when(j != gx)
        def _():
            to_x(j, gx).start()
    rs_x[gx] = acc
    for j in range(nx):
        @pl.when(j != gx)
        def _():
            to_x(j, gx).wait_send()
            to_x(j, j).wait_recv()
    acc = rs_x[0]
    for j in range(1, nx):
        acc = acc + rs_x[j]
    mine_x[...] = acc
    for j in range(ny):
        @pl.when(j != gy)
        def _():
            to_y(j, mine_x, ag_y, gy, y_ag).start()
    ag_y[gy] = acc
    for j in range(ny):
        @pl.when(j != gy)
        def _():
            to_y(j, mine_x, ag_y, gy, y_ag).wait_send()
            to_y(j, mine_x, ag_y, j, y_ag).wait_recv()
    for j in range(ny):
        o_ref[pl.ds(j * part, part)] = ag_y[j]


def gram_sum(local_gram):
    size = local_gram.shape[0]
    nx, ny = lax.axis_size("gx"), lax.axis_size("gy")
    pad = 128
    py, px = pad // ny, pad // nx
    f32 = jnp.float32
    wide = jnp.pad(local_gram, ((0, pad - size), (0, pad - size)))
    vmem = pl.BlockSpec(memory_space=pltpu.VMEM)
    total = pl.pallas_call(
        lambda *refs: reduce_kernel(nx, ny, *refs),
        out_shape=jax.ShapeDtypeStruct((pad, pad), f32),
        in_specs=[vmem],
        out_specs=vmem,
        scratch_shapes=[
            pltpu.VMEM((pad, pad), f32),
            pltpu.VMEM((py, pad), f32),
            pltpu.VMEM((ny, py, pad), f32),
            pltpu.VMEM((ny, py, pad), f32),
            pltpu.VMEM((py, pad), f32),
            pltpu.VMEM((nx, py, pad), f32),
            pltpu.VMEM((nx, py, pad), f32),
            pltpu.SemaphoreType.DMA((ny,)),
            pltpu.SemaphoreType.DMA((ny,)),
            pltpu.SemaphoreType.DMA((ny,)),
            pltpu.SemaphoreType.DMA((nx,)),
            pltpu.SemaphoreType.DMA((nx,)),
            pltpu.SemaphoreType.DMA((nx,)),
        ],
        compiler_params=pltpu.CompilerParams(collective_id=4, has_side_effects=True),
        name="gram_allreduce",
    )(wide)
    return total[:size, :size]


def krylov_kernel(nx, ny, bx, v0_ref, terms_ref, diag_ref, out_ref,
                  halo_x, xsend, ysend, xr, yr, send_sem, recv_sem):
    gx = lax.axis_index("gx")
    gy = lax.axis_index("gy")
    rhs = out_ref.shape[1] // terms_ref.shape[1]
    rows, lanes = terms_ref.shape[1], terms_ref.shape[2]
    cells = out_ref.shape[1]
    zero_x = jnp.zeros(xr.shape[2:], jnp.float32)
    zero_y = jnp.zeros(yr.shape[2:], jnp.float32)
    for k in range(xr.shape[0]):
        for d in range(2):
            xr[k, d] = zero_x
            yr[k, d] = zero_y
    targets = (
        (gx < nx - 1, {"gx": gx + 1, "gy": gy}, gx > 0),
        (gx > 0, {"gx": gx - 1, "gy": gy}, gx < nx - 1),
        (gy < ny - 1, {"gx": gx, "gy": gy + 1}, gy > 0),
        (gy > 0, {"gx": gx, "gy": gy - 1}, gy < ny - 1),
    )
    barrier = pltpu.get_barrier_semaphore()
    for has_target, target, _ in targets:
        @pl.when(has_target)
        def _():
            pl.semaphore_signal(barrier, inc=1, device_id=target, device_id_type=pl.DeviceIdType.MESH)
    peers = (gx + nx - 1) // nx + (2 * nx - 2 - gx) // nx + (gy + ny - 1) // ny + (2 * ny - 2 - gy) // ny
    pl.semaphore_wait(barrier, peers)

    row = lax.broadcasted_iota(jnp.int32, (rhs, rows, lanes), 1)
    lane = lax.broadcasted_iota(jnp.int32, (rhs, rows, lanes), 2)
    xpos = row % bx
    zpos = row // bx
    nzp = rows // bx
    t = [terms_ref[i][None] for i in range(6)]
    diag = diag_ref[...][None]
    trow = lax.broadcasted_iota(jnp.int32, (lanes, cells), 0)

    out_ref[0] = v0_ref[...]
    for k in range(xr.shape[0]):
        flat = out_ref[k]
        xsend[0] = out_ref[k, pl.ds(0, cells // bx, stride=bx), :]
        xsend[1] = out_ref[k, pl.ds(bx - 1, cells // bx, stride=bx), :]
        tr = flat.T
        ysend[...] = jnp.where(trow[:8] == 0, tr[0:1], jnp.where(trow[:8] == 1, tr[lanes - 1:lanes], 0.0))
        plan = (
            (xsend.at[1], xr.at[k, 0]),
            (xsend.at[0], xr.at[k, 1]),
            (ysend, yr.at[k, 0]),
            (ysend, yr.at[k, 1]),
        )

        def copy(d):
            return pltpu.make_async_remote_copy(
                src_ref=plan[d][0], dst_ref=plan[d][1], send_sem=send_sem.at[d],
                recv_sem=recv_sem.at[k, d], device_id=targets[d][1],
                device_id_type=pl.DeviceIdType.MESH,
            )

        for d in range(4):
            @pl.when(targets[d][0])
            def _():
                copy(d).start()
        for d in range(4):
            @pl.when(targets[d][2])
            def _():
                copy(d).wait_recv()

        halo_x[pl.ds(0, cells // bx, stride=bx), :] = xr[k, 0]
        halo_x[pl.ds(bx - 1, cells // bx, stride=bx), :] = xr[k, 1]
        before = yr[k, 0][1:2]
        after = yr[k, 1][0:1]
        ycols = jnp.where(trow == 0, before, jnp.where(trow == lanes - 1, after, 0.0)).T
        v = flat.reshape(rhs, rows, lanes)
        hx = halo_x[...].reshape(rhs, rows, lanes)
        hy = ycols.reshape(rhs, rows, lanes)
        zm = jnp.where(zpos == 0, 0.0, pltpu.roll(v, bx, 1))
        zp = jnp.where(zpos == nzp - 1, 0.0, pltpu.roll(v, rows - bx, 1))
        xm = jnp.where(xpos == 0, hx, pltpu.roll(v, 1, 1))
        xp = jnp.where(xpos == bx - 1, hx, pltpu.roll(v, rows - 1, 1))
        ym = jnp.where(lane == 0, hy, pltpu.roll(v, 1, 2))
        yp = jnp.where(lane == lanes - 1, hy, pltpu.roll(v, lanes - 1, 2))
        total = t[0] * zm + t[1] * zp
        total = total + t[2] * xm + t[3] * xp
        total = total + t[4] * ym + t[5] * yp
        out_ref[k + 1] = (-total / diag).reshape(cells, lanes)
        for d in range(4):
            @pl.when(targets[d][0])
            def _():
                copy(d).wait_send()


def krylov_basis(v0, terms, diagonal):
    rhs, nz, bx, by = v0.shape
    nx, ny = lax.axis_size("gx"), lax.axis_size("gy")
    cells = rhs * nz * bx
    vmem = pl.BlockSpec(memory_space=pltpu.VMEM)
    out = pl.pallas_call(
        lambda *refs: krylov_kernel(nx, ny, bx, *refs),
        out_shape=jax.ShapeDtypeStruct((S + 1, cells, by), jnp.float32),
        in_specs=[vmem] * 3,
        out_specs=vmem,
        scratch_shapes=[
            pltpu.VMEM((cells, by), jnp.float32),
            pltpu.VMEM((2, cells // bx, by), jnp.float32),
            pltpu.VMEM((8, cells), jnp.float32),
            pltpu.VMEM((S, 2, cells // bx, by), jnp.float32),
            pltpu.VMEM((S, 2, 8, cells), jnp.float32),
            pltpu.SemaphoreType.DMA((4,)),
            pltpu.SemaphoreType.DMA((S, 4)),
        ],
        compiler_params=pltpu.CompilerParams(collective_id=3, has_side_effects=True),
        name="krylov_basis",
    )(v0.reshape(cells, by), jnp.stack(terms).reshape(6, nz * bx, by), diagonal.reshape(nz * bx, by))
    return out.reshape(S + 1, rhs, nz, bx, by)


def face_terms(padded, storage):
    core = padded[1:-1, 1:-1, 1:-1]
    terms = (
        (core + padded[:-2, 1:-1, 1:-1]) * 0.5,
        (core + padded[2:, 1:-1, 1:-1]) * 0.5,
        (core + padded[1:-1, :-2, 1:-1]) * 0.5,
        (core + padded[1:-1, 2:, 1:-1]) * 0.5,
        (core + padded[1:-1, 1:-1, :-2]) * 0.5,
        (core + padded[1:-1, 1:-1, 2:]) * 0.5,
    )
    diagonal = storage + terms[0] + terms[1] + terms[2] + terms[3] + terms[4] + terms[5]
    return (terms, diagonal)


def _device(axis, index, other_axis, other_index):
    return {axis: index, other_axis: other_index}


def small_solve(gram_all):
    shift_matrix = jnp.eye(BASIS, BASIS - RHS, dtype=jnp.float32) + jnp.eye(
        BASIS, BASIS - RHS, k=-RHS, dtype=jnp.float32
    )
    first_block = jnp.eye(BASIS, RHS, dtype=jnp.float32)
    hp = lax.Precision.HIGHEST
    gram_shift = jnp.dot(gram_all, shift_matrix, precision=hp)
    normal = jnp.dot(shift_matrix.T, gram_shift, precision=hp)
    right_side = jnp.dot(gram_shift.T, first_block, precision=hp)
    lower = jnp.linalg.cholesky(normal)
    y = jax.scipy.linalg.cho_solve((lower, True), right_side)
    coeffs = first_block - jnp.dot(shift_matrix, y, precision=hp)
    return (y, coeffs)


def shards(pumping, conductivity, capacity):
    hp = lax.Precision.HIGHEST
    shape = pumping.shape
    cond_halo = padded_2(conductivity, (("gx", 1), ("gy", 2)), 1)
    cond_pad = jnp.pad(cond_halo, ((1, 1), (0, 0), (0, 0)))
    terms, diagonal = face_terms(cond_pad, capacity)
    solution = jnp.zeros(shape, jnp.float32)
    residual = pumping / diagonal
    for restart in range(CYCLES):
        stacked = krylov_basis(residual, terms, diagonal).reshape(BASIS, -1)
        local_gram = jnp.dot(stacked, stacked.T, precision=hp)
        gram_all = gram_sum(local_gram)
        y, coeffs = small_solve(gram_all)
        y_full = jnp.concatenate([y, jnp.zeros((RHS, RHS), jnp.float32)], axis=0)
        both = jnp.dot(jnp.concatenate([y_full, coeffs], axis=1).T, stacked, precision=hp)
        solution = solution + both[:RHS].reshape(shape)
        residual = both[RHS:].reshape(shape)
    return (solution, residual)


def solution(mesh):
    return jax.shard_map(
        shards,
        mesh=mesh,
        in_specs=(P(None, None, "gx", "gy"), P(None, "gx", "gy"), P(None, "gx", "gy")),
        out_specs=(P(None, None, "gx", "gy"), P(None, None, "gx", "gy")),
        check_vma=False,
    )
```

```python
import jax
import jax.numpy as jnp
from jax import lax
from jax.sharding import PartitionSpec as P
from jax.experimental import pallas as pl
from jax.experimental.pallas import tpu as pltpu

RHS = 16
S = 4
CYCLES = 5
BASIS = 80


def padded_2(array, sides, width):
    for axis, dim in sides:
        devices, length = (lax.axis_size(axis), array.shape[dim])
        up = [(i, (i + 1) % devices) for i in range(devices - 1)]
        down = [(j, i) for i, j in up]
        last = lax.slice_in_dim(array, length - width, length, axis=dim)
        leading = lax.slice_in_dim(array, 0, width, axis=dim)
        before = lax.ppermute(last, axis, up)
        after = lax.ppermute(leading, axis, down)
        array = jnp.concatenate([before, array, after], axis=dim)
    return array


def halo_faces(array, xdim, ydim):
    out = {}
    for axis, dim in (("gx", xdim), ("gy", ydim)):
        devices, length = (lax.axis_size(axis), array.shape[dim])
        up = [(i, (i + 1) % devices) for i in range(devices - 1)]
        down = [(j, i) for i, j in up]
        last = lax.slice_in_dim(array, length - 1, length, axis=dim)
        leading = lax.slice_in_dim(array, 0, 1, axis=dim)
        out[axis] = (lax.ppermute(last, axis, up), lax.ppermute(leading, axis, down))
    rows = jnp.concatenate([out["gx"][0], array, out["gx"][1]], axis=xdim)
    widths = [(0, 0)] * array.ndim
    widths[xdim] = (1, 1)
    return jnp.concatenate([jnp.pad(out["gy"][0], widths), rows, jnp.pad(out["gy"][1], widths)], axis=ydim)


def exchange_reduce(axis, other_axis, n, src, mine, rs, ag, full, send_sem, rs_sem, ag_sem):
    me = lax.axis_index(axis)
    other = lax.axis_index(other_axis)
    part = src.shape[0] // n

    def scatter(j, slot):
        return pltpu.make_async_remote_copy(
            src_ref=src.at[pl.ds(j * part, part)], dst_ref=rs.at[slot], send_sem=send_sem.at[j],
            recv_sem=rs_sem.at[slot], device_id=_device(axis, j, other_axis, other),
            device_id_type=pl.DeviceIdType.MESH,
        )

    def gather(j, slot):
        return pltpu.make_async_remote_copy(
            src_ref=mine, dst_ref=ag.at[slot], send_sem=send_sem.at[j],
            recv_sem=ag_sem.at[slot], device_id=_device(axis, j, other_axis, other),
            device_id_type=pl.DeviceIdType.MESH,
        )

    for j in range(n):
        @pl.when(j != me)
        def _():
            scatter(j, me).start()
    rs[me] = src[pl.ds(pl.multiple_of(me * part, part), part)]
    for j in range(n):
        @pl.when(j != me)
        def _():
            scatter(j, me).wait_send()
            scatter(j, j).wait_recv()
    acc = rs[0]
    for j in range(1, n):
        acc = acc + rs[j]
    mine[...] = acc
    for j in range(n):
        @pl.when(j != me)
        def _():
            gather(j, me).start()
    ag[me] = acc
    for j in range(n):
        @pl.when(j != me)
        def _():
            gather(j, me).wait_send()
            gather(j, j).wait_recv()
    for j in range(n):
        full[pl.ds(j * part, part)] = ag[j]


def reduce_kernel(nx, ny, x_ref, o_ref, gy_full, mine_y, rs_y, ag_y, mine_x, rs_x, ag_x,
                  y_send, y_rs, y_ag, x_send, x_rs, x_ag):
    gx = lax.axis_index("gx")
    gy = lax.axis_index("gy")
    barrier = pltpu.get_barrier_semaphore()
    for j in range(nx):
        @pl.when(j != gx)
        def _():
            pl.semaphore_signal(barrier, inc=1, device_id={"gx": j, "gy": gy},
                                device_id_type=pl.DeviceIdType.MESH)
    for j in range(ny):
        @pl.when(j != gy)
        def _():
            pl.semaphore_signal(barrier, inc=1, device_id={"gx": gx, "gy": j},
                                device_id_type=pl.DeviceIdType.MESH)
    pl.semaphore_wait(barrier, nx + ny - 2)
    part = x_ref.shape[0] // ny

    def to_y(j, src, dst, slot, sem):
        return pltpu.make_async_remote_copy(
            src_ref=src, dst_ref=dst.at[slot], send_sem=y_send.at[j], recv_sem=sem.at[slot],
            device_id={"gx": gx, "gy": j}, device_id_type=pl.DeviceIdType.MESH,
        )

    def to_x(j, slot):
        return pltpu.make_async_remote_copy(
            src_ref=mine_y, dst_ref=rs_x.at[slot], send_sem=x_send.at[j], recv_sem=x_rs.at[slot],
            device_id={"gx": j, "gy": gy}, device_id_type=pl.DeviceIdType.MESH,
        )

    for j in range(ny):
        @pl.when(j != gy)
        def _():
            to_y(j, x_ref.at[pl.ds(j * part, part)], rs_y, gy, y_rs).start()
    rs_y[gy] = x_ref[pl.ds(pl.multiple_of(gy * part, part), part)]
    for j in range(ny):
        @pl.when(j != gy)
        def _():
            to_y(j, x_ref.at[pl.ds(j * part, part)], rs_y, gy, y_rs).wait_send()
            to_y(j, x_ref.at[pl.ds(j * part, part)], rs_y, j, y_rs).wait_recv()
    acc = rs_y[0]
    for j in range(1, ny):
        acc = acc + rs_y[j]
    mine_y[...] = acc
    for j in range(nx):
        @pl.when(j != gx)
        def _():
            to_x(j, gx).start()
    rs_x[gx] = acc
    for j in range(nx):
        @pl.when(j != gx)
        def _():
            to_x(j, gx).wait_send()
            to_x(j, j).wait_recv()
    acc = rs_x[0]
    for j in range(1, nx):
        acc = acc + rs_x[j]
    mine_x[...] = acc
    for j in range(ny):
        @pl.when(j != gy)
        def _():
            to_y(j, mine_x, ag_y, gy, y_ag).start()
    ag_y[gy] = acc
    for j in range(ny):
        @pl.when(j != gy)
        def _():
            to_y(j, mine_x, ag_y, gy, y_ag).wait_send()
            to_y(j, mine_x, ag_y, j, y_ag).wait_recv()
    for j in range(ny):
        o_ref[pl.ds(j * part, part)] = ag_y[j]


def gram_sum(local_gram):
    size = local_gram.shape[0]
    nx, ny = lax.axis_size("gx"), lax.axis_size("gy")
    pad = 128
    py, px = pad // ny, pad // nx
    f32 = jnp.float32
    wide = jnp.pad(local_gram, ((0, pad - size), (0, pad - size)))
    vmem = pl.BlockSpec(memory_space=pltpu.VMEM)
    total = pl.pallas_call(
        lambda *refs: reduce_kernel(nx, ny, *refs),
        out_shape=jax.ShapeDtypeStruct((pad, pad), f32),
        in_specs=[vmem],
        out_specs=vmem,
        scratch_shapes=[
            pltpu.VMEM((pad, pad), f32),
            pltpu.VMEM((py, pad), f32),
            pltpu.VMEM((ny, py, pad), f32),
            pltpu.VMEM((ny, py, pad), f32),
            pltpu.VMEM((py, pad), f32),
            pltpu.VMEM((nx, py, pad), f32),
            pltpu.VMEM((nx, py, pad), f32),
            pltpu.SemaphoreType.DMA((ny,)),
            pltpu.SemaphoreType.DMA((ny,)),
            pltpu.SemaphoreType.DMA((ny,)),
            pltpu.SemaphoreType.DMA((nx,)),
            pltpu.SemaphoreType.DMA((nx,)),
            pltpu.SemaphoreType.DMA((nx,)),
        ],
        compiler_params=pltpu.CompilerParams(collective_id=4, has_side_effects=True),
        name="gram_allreduce",
    )(wide)
    return total[:size, :size]


def krylov_kernel(nx, ny, bx, v0_ref, terms_ref, diag_ref, out_ref,
                  halo_x, xsend, ysend, xr, yr, send_sem, recv_sem):
    gx = lax.axis_index("gx")
    gy = lax.axis_index("gy")
    rhs = out_ref.shape[1] // terms_ref.shape[1]
    rows, lanes = terms_ref.shape[1], terms_ref.shape[2]
    cells = out_ref.shape[1]
    zero_x = jnp.zeros(xr.shape[2:], jnp.float32)
    zero_y = jnp.zeros(yr.shape[2:], jnp.float32)
    for k in range(xr.shape[0]):
        for d in range(2):
            xr[k, d] = zero_x
            yr[k, d] = zero_y
    targets = (
        (gx < nx - 1, {"gx": gx + 1, "gy": gy}, gx > 0),
        (gx > 0, {"gx": gx - 1, "gy": gy}, gx < nx - 1),
        (gy < ny - 1, {"gx": gx, "gy": gy + 1}, gy > 0),
        (gy > 0, {"gx": gx, "gy": gy - 1}, gy < ny - 1),
    )
    barrier = pltpu.get_barrier_semaphore()
    for has_target, target, _ in targets:
        @pl.when(has_target)
        def _():
            pl.semaphore_signal(barrier, inc=1, device_id=target, device_id_type=pl.DeviceIdType.MESH)
    peers = (gx + nx - 1) // nx + (2 * nx - 2 - gx) // nx + (gy + ny - 1) // ny + (2 * ny - 2 - gy) // ny
    pl.semaphore_wait(barrier, peers)

    row = lax.broadcasted_iota(jnp.int32, (rhs, rows, lanes), 1)
    lane = lax.broadcasted_iota(jnp.int32, (rhs, rows, lanes), 2)
    xpos = row % bx
    zpos = row // bx
    nzp = rows // bx
    t = [terms_ref[i][None] for i in range(6)]
    diag = diag_ref[...][None]
    trow = lax.broadcasted_iota(jnp.int32, (lanes, cells), 0)

    out_ref[0] = v0_ref[...]
    for k in range(xr.shape[0]):
        flat = out_ref[k]
        xsend[0] = out_ref[k, pl.ds(0, cells // bx, stride=bx), :]
        xsend[1] = out_ref[k, pl.ds(bx - 1, cells // bx, stride=bx), :]
        tr = flat.T
        ysend[...] = jnp.where(trow[:8] == 0, tr[0:1], jnp.where(trow[:8] == 1, tr[lanes - 1:lanes], 0.0))
        plan = (
            (xsend.at[1], xr.at[k, 0]),
            (xsend.at[0], xr.at[k, 1]),
            (ysend, yr.at[k, 0]),
            (ysend, yr.at[k, 1]),
        )

        def copy(d):
            return pltpu.make_async_remote_copy(
                src_ref=plan[d][0], dst_ref=plan[d][1], send_sem=send_sem.at[d],
                recv_sem=recv_sem.at[k, d], device_id=targets[d][1],
                device_id_type=pl.DeviceIdType.MESH,
            )

        for d in range(4):
            @pl.when(targets[d][0])
            def _():
                copy(d).start()
        for d in range(4):
            @pl.when(targets[d][0])
            def _():
                copy(d).wait_send()

            @pl.when(targets[d][2])
            def _():
                copy(d).wait_recv()

        halo_x[pl.ds(0, cells // bx, stride=bx), :] = xr[k, 0]
        halo_x[pl.ds(bx - 1, cells // bx, stride=bx), :] = xr[k, 1]
        before = yr[k, 0][1:2]
        after = yr[k, 1][0:1]
        ycols = jnp.where(trow == 0, before, jnp.where(trow == lanes - 1, after, 0.0)).T
        v = flat.reshape(rhs, rows, lanes)
        hx = halo_x[...].reshape(rhs, rows, lanes)
        hy = ycols.reshape(rhs, rows, lanes)
        zm = jnp.where(zpos == 0, 0.0, pltpu.roll(v, bx, 1))
        zp = jnp.where(zpos == nzp - 1, 0.0, pltpu.roll(v, rows - bx, 1))
        xm = jnp.where(xpos == 0, hx, pltpu.roll(v, 1, 1))
        xp = jnp.where(xpos == bx - 1, hx, pltpu.roll(v, rows - 1, 1))
        ym = jnp.where(lane == 0, hy, pltpu.roll(v, 1, 2))
        yp = jnp.where(lane == lanes - 1, hy, pltpu.roll(v, lanes - 1, 2))
        total = t[0] * zm + t[1] * zp
        total = total + t[2] * xm + t[3] * xp
        total = total + t[4] * ym + t[5] * yp
        out_ref[k + 1] = (-total / diag).reshape(cells, lanes)


def krylov_basis(v0, terms, diagonal):
    rhs, nz, bx, by = v0.shape
    nx, ny = lax.axis_size("gx"), lax.axis_size("gy")
    cells = rhs * nz * bx
    vmem = pl.BlockSpec(memory_space=pltpu.VMEM)
    out = pl.pallas_call(
        lambda *refs: krylov_kernel(nx, ny, bx, *refs),
        out_shape=jax.ShapeDtypeStruct((S + 1, cells, by), jnp.float32),
        in_specs=[vmem] * 3,
        out_specs=vmem,
        scratch_shapes=[
            pltpu.VMEM((cells, by), jnp.float32),
            pltpu.VMEM((2, cells // bx, by), jnp.float32),
            pltpu.VMEM((8, cells), jnp.float32),
            pltpu.VMEM((S, 2, cells // bx, by), jnp.float32),
            pltpu.VMEM((S, 2, 8, cells), jnp.float32),
            pltpu.SemaphoreType.DMA((4,)),
            pltpu.SemaphoreType.DMA((S, 4)),
        ],
        compiler_params=pltpu.CompilerParams(collective_id=3, has_side_effects=True),
        name="krylov_basis",
    )(v0.reshape(cells, by), jnp.stack(terms).reshape(6, nz * bx, by), diagonal.reshape(nz * bx, by))
    return out.reshape(S + 1, rhs, nz, bx, by)


def face_terms(padded, storage):
    core = padded[1:-1, 1:-1, 1:-1]
    terms = (
        (core + padded[:-2, 1:-1, 1:-1]) * 0.5,
        (core + padded[2:, 1:-1, 1:-1]) * 0.5,
        (core + padded[1:-1, :-2, 1:-1]) * 0.5,
        (core + padded[1:-1, 2:, 1:-1]) * 0.5,
        (core + padded[1:-1, 1:-1, :-2]) * 0.5,
        (core + padded[1:-1, 1:-1, 2:]) * 0.5,
    )
    diagonal = storage + terms[0] + terms[1] + terms[2] + terms[3] + terms[4] + terms[5]
    return (terms, diagonal)


def _device(axis, index, other_axis, other_index):
    return {axis: index, other_axis: other_index}


def small_solve(gram_all):
    shift_matrix = jnp.eye(BASIS, BASIS - RHS, dtype=jnp.float32) + jnp.eye(
        BASIS, BASIS - RHS, k=-RHS, dtype=jnp.float32
    )
    first_block = jnp.eye(BASIS, RHS, dtype=jnp.float32)
    hp = lax.Precision.HIGHEST
    gram_shift = jnp.dot(gram_all, shift_matrix, precision=hp)
    normal = jnp.dot(shift_matrix.T, gram_shift, precision=hp)
    right_side = jnp.dot(gram_shift.T, first_block, precision=hp)
    lower = jnp.linalg.cholesky(normal)
    y = jax.scipy.linalg.cho_solve((lower, True), right_side)
    coeffs = first_block - jnp.dot(shift_matrix, y, precision=hp)
    return (y, coeffs)


def shards(pumping, conductivity, capacity):
    hp = lax.Precision.HIGHEST
    shape = pumping.shape
    cond_halo = halo_faces(conductivity, 1, 2)
    cond_pad = jnp.pad(cond_halo, ((1, 1), (0, 0), (0, 0)))
    terms, diagonal = face_terms(cond_pad, capacity)
    solution = jnp.zeros(shape, jnp.float32)
    residual = pumping / diagonal
    for restart in range(CYCLES):
        stacked = krylov_basis(residual, terms, diagonal).reshape(BASIS, -1)
        local_gram = jnp.dot(stacked, stacked.T, precision=hp)
        gram_all = gram_sum(local_gram)
        y, coeffs = small_solve(gram_all)
        y_full = jnp.concatenate([y, jnp.zeros((RHS, RHS), jnp.float32)], axis=0)
        both = jnp.dot(jnp.concatenate([y_full, coeffs], axis=1).T, stacked, precision=hp)
        solution = solution + both[:RHS].reshape(shape)
        residual = both[RHS:].reshape(shape)
    return (solution, residual)


def solution(mesh):
    return jax.shard_map(
        shards,
        mesh=mesh,
        in_specs=(P(None, None, "gx", "gy"), P(None, "gx", "gy"), P(None, "gx", "gy")),
        out_specs=(P(None, None, "gx", "gy"), P(None, None, "gx", "gy")),
        check_vma=False,
    )
```

```python
import jax
import jax.numpy as jnp
from jax import lax
from jax.sharding import PartitionSpec as P
from jax.experimental import pallas as pl
from jax.experimental.pallas import tpu as pltpu

RHS = 16
S = 4
CYCLES = 5
BASIS = 80


def padded_2(array, sides, width):
    for axis, dim in sides:
        devices, length = (lax.axis_size(axis), array.shape[dim])
        up = [(i, (i + 1) % devices) for i in range(devices - 1)]
        down = [(j, i) for i, j in up]
        last = lax.slice_in_dim(array, length - width, length, axis=dim)
        leading = lax.slice_in_dim(array, 0, width, axis=dim)
        before = lax.ppermute(last, axis, up)
        after = lax.ppermute(leading, axis, down)
        array = jnp.concatenate([before, array, after], axis=dim)
    return array


def halo_faces(array, xdim, ydim):
    out = {}
    for axis, dim in (("gx", xdim), ("gy", ydim)):
        devices, length = (lax.axis_size(axis), array.shape[dim])
        up = [(i, (i + 1) % devices) for i in range(devices - 1)]
        down = [(j, i) for i, j in up]
        last = lax.slice_in_dim(array, length - 1, length, axis=dim)
        leading = lax.slice_in_dim(array, 0, 1, axis=dim)
        out[axis] = (lax.ppermute(last, axis, up), lax.ppermute(leading, axis, down))
    rows = jnp.concatenate([out["gx"][0], array, out["gx"][1]], axis=xdim)
    widths = [(0, 0)] * array.ndim
    widths[xdim] = (1, 1)
    return jnp.concatenate([jnp.pad(out["gy"][0], widths), rows, jnp.pad(out["gy"][1], widths)], axis=ydim)


def exchange_reduce(axis, other_axis, n, src, mine, rs, ag, full, send_sem, rs_sem, ag_sem):
    me = lax.axis_index(axis)
    other = lax.axis_index(other_axis)
    part = src.shape[0] // n

    def scatter(j, slot):
        return pltpu.make_async_remote_copy(
            src_ref=src.at[pl.ds(j * part, part)], dst_ref=rs.at[slot], send_sem=send_sem.at[j],
            recv_sem=rs_sem.at[slot], device_id=_device(axis, j, other_axis, other),
            device_id_type=pl.DeviceIdType.MESH,
        )

    def gather(j, slot):
        return pltpu.make_async_remote_copy(
            src_ref=mine, dst_ref=ag.at[slot], send_sem=send_sem.at[j],
            recv_sem=ag_sem.at[slot], device_id=_device(axis, j, other_axis, other),
            device_id_type=pl.DeviceIdType.MESH,
        )

    for j in range(n):
        @pl.when(j != me)
        def _():
            scatter(j, me).start()
    rs[me] = src[pl.ds(pl.multiple_of(me * part, part), part)]
    for j in range(n):
        @pl.when(j != me)
        def _():
            scatter(j, me).wait_send()
            scatter(j, j).wait_recv()
    acc = rs[0]
    for j in range(1, n):
        acc = acc + rs[j]
    mine[...] = acc
    for j in range(n):
        @pl.when(j != me)
        def _():
            gather(j, me).start()
    ag[me] = acc
    for j in range(n):
        @pl.when(j != me)
        def _():
            gather(j, me).wait_send()
            gather(j, j).wait_recv()
    for j in range(n):
        full[pl.ds(j * part, part)] = ag[j]


def reduce_kernel(nx, ny, x_ref, o_ref, gy_full, mine_y, rs_y, ag_y, mine_x, rs_x, ag_x,
                  y_send, y_rs, y_ag, x_send, x_rs, x_ag):
    gx = lax.axis_index("gx")
    gy = lax.axis_index("gy")
    barrier = pltpu.get_barrier_semaphore()
    for j in range(nx):
        @pl.when(j != gx)
        def _():
            pl.semaphore_signal(barrier, inc=1, device_id={"gx": j, "gy": gy},
                                device_id_type=pl.DeviceIdType.MESH)
    for j in range(ny):
        @pl.when(j != gy)
        def _():
            pl.semaphore_signal(barrier, inc=1, device_id={"gx": gx, "gy": j},
                                device_id_type=pl.DeviceIdType.MESH)
    pl.semaphore_wait(barrier, nx + ny - 2)
    part = x_ref.shape[0] // ny

    def to_y(j, src, dst, slot, sem):
        return pltpu.make_async_remote_copy(
            src_ref=src, dst_ref=dst.at[slot], send_sem=y_send.at[j], recv_sem=sem.at[slot],
            device_id={"gx": gx, "gy": j}, device_id_type=pl.DeviceIdType.MESH,
        )

    def to_x(j, slot):
        return pltpu.make_async_remote_copy(
            src_ref=mine_y, dst_ref=rs_x.at[slot], send_sem=x_send.at[j], recv_sem=x_rs.at[slot],
            device_id={"gx": j, "gy": gy}, device_id_type=pl.DeviceIdType.MESH,
        )

    for j in range(ny):
        @pl.when(j != gy)
        def _():
            to_y(j, x_ref.at[pl.ds(j * part, part)], rs_y, gy, y_rs).start()
    rs_y[gy] = x_ref[pl.ds(pl.multiple_of(gy * part, part), part)]
    for j in range(ny):
        @pl.when(j != gy)
        def _():
            to_y(j, x_ref.at[pl.ds(j * part, part)], rs_y, gy, y_rs).wait_send()
            to_y(j, x_ref.at[pl.ds(j * part, part)], rs_y, j, y_rs).wait_recv()
    acc = rs_y[0]
    for j in range(1, ny):
        acc = acc + rs_y[j]
    mine_y[...] = acc
    for j in range(nx):
        @pl.when(j != gx)
        def _():
            to_x(j, gx).start()
    rs_x[gx] = acc
    for j in range(nx):
        @pl.when(j != gx)
        def _():
            to_x(j, gx).wait_send()
            to_x(j, j).wait_recv()
    acc = rs_x[0]
    for j in range(1, nx):
        acc = acc + rs_x[j]
    mine_x[...] = acc
    for j in range(ny):
        @pl.when(j != gy)
        def _():
            to_y(j, mine_x, ag_y, gy, y_ag).start()
    ag_y[gy] = acc
    for j in range(ny):
        @pl.when(j != gy)
        def _():
            to_y(j, mine_x, ag_y, gy, y_ag).wait_send()
            to_y(j, mine_x, ag_y, j, y_ag).wait_recv()
    for j in range(ny):
        o_ref[pl.ds(j * part, part)] = ag_y[j]


def gram_sum(local_gram):
    size = local_gram.shape[0]
    nx, ny = lax.axis_size("gx"), lax.axis_size("gy")
    pad = 128
    py, px = pad // ny, pad // nx
    f32 = jnp.float32
    wide = jnp.pad(local_gram, ((0, pad - size), (0, pad - size)))
    vmem = pl.BlockSpec(memory_space=pltpu.VMEM)
    total = pl.pallas_call(
        lambda *refs: reduce_kernel(nx, ny, *refs),
        out_shape=jax.ShapeDtypeStruct((pad, pad), f32),
        in_specs=[vmem],
        out_specs=vmem,
        scratch_shapes=[
            pltpu.VMEM((pad, pad), f32),
            pltpu.VMEM((py, pad), f32),
            pltpu.VMEM((ny, py, pad), f32),
            pltpu.VMEM((ny, py, pad), f32),
            pltpu.VMEM((py, pad), f32),
            pltpu.VMEM((nx, py, pad), f32),
            pltpu.VMEM((nx, py, pad), f32),
            pltpu.SemaphoreType.DMA((ny,)),
            pltpu.SemaphoreType.DMA((ny,)),
            pltpu.SemaphoreType.DMA((ny,)),
            pltpu.SemaphoreType.DMA((nx,)),
            pltpu.SemaphoreType.DMA((nx,)),
            pltpu.SemaphoreType.DMA((nx,)),
        ],
        compiler_params=pltpu.CompilerParams(collective_id=4, has_side_effects=True),
        name="gram_allreduce",
    )(wide)
    return total[:size, :size]


def krylov_kernel(nx, ny, bx, v0_ref, terms_ref, diag_ref, tiled_ref, out_ref,
                  halo_x, xsend, ysend, xr, yr, send_sem, recv_sem):
    gx = lax.axis_index("gx")
    gy = lax.axis_index("gy")
    rhs = out_ref.shape[1] // terms_ref.shape[1]
    rows, lanes = terms_ref.shape[1], terms_ref.shape[2]
    cells = out_ref.shape[1]
    zero_x = jnp.zeros(xr.shape[2:], jnp.float32)
    zero_y = jnp.zeros(yr.shape[2:], jnp.float32)
    for k in range(xr.shape[0]):
        for d in range(2):
            xr[k, d] = zero_x
            yr[k, d] = zero_y
    targets = (
        (gx < nx - 1, {"gx": gx + 1, "gy": gy}, gx > 0),
        (gx > 0, {"gx": gx - 1, "gy": gy}, gx < nx - 1),
        (gy < ny - 1, {"gx": gx, "gy": gy + 1}, gy > 0),
        (gy > 0, {"gx": gx, "gy": gy - 1}, gy < ny - 1),
    )
    barrier = pltpu.get_barrier_semaphore()
    for has_target, target, _ in targets:
        @pl.when(has_target)
        def _():
            pl.semaphore_signal(barrier, inc=1, device_id=target, device_id_type=pl.DeviceIdType.MESH)
    peers = (gx + nx - 1) // nx + (2 * nx - 2 - gx) // nx + (gy + ny - 1) // ny + (2 * ny - 2 - gy) // ny
    pl.semaphore_wait(barrier, peers)

    row = lax.broadcasted_iota(jnp.int32, (rhs, rows, lanes), 1)
    lane = lax.broadcasted_iota(jnp.int32, (rhs, rows, lanes), 2)
    xpos = row % bx
    zpos = row // bx
    nzp = rows // bx
    t = [terms_ref[i][None] for i in range(6)]
    diag = diag_ref[...][None]
    trow = lax.broadcasted_iota(jnp.int32, (lanes, cells), 0)

    out_ref[0] = v0_ref[...]
    for k in range(xr.shape[0]):
        flat = out_ref[k]
        xsend[0] = out_ref[k, pl.ds(0, cells // bx, stride=bx), :]
        xsend[1] = out_ref[k, pl.ds(bx - 1, cells // bx, stride=bx), :]
        tr = flat.T
        ysend[...] = jnp.where(trow[:8] == 0, tr[0:1], jnp.where(trow[:8] == 1, tr[lanes - 1:lanes], 0.0))
        plan = (
            (xsend.at[1], xr.at[k, 0]),
            (xsend.at[0], xr.at[k, 1]),
            (ysend, yr.at[k, 0]),
            (ysend, yr.at[k, 1]),
        )

        def copy(d):
            return pltpu.make_async_remote_copy(
                src_ref=plan[d][0], dst_ref=plan[d][1], send_sem=send_sem.at[d],
                recv_sem=recv_sem.at[k, d], device_id=targets[d][1],
                device_id_type=pl.DeviceIdType.MESH,
            )

        for d in range(4):
            @pl.when(targets[d][0])
            def _():
                copy(d).start()
        for d in range(4):
            @pl.when(targets[d][0])
            def _():
                copy(d).wait_send()

            @pl.when(targets[d][2])
            def _():
                copy(d).wait_recv()

        halo_x[pl.ds(0, cells // bx, stride=bx), :] = xr[k, 0]
        halo_x[pl.ds(bx - 1, cells // bx, stride=bx), :] = xr[k, 1]
        before = yr[k, 0][1:2]
        after = yr[k, 1][0:1]
        ycols = jnp.where(trow == 0, before, jnp.where(trow == lanes - 1, after, 0.0)).T
        v = flat.reshape(rhs, rows, lanes)
        hx = halo_x[...].reshape(rhs, rows, lanes)
        hy = ycols.reshape(rhs, rows, lanes)
        zm = jnp.where(zpos == 0, 0.0, pltpu.roll(v, bx, 1))
        zp = jnp.where(zpos == nzp - 1, 0.0, pltpu.roll(v, rows - bx, 1))
        xm = jnp.where(xpos == 0, hx, pltpu.roll(v, 1, 1))
        xp = jnp.where(xpos == bx - 1, hx, pltpu.roll(v, rows - 1, 1))
        ym = jnp.where(lane == 0, hy, pltpu.roll(v, 1, 2))
        yp = jnp.where(lane == lanes - 1, hy, pltpu.roll(v, lanes - 1, 2))
        total = t[0] * zm + t[1] * zp
        total = total + t[2] * xm + t[3] * xp
        total = total + t[4] * ym + t[5] * yp
        out_ref[k + 1] = (-total / diag).reshape(cells, lanes)

    groups = rhs // 8

    def to_tiled(zx, carry):
        for k in range(out_ref.shape[0]):
            for b in range(groups):
                tiled_ref[k * groups + b, zx] = out_ref[k, pl.ds(b * 8 * rows + zx, 8, stride=rows), :]
        return carry

    lax.fori_loop(0, rows, to_tiled, 0)


def krylov_basis(v0, terms, diagonal):
    rhs, nz, bx, by = v0.shape
    nx, ny = lax.axis_size("gx"), lax.axis_size("gy")
    cells = rhs * nz * bx
    vmem = pl.BlockSpec(memory_space=pltpu.VMEM)
    out = pl.pallas_call(
        lambda *refs: krylov_kernel(nx, ny, bx, *refs),
        out_shape=jax.ShapeDtypeStruct(((S + 1) * rhs // 8, nz * bx, 8, by), jnp.float32),
        in_specs=[vmem] * 3,
        out_specs=vmem,
        scratch_shapes=[
            pltpu.VMEM((S + 1, cells, by), jnp.float32),
            pltpu.VMEM((cells, by), jnp.float32),
            pltpu.VMEM((2, cells // bx, by), jnp.float32),
            pltpu.VMEM((8, cells), jnp.float32),
            pltpu.VMEM((S, 2, cells // bx, by), jnp.float32),
            pltpu.VMEM((S, 2, 8, cells), jnp.float32),
            pltpu.SemaphoreType.DMA((4,)),
            pltpu.SemaphoreType.DMA((S, 4)),
        ],
        compiler_params=pltpu.CompilerParams(collective_id=3, has_side_effects=True),
        name="krylov_basis",
    )(v0.reshape(cells, by), jnp.stack(terms).reshape(6, nz * bx, by), diagonal.reshape(nz * bx, by))
    return out.transpose(0, 2, 1, 3).reshape(BASIS, -1)


def face_terms(padded, storage):
    core = padded[1:-1, 1:-1, 1:-1]
    terms = (
        (core + padded[:-2, 1:-1, 1:-1]) * 0.5,
        (core + padded[2:, 1:-1, 1:-1]) * 0.5,
        (core + padded[1:-1, :-2, 1:-1]) * 0.5,
        (core + padded[1:-1, 2:, 1:-1]) * 0.5,
        (core + padded[1:-1, 1:-1, :-2]) * 0.5,
        (core + padded[1:-1, 1:-1, 2:]) * 0.5,
    )
    diagonal = storage + terms[0] + terms[1] + terms[2] + terms[3] + terms[4] + terms[5]
    return (terms, diagonal)


def _device(axis, index, other_axis, other_index):
    return {axis: index, other_axis: other_index}


def small_solve(gram_all):
    shift_matrix = jnp.eye(BASIS, BASIS - RHS, dtype=jnp.float32) + jnp.eye(
        BASIS, BASIS - RHS, k=-RHS, dtype=jnp.float32
    )
    first_block = jnp.eye(BASIS, RHS, dtype=jnp.float32)
    hp = lax.Precision.HIGHEST
    gram_shift = jnp.dot(gram_all, shift_matrix, precision=hp)
    normal = jnp.dot(shift_matrix.T, gram_shift, precision=hp)
    right_side = jnp.dot(gram_shift.T, first_block, precision=hp)
    lower = jnp.linalg.cholesky(normal)
    y = jax.scipy.linalg.cho_solve((lower, True), right_side)
    coeffs = first_block - jnp.dot(shift_matrix, y, precision=hp)
    return (y, coeffs)


def shards(pumping, conductivity, capacity):
    hp = lax.Precision.HIGHEST
    shape = pumping.shape
    cond_halo = halo_faces(conductivity, 1, 2)
    cond_pad = jnp.pad(cond_halo, ((1, 1), (0, 0), (0, 0)))
    terms, diagonal = face_terms(cond_pad, capacity)
    solution = jnp.zeros(shape, jnp.float32)
    residual = pumping / diagonal
    for restart in range(CYCLES):
        stacked = krylov_basis(residual, terms, diagonal)
        local_gram = jnp.dot(stacked, stacked.T, precision=hp)
        gram_all = gram_sum(local_gram)
        y, coeffs = small_solve(gram_all)
        y_full = jnp.concatenate([y, jnp.zeros((RHS, RHS), jnp.float32)], axis=0)
        both = jnp.dot(jnp.concatenate([y_full, coeffs], axis=1).T, stacked, precision=hp)
        solution = solution + both[:RHS].reshape(shape)
        residual = both[RHS:].reshape(shape)
    return (solution, residual)


def solution(mesh):
    return jax.shard_map(
        shards,
        mesh=mesh,
        in_specs=(P(None, None, "gx", "gy"), P(None, "gx", "gy"), P(None, "gx", "gy")),
        out_specs=(P(None, None, "gx", "gy"), P(None, None, "gx", "gy")),
        check_vma=False,
    )
```

```python
import jax
import jax.numpy as jnp
from jax import lax
from jax.sharding import PartitionSpec as P
from jax.experimental import pallas as pl
from jax.experimental.pallas import tpu as pltpu

RHS = 16
S = 4
CYCLES = 5
BASIS = 80


def padded_2(array, sides, width):
    for axis, dim in sides:
        devices, length = (lax.axis_size(axis), array.shape[dim])
        up = [(i, (i + 1) % devices) for i in range(devices - 1)]
        down = [(j, i) for i, j in up]
        last = lax.slice_in_dim(array, length - width, length, axis=dim)
        leading = lax.slice_in_dim(array, 0, width, axis=dim)
        before = lax.ppermute(last, axis, up)
        after = lax.ppermute(leading, axis, down)
        array = jnp.concatenate([before, array, after], axis=dim)
    return array


def halo_faces(array, xdim, ydim):
    out = {}
    for axis, dim in (("gx", xdim), ("gy", ydim)):
        devices, length = (lax.axis_size(axis), array.shape[dim])
        up = [(i, (i + 1) % devices) for i in range(devices - 1)]
        down = [(j, i) for i, j in up]
        last = lax.slice_in_dim(array, length - 1, length, axis=dim)
        leading = lax.slice_in_dim(array, 0, 1, axis=dim)
        out[axis] = (lax.ppermute(last, axis, up), lax.ppermute(leading, axis, down))
    rows = jnp.concatenate([out["gx"][0], array, out["gx"][1]], axis=xdim)
    widths = [(0, 0)] * array.ndim
    widths[xdim] = (1, 1)
    return jnp.concatenate([jnp.pad(out["gy"][0], widths), rows, jnp.pad(out["gy"][1], widths)], axis=ydim)


def exchange_reduce(axis, other_axis, n, src, mine, rs, ag, full, send_sem, rs_sem, ag_sem):
    me = lax.axis_index(axis)
    other = lax.axis_index(other_axis)
    part = src.shape[0] // n

    def scatter(j, slot):
        return pltpu.make_async_remote_copy(
            src_ref=src.at[pl.ds(j * part, part)], dst_ref=rs.at[slot], send_sem=send_sem.at[j],
            recv_sem=rs_sem.at[slot], device_id=_device(axis, j, other_axis, other),
            device_id_type=pl.DeviceIdType.MESH,
        )

    def gather(j, slot):
        return pltpu.make_async_remote_copy(
            src_ref=mine, dst_ref=ag.at[slot], send_sem=send_sem.at[j],
            recv_sem=ag_sem.at[slot], device_id=_device(axis, j, other_axis, other),
            device_id_type=pl.DeviceIdType.MESH,
        )

    for j in range(n):
        @pl.when(j != me)
        def _():
            scatter(j, me).start()
    rs[me] = src[pl.ds(pl.multiple_of(me * part, part), part)]
    for j in range(n):
        @pl.when(j != me)
        def _():
            scatter(j, me).wait_send()
            scatter(j, j).wait_recv()
    acc = rs[0]
    for j in range(1, n):
        acc = acc + rs[j]
    mine[...] = acc
    for j in range(n):
        @pl.when(j != me)
        def _():
            gather(j, me).start()
    ag[me] = acc
    for j in range(n):
        @pl.when(j != me)
        def _():
            gather(j, me).wait_send()
            gather(j, j).wait_recv()
    for j in range(n):
        full[pl.ds(j * part, part)] = ag[j]


def reduce_kernel(nx, ny, x_ref, o_ref, gy_full, mine_y, rs_y, ag_y, mine_x, rs_x, ag_x,
                  y_send, y_rs, y_ag, x_send, x_rs, x_ag):
    gx = lax.axis_index("gx")
    gy = lax.axis_index("gy")
    barrier = pltpu.get_barrier_semaphore()
    for j in range(nx):
        @pl.when(j != gx)
        def _():
            pl.semaphore_signal(barrier, inc=1, device_id={"gx": j, "gy": gy},
                                device_id_type=pl.DeviceIdType.MESH)
    for j in range(ny):
        @pl.when(j != gy)
        def _():
            pl.semaphore_signal(barrier, inc=1, device_id={"gx": gx, "gy": j},
                                device_id_type=pl.DeviceIdType.MESH)
    pl.semaphore_wait(barrier, nx + ny - 2)
    part = x_ref.shape[0] // ny

    def to_y(j, src, dst, slot, sem):
        return pltpu.make_async_remote_copy(
            src_ref=src, dst_ref=dst.at[slot], send_sem=y_send.at[j], recv_sem=sem.at[slot],
            device_id={"gx": gx, "gy": j}, device_id_type=pl.DeviceIdType.MESH,
        )

    def to_x(j, slot):
        return pltpu.make_async_remote_copy(
            src_ref=mine_y, dst_ref=rs_x.at[slot], send_sem=x_send.at[j], recv_sem=x_rs.at[slot],
            device_id={"gx": j, "gy": gy}, device_id_type=pl.DeviceIdType.MESH,
        )

    for j in range(ny):
        @pl.when(j != gy)
        def _():
            to_y(j, x_ref.at[pl.ds(j * part, part)], rs_y, gy, y_rs).start()
    rs_y[gy] = x_ref[pl.ds(pl.multiple_of(gy * part, part), part)]
    for j in range(ny):
        @pl.when(j != gy)
        def _():
            to_y(j, x_ref.at[pl.ds(j * part, part)], rs_y, gy, y_rs).wait_send()
            to_y(j, x_ref.at[pl.ds(j * part, part)], rs_y, j, y_rs).wait_recv()
    acc = rs_y[0]
    for j in range(1, ny):
        acc = acc + rs_y[j]
    mine_y[...] = acc
    for j in range(nx):
        @pl.when(j != gx)
        def _():
            to_x(j, gx).start()
    rs_x[gx] = acc
    for j in range(nx):
        @pl.when(j != gx)
        def _():
            to_x(j, gx).wait_send()
            to_x(j, j).wait_recv()
    acc = rs_x[0]
    for j in range(1, nx):
        acc = acc + rs_x[j]
    mine_x[...] = acc
    for j in range(ny):
        @pl.when(j != gy)
        def _():
            to_y(j, mine_x, ag_y, gy, y_ag).start()
    ag_y[gy] = acc
    for j in range(ny):
        @pl.when(j != gy)
        def _():
            to_y(j, mine_x, ag_y, gy, y_ag).wait_send()
            to_y(j, mine_x, ag_y, j, y_ag).wait_recv()
    for j in range(ny):
        o_ref[pl.ds(j * part, part)] = ag_y[j]


def gram_sum(local_gram):
    size = local_gram.shape[0]
    nx, ny = lax.axis_size("gx"), lax.axis_size("gy")
    pad = 128
    py, px = pad // ny, pad // nx
    f32 = jnp.float32
    wide = jnp.pad(local_gram, ((0, pad - size), (0, pad - size)))
    vmem = pl.BlockSpec(memory_space=pltpu.VMEM)
    total = pl.pallas_call(
        lambda *refs: reduce_kernel(nx, ny, *refs),
        out_shape=jax.ShapeDtypeStruct((pad, pad), f32),
        in_specs=[vmem],
        out_specs=vmem,
        scratch_shapes=[
            pltpu.VMEM((pad, pad), f32),
            pltpu.VMEM((py, pad), f32),
            pltpu.VMEM((ny, py, pad), f32),
            pltpu.VMEM((ny, py, pad), f32),
            pltpu.VMEM((py, pad), f32),
            pltpu.VMEM((nx, py, pad), f32),
            pltpu.VMEM((nx, py, pad), f32),
            pltpu.SemaphoreType.DMA((ny,)),
            pltpu.SemaphoreType.DMA((ny,)),
            pltpu.SemaphoreType.DMA((ny,)),
            pltpu.SemaphoreType.DMA((nx,)),
            pltpu.SemaphoreType.DMA((nx,)),
            pltpu.SemaphoreType.DMA((nx,)),
        ],
        compiler_params=pltpu.CompilerParams(collective_id=4, has_side_effects=True),
        name="gram_allreduce",
    )(wide)
    return total[:size, :size]


def krylov_kernel(nx, ny, bx, v0_ref, terms_ref, diag_ref, out_ref,
                  halo_x, xsend, ysend, xr, yr, send_sem, recv_sem):
    gx = lax.axis_index("gx")
    gy = lax.axis_index("gy")
    rhs = out_ref.shape[1] // terms_ref.shape[1]
    rows, lanes = terms_ref.shape[1], terms_ref.shape[2]
    cells = out_ref.shape[1]
    zero_x = jnp.zeros(xr.shape[2:], jnp.float32)
    zero_y = jnp.zeros(yr.shape[2:], jnp.float32)
    for k in range(xr.shape[0]):
        for d in range(2):
            xr[k, d] = zero_x
            yr[k, d] = zero_y
    targets = (
        (gx < nx - 1, {"gx": gx + 1, "gy": gy}, gx > 0),
        (gx > 0, {"gx": gx - 1, "gy": gy}, gx < nx - 1),
        (gy < ny - 1, {"gx": gx, "gy": gy + 1}, gy > 0),
        (gy > 0, {"gx": gx, "gy": gy - 1}, gy < ny - 1),
    )
    barrier = pltpu.get_barrier_semaphore()
    for has_target, target, _ in targets:
        @pl.when(has_target)
        def _():
            pl.semaphore_signal(barrier, inc=1, device_id=target, device_id_type=pl.DeviceIdType.MESH)
    peers = (gx + nx - 1) // nx + (2 * nx - 2 - gx) // nx + (gy + ny - 1) // ny + (2 * ny - 2 - gy) // ny
    pl.semaphore_wait(barrier, peers)

    row = lax.broadcasted_iota(jnp.int32, (rhs, rows, lanes), 1)
    lane = lax.broadcasted_iota(jnp.int32, (rhs, rows, lanes), 2)
    xpos = row % bx
    zpos = row // bx
    nzp = rows // bx
    t = [terms_ref[i][None] for i in range(6)]
    diag = diag_ref[...][None]
    trow = lax.broadcasted_iota(jnp.int32, (lanes, cells), 0)

    out_ref[0] = v0_ref[...]
    for k in range(xr.shape[0]):
        flat = out_ref[k]
        xsend[0] = out_ref[k, pl.ds(0, cells // bx, stride=bx), :]
        xsend[1] = out_ref[k, pl.ds(bx - 1, cells // bx, stride=bx), :]
        tr = flat.T
        ysend[...] = jnp.where(trow[:8] == 0, tr[0:1], jnp.where(trow[:8] == 1, tr[lanes - 1:lanes], 0.0))
        plan = (
            (xsend.at[1], xr.at[k, 0]),
            (xsend.at[0], xr.at[k, 1]),
            (ysend, yr.at[k, 0]),
            (ysend, yr.at[k, 1]),
        )

        def copy(d):
            return pltpu.make_async_remote_copy(
                src_ref=plan[d][0], dst_ref=plan[d][1], send_sem=send_sem.at[d],
                recv_sem=recv_sem.at[k, d], device_id=targets[d][1],
                device_id_type=pl.DeviceIdType.MESH,
            )

        for d in range(4):
            @pl.when(targets[d][0])
            def _():
                copy(d).start()
        for d in range(4):
            @pl.when(targets[d][0])
            def _():
                copy(d).wait_send()

            @pl.when(targets[d][2])
            def _():
                copy(d).wait_recv()

        halo_x[pl.ds(0, cells // bx, stride=bx), :] = xr[k, 0]
        halo_x[pl.ds(bx - 1, cells // bx, stride=bx), :] = xr[k, 1]
        before = yr[k, 0][1:2]
        after = yr[k, 1][0:1]
        ycols = jnp.where(trow == 0, before, jnp.where(trow == lanes - 1, after, 0.0)).T
        v = flat.reshape(rhs, rows, lanes)
        hx = halo_x[...].reshape(rhs, rows, lanes)
        hy = ycols.reshape(rhs, rows, lanes)
        zm = jnp.where(zpos == 0, 0.0, pltpu.roll(v, bx, 1))
        zp = jnp.where(zpos == nzp - 1, 0.0, pltpu.roll(v, rows - bx, 1))
        xm = jnp.where(xpos == 0, hx, pltpu.roll(v, 1, 1))
        xp = jnp.where(xpos == bx - 1, hx, pltpu.roll(v, rows - 1, 1))
        ym = jnp.where(lane == 0, hy, pltpu.roll(v, 1, 2))
        yp = jnp.where(lane == lanes - 1, hy, pltpu.roll(v, lanes - 1, 2))
        total = t[0] * zm + t[1] * zp
        total = total + t[2] * xm + t[3] * xp
        total = total + t[4] * ym + t[5] * yp
        out_ref[k + 1] = (-total / diag).reshape(cells, lanes)


def krylov_basis(v0, terms, diagonal):
    rhs, nz, bx, by = v0.shape
    nx, ny = lax.axis_size("gx"), lax.axis_size("gy")
    cells = rhs * nz * bx
    vmem = pl.BlockSpec(memory_space=pltpu.VMEM)
    out = pl.pallas_call(
        lambda *refs: krylov_kernel(nx, ny, bx, *refs),
        out_shape=jax.ShapeDtypeStruct((S + 1, cells, by), jnp.float32),
        in_specs=[vmem] * 3,
        out_specs=vmem,
        scratch_shapes=[
            pltpu.VMEM((cells, by), jnp.float32),
            pltpu.VMEM((2, cells // bx, by), jnp.float32),
            pltpu.VMEM((8, cells), jnp.float32),
            pltpu.VMEM((S, 2, cells // bx, by), jnp.float32),
            pltpu.VMEM((S, 2, 8, cells), jnp.float32),
            pltpu.SemaphoreType.DMA((4,)),
            pltpu.SemaphoreType.DMA((S, 4)),
        ],
        compiler_params=pltpu.CompilerParams(collective_id=3, has_side_effects=True),
        name="krylov_basis",
    )(v0.reshape(cells, by), jnp.stack(terms).reshape(6, nz * bx, by), diagonal.reshape(nz * bx, by))
    return out.reshape(S + 1, rhs, nz, bx, by)


def face_terms(padded, storage):
    core = padded[1:-1, 1:-1, 1:-1]
    terms = (
        (core + padded[:-2, 1:-1, 1:-1]) * 0.5,
        (core + padded[2:, 1:-1, 1:-1]) * 0.5,
        (core + padded[1:-1, :-2, 1:-1]) * 0.5,
        (core + padded[1:-1, 2:, 1:-1]) * 0.5,
        (core + padded[1:-1, 1:-1, :-2]) * 0.5,
        (core + padded[1:-1, 1:-1, 2:]) * 0.5,
    )
    diagonal = storage + terms[0] + terms[1] + terms[2] + terms[3] + terms[4] + terms[5]
    return (terms, diagonal)


def _device(axis, index, other_axis, other_index):
    return {axis: index, other_axis: other_index}


def small_solve(gram_all):
    shift_matrix = jnp.eye(BASIS, BASIS - RHS, dtype=jnp.float32) + jnp.eye(
        BASIS, BASIS - RHS, k=-RHS, dtype=jnp.float32
    )
    first_block = jnp.eye(BASIS, RHS, dtype=jnp.float32)
    hp = lax.Precision.HIGHEST
    gram_shift = jnp.dot(gram_all, shift_matrix, precision=hp)
    normal = jnp.dot(shift_matrix.T, gram_shift, precision=hp)
    right_side = jnp.dot(gram_shift.T, first_block, precision=hp)
    lower = jnp.linalg.cholesky(normal)
    y = jax.scipy.linalg.cho_solve((lower, True), right_side)
    coeffs = first_block - jnp.dot(shift_matrix, y, precision=hp)
    return (y, coeffs)


def shards(pumping, conductivity, capacity):
    hp = lax.Precision.HIGHEST
    shape = pumping.shape
    cond_halo = halo_faces(conductivity, 1, 2)
    cond_pad = jnp.pad(cond_halo, ((1, 1), (0, 0), (0, 0)))
    terms, diagonal = face_terms(cond_pad, capacity)
    solution = jnp.zeros(shape, jnp.float32)
    residual = pumping / diagonal
    for restart in range(CYCLES):
        powers = krylov_basis(residual, terms, diagonal)
        stacked = powers.reshape(BASIS, -1)
        local_gram = jnp.dot(stacked, stacked.T, precision=hp)
        gram_all = gram_sum(local_gram)
        y, coeffs = small_solve(gram_all)
        y_full = jnp.concatenate([y, jnp.zeros((RHS, RHS), jnp.float32)], axis=0)
        mix = jnp.concatenate([y_full, coeffs], axis=1).reshape(S + 1, RHS, 2 * RHS)
        both = jnp.einsum("kpc,kpzxy->czxy", mix, powers, precision=hp)
        solution = solution + both[:RHS]
        residual = both[RHS:]
    return (solution, residual)


def solution(mesh):
    return jax.shard_map(
        shards,
        mesh=mesh,
        in_specs=(P(None, None, "gx", "gy"), P(None, "gx", "gy"), P(None, "gx", "gy")),
        out_specs=(P(None, None, "gx", "gy"), P(None, None, "gx", "gy")),
        check_vma=False,
    )
```

```python
import jax
import jax.numpy as jnp
from jax import lax
from jax.sharding import PartitionSpec as P
from jax.experimental import pallas as pl
from jax.experimental.pallas import tpu as pltpu

RHS = 16
S = 4
CYCLES = 5
BASIS = 80


def padded_2(array, sides, width):
    for axis, dim in sides:
        devices, length = (lax.axis_size(axis), array.shape[dim])
        up = [(i, (i + 1) % devices) for i in range(devices - 1)]
        down = [(j, i) for i, j in up]
        last = lax.slice_in_dim(array, length - width, length, axis=dim)
        leading = lax.slice_in_dim(array, 0, width, axis=dim)
        before = lax.ppermute(last, axis, up)
        after = lax.ppermute(leading, axis, down)
        array = jnp.concatenate([before, array, after], axis=dim)
    return array


def halo_faces(array, xdim, ydim):
    out = {}
    for axis, dim in (("gx", xdim), ("gy", ydim)):
        devices, length = (lax.axis_size(axis), array.shape[dim])
        up = [(i, (i + 1) % devices) for i in range(devices - 1)]
        down = [(j, i) for i, j in up]
        last = lax.slice_in_dim(array, length - 1, length, axis=dim)
        leading = lax.slice_in_dim(array, 0, 1, axis=dim)
        out[axis] = (lax.ppermute(last, axis, up), lax.ppermute(leading, axis, down))
    rows = jnp.concatenate([out["gx"][0], array, out["gx"][1]], axis=xdim)
    widths = [(0, 0)] * array.ndim
    widths[xdim] = (1, 1)
    return jnp.concatenate([jnp.pad(out["gy"][0], widths), rows, jnp.pad(out["gy"][1], widths)], axis=ydim)


def exchange_reduce(axis, other_axis, n, src, mine, rs, ag, full, send_sem, rs_sem, ag_sem):
    me = lax.axis_index(axis)
    other = lax.axis_index(other_axis)
    part = src.shape[0] // n

    def scatter(j, slot):
        return pltpu.make_async_remote_copy(
            src_ref=src.at[pl.ds(j * part, part)], dst_ref=rs.at[slot], send_sem=send_sem.at[j],
            recv_sem=rs_sem.at[slot], device_id=_device(axis, j, other_axis, other),
            device_id_type=pl.DeviceIdType.MESH,
        )

    def gather(j, slot):
        return pltpu.make_async_remote_copy(
            src_ref=mine, dst_ref=ag.at[slot], send_sem=send_sem.at[j],
            recv_sem=ag_sem.at[slot], device_id=_device(axis, j, other_axis, other),
            device_id_type=pl.DeviceIdType.MESH,
        )

    for j in range(n):
        @pl.when(j != me)
        def _():
            scatter(j, me).start()
    rs[me] = src[pl.ds(pl.multiple_of(me * part, part), part)]
    for j in range(n):
        @pl.when(j != me)
        def _():
            scatter(j, me).wait_send()
            scatter(j, j).wait_recv()
    acc = rs[0]
    for j in range(1, n):
        acc = acc + rs[j]
    mine[...] = acc
    for j in range(n):
        @pl.when(j != me)
        def _():
            gather(j, me).start()
    ag[me] = acc
    for j in range(n):
        @pl.when(j != me)
        def _():
            gather(j, me).wait_send()
            gather(j, j).wait_recv()
    for j in range(n):
        full[pl.ds(j * part, part)] = ag[j]


def reduce_kernel(nx, ny, x_ref, o_ref, gy_full, mine_y, rs_y, ag_y, mine_x, rs_x, ag_x,
                  y_send, y_rs, y_ag, x_send, x_rs, x_ag):
    gx = lax.axis_index("gx")
    gy = lax.axis_index("gy")
    barrier = pltpu.get_barrier_semaphore()
    for j in range(nx):
        @pl.when(j != gx)
        def _():
            pl.semaphore_signal(barrier, inc=1, device_id={"gx": j, "gy": gy},
                                device_id_type=pl.DeviceIdType.MESH)
    for j in range(ny):
        @pl.when(j != gy)
        def _():
            pl.semaphore_signal(barrier, inc=1, device_id={"gx": gx, "gy": j},
                                device_id_type=pl.DeviceIdType.MESH)
    pl.semaphore_wait(barrier, nx + ny - 2)
    part = x_ref.shape[0] // ny

    def to_y(j, src, dst, slot, sem):
        return pltpu.make_async_remote_copy(
            src_ref=src, dst_ref=dst.at[slot], send_sem=y_send.at[j], recv_sem=sem.at[slot],
            device_id={"gx": gx, "gy": j}, device_id_type=pl.DeviceIdType.MESH,
        )

    def to_x(j, slot):
        return pltpu.make_async_remote_copy(
            src_ref=mine_y, dst_ref=rs_x.at[slot], send_sem=x_send.at[j], recv_sem=x_rs.at[slot],
            device_id={"gx": j, "gy": gy}, device_id_type=pl.DeviceIdType.MESH,
        )

    for j in range(ny):
        @pl.when(j != gy)
        def _():
            to_y(j, x_ref.at[pl.ds(j * part, part)], rs_y, gy, y_rs).start()
    rs_y[gy] = x_ref[pl.ds(pl.multiple_of(gy * part, part), part)]
    for j in range(ny):
        @pl.when(j != gy)
        def _():
            to_y(j, x_ref.at[pl.ds(j * part, part)], rs_y, gy, y_rs).wait_send()
            to_y(j, x_ref.at[pl.ds(j * part, part)], rs_y, j, y_rs).wait_recv()
    acc = rs_y[0]
    for j in range(1, ny):
        acc = acc + rs_y[j]
    mine_y[...] = acc
    for j in range(nx):
        @pl.when(j != gx)
        def _():
            to_x(j, gx).start()
    rs_x[gx] = acc
    for j in range(nx):
        @pl.when(j != gx)
        def _():
            to_x(j, gx).wait_send()
            to_x(j, j).wait_recv()
    acc = rs_x[0]
    for j in range(1, nx):
        acc = acc + rs_x[j]
    mine_x[...] = acc
    for j in range(ny):
        @pl.when(j != gy)
        def _():
            to_y(j, mine_x, ag_y, gy, y_ag).start()
    ag_y[gy] = acc
    for j in range(ny):
        @pl.when(j != gy)
        def _():
            to_y(j, mine_x, ag_y, gy, y_ag).wait_send()
            to_y(j, mine_x, ag_y, j, y_ag).wait_recv()
    for j in range(ny):
        o_ref[pl.ds(j * part, part)] = ag_y[j]


def gram_sum(local_gram):
    size = local_gram.shape[0]
    nx, ny = lax.axis_size("gx"), lax.axis_size("gy")
    pad = 128
    py, px = pad // ny, pad // nx
    f32 = jnp.float32
    wide = jnp.zeros((pad, pad), f32).at[:size, :size].set(local_gram)
    vmem = pl.BlockSpec(memory_space=pltpu.VMEM)
    total = pl.pallas_call(
        lambda *refs: reduce_kernel(nx, ny, *refs),
        out_shape=jax.ShapeDtypeStruct((pad, pad), f32),
        in_specs=[vmem],
        out_specs=vmem,
        scratch_shapes=[
            pltpu.VMEM((pad, pad), f32),
            pltpu.VMEM((py, pad), f32),
            pltpu.VMEM((ny, py, pad), f32),
            pltpu.VMEM((ny, py, pad), f32),
            pltpu.VMEM((py, pad), f32),
            pltpu.VMEM((nx, py, pad), f32),
            pltpu.VMEM((nx, py, pad), f32),
            pltpu.SemaphoreType.DMA((ny,)),
            pltpu.SemaphoreType.DMA((ny,)),
            pltpu.SemaphoreType.DMA((ny,)),
            pltpu.SemaphoreType.DMA((nx,)),
            pltpu.SemaphoreType.DMA((nx,)),
            pltpu.SemaphoreType.DMA((nx,)),
        ],
        compiler_params=pltpu.CompilerParams(collective_id=4, has_side_effects=True),
        name="gram_allreduce",
    )(wide)
    return total[:size, :size]


def krylov_kernel(nx, ny, bx, v0_ref, terms_ref, diag_ref, out_ref,
                  halo_x, xsend, ysend, xr, yr, send_sem, recv_sem):
    gx = lax.axis_index("gx")
    gy = lax.axis_index("gy")
    rhs = out_ref.shape[1] // terms_ref.shape[1]
    rows, lanes = terms_ref.shape[1], terms_ref.shape[2]
    cells = out_ref.shape[1]
    zero_x = jnp.zeros(xr.shape[2:], jnp.float32)
    zero_y = jnp.zeros(yr.shape[2:], jnp.float32)
    for k in range(xr.shape[0]):
        for d in range(2):
            xr[k, d] = zero_x
            yr[k, d] = zero_y
    targets = (
        (gx < nx - 1, {"gx": gx + 1, "gy": gy}, gx > 0),
        (gx > 0, {"gx": gx - 1, "gy": gy}, gx < nx - 1),
        (gy < ny - 1, {"gx": gx, "gy": gy + 1}, gy > 0),
        (gy > 0, {"gx": gx, "gy": gy - 1}, gy < ny - 1),
    )
    barrier = pltpu.get_barrier_semaphore()
    for has_target, target, _ in targets:
        @pl.when(has_target)
        def _():
            pl.semaphore_signal(barrier, inc=1, device_id=target, device_id_type=pl.DeviceIdType.MESH)
    peers = (gx + nx - 1) // nx + (2 * nx - 2 - gx) // nx + (gy + ny - 1) // ny + (2 * ny - 2 - gy) // ny
    pl.semaphore_wait(barrier, peers)

    row = lax.broadcasted_iota(jnp.int32, (rhs, rows, lanes), 1)
    lane = lax.broadcasted_iota(jnp.int32, (rhs, rows, lanes), 2)
    xpos = row % bx
    zpos = row // bx
    nzp = rows // bx
    t = [terms_ref[i][None] for i in range(6)]
    diag = diag_ref[...][None]
    trow = lax.broadcasted_iota(jnp.int32, (lanes, cells), 0)

    out_ref[0] = v0_ref[...]
    for k in range(xr.shape[0]):
        flat = out_ref[k]
        xsend[0] = out_ref[k, pl.ds(0, cells // bx, stride=bx), :]
        xsend[1] = out_ref[k, pl.ds(bx - 1, cells // bx, stride=bx), :]
        tr = flat.T
        ysend[...] = jnp.where(trow[:8] == 0, tr[0:1], jnp.where(trow[:8] == 1, tr[lanes - 1:lanes], 0.0))
        plan = (
            (xsend.at[1], xr.at[k, 0]),
            (xsend.at[0], xr.at[k, 1]),
            (ysend, yr.at[k, 0]),
            (ysend, yr.at[k, 1]),
        )

        def copy(d):
            return pltpu.make_async_remote_copy(
                src_ref=plan[d][0], dst_ref=plan[d][1], send_sem=send_sem.at[d],
                recv_sem=recv_sem.at[k, d], device_id=targets[d][1],
                device_id_type=pl.DeviceIdType.MESH,
            )

        for d in range(4):
            @pl.when(targets[d][0])
            def _():
                copy(d).start()
        for d in range(4):
            @pl.when(targets[d][0])
            def _():
                copy(d).wait_send()

            @pl.when(targets[d][2])
            def _():
                copy(d).wait_recv()

        halo_x[pl.ds(0, cells // bx, stride=bx), :] = xr[k, 0]
        halo_x[pl.ds(bx - 1, cells // bx, stride=bx), :] = xr[k, 1]
        before = yr[k, 0][1:2]
        after = yr[k, 1][0:1]
        ycols = jnp.where(trow == 0, before, jnp.where(trow == lanes - 1, after, 0.0)).T
        v = flat.reshape(rhs, rows, lanes)
        hx = halo_x[...].reshape(rhs, rows, lanes)
        hy = ycols.reshape(rhs, rows, lanes)
        zm = jnp.where(zpos == 0, 0.0, pltpu.roll(v, bx, 1))
        zp = jnp.where(zpos == nzp - 1, 0.0, pltpu.roll(v, rows - bx, 1))
        xm = jnp.where(xpos == 0, hx, pltpu.roll(v, 1, 1))
        xp = jnp.where(xpos == bx - 1, hx, pltpu.roll(v, rows - 1, 1))
        ym = jnp.where(lane == 0, hy, pltpu.roll(v, 1, 2))
        yp = jnp.where(lane == lanes - 1, hy, pltpu.roll(v, lanes - 1, 2))
        total = t[0] * zm + t[1] * zp
        total = total + t[2] * xm + t[3] * xp
        total = total + t[4] * ym + t[5] * yp
        out_ref[k + 1] = (-total / diag).reshape(cells, lanes)


def krylov_basis(v0, terms, diagonal):
    rhs, nz, bx, by = v0.shape
    nx, ny = lax.axis_size("gx"), lax.axis_size("gy")
    cells = rhs * nz * bx
    vmem = pl.BlockSpec(memory_space=pltpu.VMEM)
    out = pl.pallas_call(
        lambda *refs: krylov_kernel(nx, ny, bx, *refs),
        out_shape=jax.ShapeDtypeStruct((S + 1, cells, by), jnp.float32),
        in_specs=[vmem] * 3,
        out_specs=vmem,
        scratch_shapes=[
            pltpu.VMEM((cells, by), jnp.float32),
            pltpu.VMEM((2, cells // bx, by), jnp.float32),
            pltpu.VMEM((8, cells), jnp.float32),
            pltpu.VMEM((S, 2, cells // bx, by), jnp.float32),
            pltpu.VMEM((S, 2, 8, cells), jnp.float32),
            pltpu.SemaphoreType.DMA((4,)),
            pltpu.SemaphoreType.DMA((S, 4)),
        ],
        compiler_params=pltpu.CompilerParams(collective_id=3, has_side_effects=True),
        name="krylov_basis",
    )(v0.reshape(cells, by), jnp.stack(terms).reshape(6, nz * bx, by), diagonal.reshape(nz * bx, by))
    return out.reshape(S + 1, rhs, nz, bx, by)


def face_terms(padded, storage):
    core = padded[1:-1, 1:-1, 1:-1]
    terms = (
        (core + padded[:-2, 1:-1, 1:-1]) * 0.5,
        (core + padded[2:, 1:-1, 1:-1]) * 0.5,
        (core + padded[1:-1, :-2, 1:-1]) * 0.5,
        (core + padded[1:-1, 2:, 1:-1]) * 0.5,
        (core + padded[1:-1, 1:-1, :-2]) * 0.5,
        (core + padded[1:-1, 1:-1, 2:]) * 0.5,
    )
    diagonal = storage + terms[0] + terms[1] + terms[2] + terms[3] + terms[4] + terms[5]
    return (terms, diagonal)


def _device(axis, index, other_axis, other_index):
    return {axis: index, other_axis: other_index}


def small_solve(gram_all):
    shift_matrix = jnp.eye(BASIS, BASIS - RHS, dtype=jnp.float32) + jnp.eye(
        BASIS, BASIS - RHS, k=-RHS, dtype=jnp.float32
    )
    first_block = jnp.eye(BASIS, RHS, dtype=jnp.float32)
    hp = lax.Precision.HIGHEST
    gram_shift = jnp.dot(gram_all, shift_matrix, precision=hp)
    normal = jnp.dot(shift_matrix.T, gram_shift, precision=hp)
    right_side = jnp.dot(gram_shift.T, first_block, precision=hp)
    lower = jnp.linalg.cholesky(normal)
    y = jax.scipy.linalg.cho_solve((lower, True), right_side)
    coeffs = first_block - jnp.dot(shift_matrix, y, precision=hp)
    return (y, coeffs)


def shards(pumping, conductivity, capacity):
    hp = lax.Precision.HIGHEST
    shape = pumping.shape
    cond_halo = halo_faces(conductivity, 1, 2)
    cond_pad = jnp.pad(cond_halo, ((1, 1), (0, 0), (0, 0)))
    terms, diagonal = face_terms(cond_pad, capacity)
    solution = jnp.zeros(shape, jnp.float32)
    residual = pumping / diagonal
    for restart in range(CYCLES):
        stacked = krylov_basis(residual, terms, diagonal).reshape(BASIS, -1)
        local_gram = jnp.dot(stacked, stacked.T, precision=hp)
        gram_all = gram_sum(local_gram)
        y, coeffs = small_solve(gram_all)
        y_full = jnp.concatenate([y, jnp.zeros((RHS, RHS), jnp.float32)], axis=0)
        both = jnp.dot(jnp.concatenate([y_full, coeffs], axis=1).T, stacked, precision=hp)
        solution = solution + both[:RHS].reshape(shape)
        residual = both[RHS:].reshape(shape)
    return (solution, residual)


def solution(mesh):
    return jax.shard_map(
        shards,
        mesh=mesh,
        in_specs=(P(None, None, "gx", "gy"), P(None, "gx", "gy"), P(None, "gx", "gy")),
        out_specs=(P(None, None, "gx", "gy"), P(None, None, "gx", "gy")),
        check_vma=False,
    )
```
